256 devices in a mesh: graph: 64 (over x, z, core), mp: 4 (over y).
Axes of the slice: x: 4, y: 4, z: 8, core: 2. Of those that a mesh axis runs over, the one named last changes fastest.
Arguments:
- edge_state: bfloat16 [32768, 1536], P('graph', 'mp'), may hold values from -6 to 6
- down_weight: bfloat16 [1536, 384], P('mp'), may hold values from -0.15625 to 0.15625
- basis: float32 [42, 1048576], P(None, ('graph', 'mp')), may hold values from -6 to 6
- basis_weight: float32 [42, 384], replicated, may hold values from -1 to 1
- up_weight: bfloat16 [384, 1536], P(None, 'mp'), may hold values from -0.3125 to 0.3125
- dense_weight: bfloat16 [3, 2, 1536, 1536], P(None, None, None, 'mp'), may hold values from -0.15625 to 0.15625
- send_rows: int32 [64, 256, 64], P('graph', 'mp'), may hold values from 0 to 512, as said below
- trip_in: int32 [1048576], P(('graph', 'mp')), may hold values from 0 to 4095, as said below
- trip_out: int32 [1048576], P(('graph', 'mp')), may hold values from 0 to 4095, as said below
- trip_live: int32 [1048576], P(('graph', 'mp')), may hold values from 0 to 1, as said below
- edge_atom: int32 [32768], P('graph'), may hold values from 0 to 2047
Outputs:
- edge_out: bfloat16 [32768, 1536], P('graph', 'mp')
- atom_out: bfloat16 [2048, 1536], P('graph', 'mp')
The draws below stay inside these ranges and needn't reach their ends.
Inputs may be any that keep to these rules, and one draw needn't show every extreme that they name: `send_rows`: entry [s, m * 64 + g, c] is a row among the 512 edges of graph index s listed in slot c for the device at graph index g and mp index m, or 512 for an empty slot; used slots come first in each list, and some device has every list full. `trip_in`: A slot s * 64 + c of the triplet's own device whose list entry from graph index s is used. `trip_out`: A slot s * 64 + c of the triplet's own device whose list entry from graph index s is used. `trip_live`: on each device the real triplets come first; some device has no padding.
All inputs are finite; a program needn't handle non-finite values.
Results may differ from the reference program's by a relative error of at most 0.014.
Values may be sent and summed in bfloat16 or wider, within the bound.
No kernel may reach another device: no remote copies, remote signals or barrier semaphores. Data moves between devices by JAX's collectives and lax.ppermute only.
A program may use at most 128 MiB of HBM per device.

```python
import jax
import jax.numpy as jnp
from jax import lax

D = 1536
TRIP = 384
NSBF = 42
TILE = 128
LAYERS = 3
EDGE_DEV = 512
CAP = 64
TILES_DEV = 32
EDGES = 32768
ATOMS = 2048
TRIPLETS = 1048576
N_GRAPH = 64
N_MP = 4


def list_counts(key):
    count_key = jax.random.fold_in(key, 1701)
    counts = jax.random.randint(count_key, (N_GRAPH * N_MP, N_GRAPH), 1, CAP + 1)
    return counts.at[0].set(CAP)


def draw_send_rows(key, part):
    counts = list_counts(key)
    shaped = counts.reshape(N_GRAPH, N_MP, N_GRAPH).transpose(2, 1, 0).reshape(N_GRAPH, N_MP * N_GRAPH)
    start_rows = jax.random.randint(jax.random.fold_in(key, 2203), (N_GRAPH, N_MP * N_GRAPH), 0, EDGE_DEV)
    position = jnp.arange(CAP, dtype=jnp.int32)
    rows = (start_rows[:, :, None] + position) % EDGE_DEV
    return jnp.where(position < shaped[:, :, None], rows, EDGE_DEV).astype(jnp.int32)


def slot_draw(key, salt):
    counts = list_counts(key)
    per_device = TILES_DEV * TILE
    source = jax.random.randint(jax.random.fold_in(key, salt), (N_GRAPH * N_MP, per_device), 0, N_GRAPH)
    raw = jax.random.randint(jax.random.fold_in(key, salt + 1), (N_GRAPH * N_MP, per_device), 0, 1048576)
    limit = jnp.take_along_axis(counts, source, axis=1)
    return (source * CAP + raw % limit).reshape(-1).astype(jnp.int32)


def draw_trip_in(key, part):
    return slot_draw(key, 3301)


def draw_trip_out(key, part):
    return slot_draw(key, 4409)


def draw_trip_live(key, part):
    per_device = TILES_DEV * TILE
    live_count = jax.random.randint(jax.random.fold_in(key, 5507), (N_GRAPH * N_MP,), per_device // 4, per_device + 1)
    live_count = live_count.at[0].set(per_device)
    position = jnp.arange(per_device, dtype=jnp.int32)
    return (position[None, :] < live_count[:, None]).reshape(-1).astype(jnp.int32)


def place_ends(result, stream_key, smallest, largest):
    shape = result.shape
    place = [jax.random.randint(jax.random.fold_in(stream_key, axis), (), 0, shape[axis]) for axis in range(len(shape))]
    result = result.at[tuple(place)].set(smallest)
    longest = shape.index(max(shape))
    place[longest] = (place[longest] + 1) % shape[longest]
    return result.at[tuple(place)].set(largest)


def levels(key, shape, split, smallest, high):
    def one(dim, blocks):
        draws = jax.random.uniform(jax.random.fold_in(jax.random.fold_in(key, 6), dim), (blocks,), jnp.float32, smallest / len(split), high / len(split))
        return jnp.repeat(jnp.exp(draws), shape[dim] // blocks).reshape((-1,) + (1,) * (len(shape) - dim - 1))

    loudness = one(*split[0])
    for cut in split[1:]:
        loudness = loudness * one(*cut)
    return loudness


def normal_values(key, shape, deviation, most, pieces=(), kind=jnp.bfloat16):
    factor_of = levels(key, shape, pieces, -0.22, 0.18) if pieces else 1.0
    entries = jax.random.normal(key, shape, jnp.float32) * deviation * factor_of
    return jnp.minimum(jnp.maximum(entries, -most), most).astype(kind)


def setup_inputs(seed: int = 0) -> dict:
    streams_of = jax.random.split(jax.random.key(seed), 12)
    edge_state = normal_values(streams_of[0], (EDGES, D), 1.0, 6.0, ((0, 64), (1, 4)))
    down_weight = normal_values(streams_of[1], (D, TRIP), D ** -0.5, 0.15625, ((0, 4),))
    basis = normal_values(streams_of[2], (NSBF, TRIPLETS), 1.0, 6.0, ((1, 256),), jnp.float32)
    basis_weight = normal_values(streams_of[3], (NSBF, TRIP), NSBF ** -0.5, 1.0, (), jnp.float32)
    up_weight = normal_values(streams_of[4], (TRIP, D), TRIP ** -0.5, 0.3125, ((1, 4),))
    dense_weight = normal_values(streams_of[5], (LAYERS, 2, D, D), D ** -0.5, 0.15625, ((3, 4),))
    send_rows = draw_send_rows(jax.random.fold_in(streams_of[11], 71), 0)
    trip_in = draw_trip_in(jax.random.fold_in(streams_of[11], 71), 0)
    trip_out = draw_trip_out(jax.random.fold_in(streams_of[11], 71), 0)
    trip_live = draw_trip_live(jax.random.fold_in(streams_of[11], 71), 0)
    edge_atom = place_ends(jax.random.randint(streams_of[10], (EDGES,), 0, ATOMS), jax.random.fold_in(streams_of[10], 1), 0, ATOMS - 1).astype(jnp.int32)
    return {"edge_state": edge_state, "down_weight": down_weight, "basis": basis, "basis_weight": basis_weight, "up_weight": up_weight, "dense_weight": dense_weight, "send_rows": send_rows, "trip_in": trip_in, "trip_out": trip_out, "trip_live": trip_live, "edge_atom": edge_atom}


inv_root_two = 0.7071067811865476
atom_scale = 0.2


def reference(edge_state, down_weight, basis, basis_weight, up_weight, dense_weight, send_rows, trip_in, trip_out, trip_live, edge_atom):
    projected = jnp.dot(edge_state, down_weight, preferred_element_type=jnp.float32).astype(jnp.bfloat16)
    per_device = TILES_DEV * TILE
    slot_count = N_GRAPH * CAP
    sources = (jnp.arange(N_GRAPH, dtype=jnp.int32) * EDGE_DEV)[:, None]

    def visit(carry, device):
        graph_index = device // N_MP
        mp_index = device % N_MP
        row_lists = lax.dynamic_index_in_dim(send_rows, (mp_index * N_GRAPH + graph_index).astype(jnp.int32), 1, keepdims=False)
        valid_flat = (row_lists < EDGE_DEV).reshape(-1)
        global_rows = (sources + jnp.minimum(row_lists, EDGE_DEV - 1)).reshape(-1).astype(jnp.int32)
        received = jnp.where(valid_flat[:, None], jnp.take(projected, global_rows, axis=0), jnp.zeros((), jnp.bfloat16))
        offset = (device * per_device).astype(jnp.int32)
        basis_part = lax.dynamic_slice_in_dim(basis, offset, per_device, 1)
        in_part = lax.dynamic_slice_in_dim(trip_in, offset, per_device, 0)
        out_part = lax.dynamic_slice_in_dim(trip_out, offset, per_device, 0)
        live_part = lax.dynamic_slice_in_dim(trip_live, offset, per_device, 0)
        angle_coef = lax.dot_general(basis_part, basis_weight, (((0,), (0,)), ((), ())), precision=lax.Precision.HIGHEST, preferred_element_type=jnp.float32)
        trip_values = jnp.take(received, in_part, axis=0).astype(jnp.float32) * angle_coef * live_part[:, None].astype(jnp.float32)
        slot_sums = jax.ops.segment_sum(trip_values, out_part, num_segments=slot_count).astype(jnp.bfloat16)
        contrib = jnp.where(valid_flat[:, None], slot_sums.astype(jnp.float32), jnp.zeros((), jnp.float32))
        carry = carry.at[global_rows].add(contrib)
        return carry, None

    edge_update, _ = lax.scan(visit, jnp.zeros((EDGES, TRIP), jnp.float32), jnp.arange(N_GRAPH * N_MP, dtype=jnp.int32))
    update_rows = edge_update.astype(jnp.bfloat16)
    hidden = edge_state.astype(jnp.float32) + jnp.dot(update_rows, up_weight, preferred_element_type=jnp.float32)
    for layer_index in range(LAYERS):
        inner = jax.nn.silu(jnp.dot(hidden.astype(jnp.bfloat16), dense_weight[layer_index, 0], preferred_element_type=jnp.float32)).astype(jnp.bfloat16)
        outer = jax.nn.silu(jnp.dot(inner, dense_weight[layer_index, 1], preferred_element_type=jnp.float32))
        hidden = (hidden + outer) * inv_root_two
    atom_sum = jax.ops.segment_sum(hidden, edge_atom, num_segments=ATOMS)
    atom_out = jax.nn.silu(atom_scale * atom_sum).astype(jnp.bfloat16)
    edge_out = (hidden + jnp.take(atom_out, edge_atom, axis=0).astype(jnp.float32)).astype(jnp.bfloat16)
    return (edge_out, atom_out)
```

```python
import functools

import jax
import jax.numpy as jnp
from jax import lax
from jax.experimental import pallas as pl
from jax.experimental.pallas import tpu as pltpu
from jax.sharding import Mesh
from jax.sharding import PartitionSpec as P

ATOM_DEV = 32
GRAPH = ("graph_0", "graph_1", "graph_2")
GRAPH_MP = ("graph_0", "graph_1", "graph_2", "mp")
N_X, N_Z, N_CORE, N_MP = 4, 8, 2, 4
N_GRAPH = N_X * N_Z * N_CORE
CAP = 64
EDGE_DEV = 512
ROWS = EDGE_DEV // N_MP
SLOTS = N_GRAPH * CAP
TRIPS = 4096
NSBF = 42
BASIS_PAD = 48
D = 1536
COLS = D // N_MP
TRIP = 384
MAPS = 6
HALF_MAPS = MAPS // N_CORE
UP_HALF = TRIP // N_CORE
ATOMS = ATOM_DEV * N_GRAPH
HALF_ATOMS = ATOMS // N_CORE
BLOCK = 512

F32 = jnp.float32
BF16 = jnp.bfloat16
I32 = jnp.int32

inv_root_two = 0.7071067811865476
atom_scale = 0.2


def silu(v):
    return v / (1.0 + jnp.exp(-v))


def product(a, b):
    return jnp.dot(a, b, preferred_element_type=F32)


def ones_where(mask):
    return jnp.where(mask, jnp.ones((), F32), jnp.zeros((), F32)).astype(BF16)


def picks(row, count, first):
    n = row.shape[1]
    column = jnp.broadcast_to(row, (128, n)).T
    lane = lax.broadcasted_iota(I32, (n, 128), 1)
    return jnp.concatenate(
        [ones_where(column == lane + (first + k)) for k in range(0, count, 128)], axis=1
    )


def members(row, count, first):
    place = lax.broadcasted_iota(I32, (count, 128), 0) + first
    return jnp.concatenate(
        [ones_where(place == row[:, k : k + 128]) for k in range(0, row.shape[1], 128)], axis=1
    )


def params(mib):
    return pltpu.CompilerParams(
        dimension_semantics=("arbitrary",), vmem_limit_bytes=mib * 1024 * 1024
    )


def whole(shape):
    return pl.BlockSpec(shape, lambda *_: (0,) * len(shape))


def shape_of(*shape, kind=BF16):
    return jax.ShapeDtypeStruct(shape, kind)


SCALAR = pl.BlockSpec(memory_space=pltpu.SMEM)


def project_kernel(mp_ref, state_ref, weight_ref, partial_ref, *turned_refs):
    partial_ref[...] = product(state_ref[...], weight_ref[...]).astype(BF16)
    for k, turned_ref in enumerate(turned_refs):
        place = lax.rem(mp_ref[0] + k, N_MP) * ROWS
        turned_ref[...] = state_ref[pl.ds(pl.multiple_of(place, ROWS), ROWS), :]


def project(mp, edge_state, down_weight):
    return pl.pallas_call(
        project_kernel,
        grid=(1,),
        in_specs=[SCALAR, whole((EDGE_DEV, COLS)), whole((COLS, TRIP))],
        out_specs=[whole((EDGE_DEV, TRIP))] + [whole((ROWS, COLS))] * N_MP,
        out_shape=[shape_of(EDGE_DEV, TRIP)] + [shape_of(ROWS, COLS)] * N_MP,
        compiler_params=params(24),
        name="project",
        cost_estimate=pl.CostEstimate(
            flops=2 * EDGE_DEV * COLS * TRIP, bytes_accessed=1500000, transcendentals=0
        ),
    )(mp, edge_state, down_weight)


def send_kernel(list_ref, a_ref, b_ref, c_ref, d_ref, out_ref, table):
    @pl.when(pl.program_id(0) == 0)
    def _():
        total = a_ref[...].astype(F32) + b_ref[...].astype(F32)
        total = total + (c_ref[...].astype(F32) + d_ref[...].astype(F32))
        table[...] = total.astype(BF16)

    out_ref[...] = product(picks(list_ref[...], EDGE_DEV, 0), table[...]).astype(BF16)


def send(lists, partials):
    return pl.pallas_call(
        send_kernel,
        grid=(SLOTS // BLOCK,),
        in_specs=[pl.BlockSpec((1, BLOCK), lambda i: (0, i))] + [whole((EDGE_DEV, TRIP))] * N_MP,
        out_specs=pl.BlockSpec((BLOCK, TRIP), lambda i: (i, 0)),
        out_shape=shape_of(SLOTS, TRIP),
        scratch_shapes=[pltpu.VMEM((EDGE_DEV, TRIP), BF16)],
        compiler_params=params(24),
        name="send",
        cost_estimate=pl.CostEstimate(
            flops=2 * SLOTS * EDGE_DEV * TRIP, bytes_accessed=4700000, transcendentals=0
        ),
    )(lists, *partials)


TRIP_STEPS = TRIPS // BLOCK
CHUNK = 1024


def triplet_kernel(
    in_ref, live_ref, to_ref, basis_ref, weight_ref, table_ref, out_ref, values, padded
):
    step = pl.program_id(0)

    @pl.when(step == 0)
    def _():
        padded[...] = jnp.zeros_like(padded)

    @pl.when(step < TRIP_STEPS)
    def _():
        padded[0:NSBF, :] = basis_ref[...] * live_ref[...].astype(F32)
        basis = padded[...]
        high = basis.astype(BF16)
        low = (basis - high.astype(F32)).astype(BF16)
        stacked = jnp.concatenate([high, low, high], axis=0)
        coef = lax.dot_general(
            stacked, weight_ref[...], (((0,), (0,)), ((), ())), preferred_element_type=F32
        )
        row = in_ref[...]
        gathered = product(picks(row, CHUNK, 0), table_ref[0:CHUNK, :])
        for k in range(CHUNK, SLOTS, CHUNK):
            gathered = gathered + product(picks(row, CHUNK, k), table_ref[k : k + CHUNK, :])
        place = pl.multiple_of(step * BLOCK, BLOCK)
        values[pl.ds(place, BLOCK), :] = (gathered * coef).astype(BF16)

    @pl.when(step >= TRIP_STEPS)
    def _():
        first = (step - TRIP_STEPS) * BLOCK
        total = product(members(to_ref[:, 0:CHUNK], BLOCK, first), values[0:CHUNK, :])
        for k in range(CHUNK, TRIPS, CHUNK):
            total = total + product(
                members(to_ref[:, k : k + CHUNK], BLOCK, first), values[k : k + CHUNK, :]
            )
        out_ref[...] = total.astype(BF16)


def triplets(trip_in, trip_live, trip_out, basis, weight, table):
    gather_step = lambda i: (0, jnp.minimum(i, TRIP_STEPS - 1))
    return pl.pallas_call(
        triplet_kernel,
        grid=(TRIP_STEPS + SLOTS // BLOCK,),
        in_specs=[
            pl.BlockSpec((1, BLOCK), gather_step),
            pl.BlockSpec((1, BLOCK), gather_step),
            whole((1, TRIPS)),
            pl.BlockSpec((NSBF, BLOCK), gather_step),
            whole((3 * BASIS_PAD, TRIP)),
            whole((SLOTS, TRIP)),
        ],
        out_specs=pl.BlockSpec((BLOCK, TRIP), lambda i: (jnp.maximum(i - TRIP_STEPS, 0), 0)),
        out_shape=shape_of(SLOTS, TRIP),
        scratch_shapes=[pltpu.VMEM((TRIPS, TRIP), BF16), pltpu.VMEM((BASIS_PAD, BLOCK), F32)],
        compiler_params=params(48),
        name="triplets",
        cost_estimate=pl.CostEstimate(
            flops=4 * TRIPS * SLOTS * TRIP, bytes_accessed=7000000, transcendentals=0
        ),
    )(trip_in, trip_live, trip_out, basis, weight, table)


EDGE_CHUNK = 1024


def edges_kernel(mp_ref, list_ref, table_ref, *refs):
    outs, total = refs[:N_MP], refs[N_MP]
    step = pl.program_id(0)
    part = product(members(list_ref[...], EDGE_DEV, 0), table_ref[...])

    @pl.when(step == 0)
    def _():
        total[...] = part

    @pl.when(step > 0)
    def _():
        total[...] += part

    @pl.when(step == SLOTS // EDGE_CHUNK - 1)
    def _():
        for k, out_ref in enumerate(outs):
            place = lax.rem(mp_ref[0] + k, N_MP) * ROWS
            out_ref[...] = total[pl.ds(pl.multiple_of(place, ROWS), ROWS), :].astype(BF16)


def edges(mp, lists, returned):
    return pl.pallas_call(
        edges_kernel,
        grid=(SLOTS // EDGE_CHUNK,),
        in_specs=[
            SCALAR,
            pl.BlockSpec((1, EDGE_CHUNK), lambda i: (0, i)),
            pl.BlockSpec((EDGE_CHUNK, TRIP), lambda i: (i, 0)),
        ],
        out_specs=[whole((ROWS, TRIP))] * N_MP,
        out_shape=[shape_of(ROWS, TRIP)] * N_MP,
        scratch_shapes=[pltpu.VMEM((EDGE_DEV, TRIP), F32)],
        compiler_params=params(24),
        name="edges",
        cost_estimate=pl.CostEstimate(
            flops=2 * SLOTS * EDGE_DEV * TRIP, bytes_accessed=3500000, transcendentals=0
        ),
    )(mp, lists, returned)


SIDE = 2
MAP_STEPS = N_MP // SIDE


def layers_kernel(mp_ref, u0, u1, u2, u3, s0, s1, s2, s3, up_ref, weight_ref, *refs):
    outs = refs[:N_MP]
    hidden, given, inner = refs[N_MP:]
    step = pl.program_id(0)
    me = mp_ref[0]
    which = lax.div(step, MAP_STEPS)
    side = lax.rem(step, MAP_STEPS) * SIDE

    def columns(block):
        return pl.ds(pl.multiple_of(block * COLS, 128), COLS)

    @pl.when(step == 0)
    def _():
        total = u0[...].astype(F32) + u1[...].astype(F32)
        total = total + (u2[...].astype(F32) + u3[...].astype(F32))
        update = total.astype(BF16)
        for k, state_ref in enumerate((s0, s1, s2, s3)):
            hidden[:, columns(lax.rem(me + N_MP - k, N_MP))] = state_ref[...].astype(F32)
        for block in range(N_MP):
            added = product(update[:, :UP_HALF], up_ref[block])
            added = added + product(update[:, UP_HALF:], up_ref[N_MP + block])
            at = slice(block * COLS, (block + 1) * COLS)
            fresh = hidden[:, at] + added
            hidden[:, at] = fresh
            given[:, at] = fresh.astype(BF16)

    @pl.when(lax.rem(which, 2) == 0)
    def _():
        x = given[...]
        for j in range(SIDE):
            inner[:, columns(side + j)] = silu(product(x, weight_ref[j])).astype(BF16)

    @pl.when(lax.rem(which, 2) == 1)
    def _():
        x = inner[...]
        for j in range(SIDE):
            at = columns(side + j)
            fresh = (hidden[:, at] + silu(product(x, weight_ref[j]))) * inv_root_two
            hidden[:, at] = fresh
            given[:, at] = fresh.astype(BF16)

    @pl.when(step == MAPS * MAP_STEPS - 1)
    def _():
        for k, out_ref in enumerate(outs):
            out_ref[...] = given[:, columns(lax.rem(me + k, N_MP))]


def layers(mp, updates, states, gathered):
    def weight_block(i):
        which = i // MAP_STEPS
        side = i % MAP_STEPS
        return ((which // HALF_MAPS) * MAP_STEPS + side, which % HALF_MAPS, 0)

    return pl.pallas_call(
        layers_kernel,
        grid=(MAPS * MAP_STEPS,),
        in_specs=[SCALAR]
        + [whole((ROWS, TRIP))] * N_MP
        + [whole((ROWS, COLS))] * N_MP
        + [
            pl.BlockSpec(
                (N_CORE * N_MP, UP_HALF, COLS), lambda i: (0, HALF_MAPS * D // UP_HALF, 0)
            ),
            pl.BlockSpec((SIDE, D, COLS), weight_block),
        ],
        out_specs=[whole((ROWS, COLS))] * N_MP,
        out_shape=[shape_of(ROWS, COLS)] * N_MP,
        scratch_shapes=[
            pltpu.VMEM((ROWS, D), F32),
            pltpu.VMEM((ROWS, D), BF16),
            pltpu.VMEM((ROWS, D), BF16),
        ],
        compiler_params=params(32),
        name="layers",
        cost_estimate=pl.CostEstimate(
            flops=2 * ROWS * D * D * MAPS,
            bytes_accessed=2 * D * D * MAPS,
            transcendentals=ROWS * D * MAPS,
        ),
    )(mp, *updates, *states, gathered, gathered)


def at_block(ref, me, k):
    place = lax.rem(me + N_MP - k, N_MP) * ROWS
    return ref[:, pl.ds(pl.multiple_of(place, ROWS), ROWS)]


def atoms_kernel(mp_ref, core_ref, atom_ref, h0, h1, h2, h3, keep_ref, give_ref):
    me, core = mp_ref[0], core_ref[0]
    row = jnp.concatenate([at_block(atom_ref, me, k) for k in range(N_MP)], axis=1)
    hidden = jnp.concatenate([h0[...], h1[...], h2[...], h3[...]], axis=0)
    group = row // ATOM_DEV
    spot = (group // N_CORE) * ATOM_DEV + row % ATOM_DEV
    for out_ref, owner in ((keep_ref, core), (give_ref, 1 - core)):
        mine = jnp.where(group % N_CORE == owner, spot, -1)
        for first in range(0, HALF_ATOMS, BLOCK):
            part = product(members(mine, BLOCK, first), hidden)
            out_ref[first : first + BLOCK, :] = part.astype(BF16)


def atoms(mp, core, edge_atom, hiddens):
    return pl.pallas_call(
        atoms_kernel,
        grid=(1,),
        in_specs=[SCALAR, SCALAR, whole((1, EDGE_DEV))] + [whole((ROWS, COLS))] * N_MP,
        out_specs=[whole((HALF_ATOMS, COLS))] * 2,
        out_shape=[shape_of(HALF_ATOMS, COLS)] * 2,
        compiler_params=params(24),
        name="atoms",
        cost_estimate=pl.CostEstimate(
            flops=2 * ATOMS * EDGE_DEV * COLS, bytes_accessed=2000000, transcendentals=0
        ),
    )(mp, core, edge_atom, *hiddens)


def final_kernel(mp_ref, core_ref, atom_ref, h0, h1, h2, h3, mine_ref, other_ref, out_ref):
    me, core = mp_ref[0], core_ref[0]
    for k, hidden_ref in enumerate((h0, h1, h2, h3)):
        row = at_block(atom_ref, me, k)
        group = row // ATOM_DEV
        spot = (group // N_CORE) * ATOM_DEV + row % ATOM_DEV
        near = jnp.where(group % N_CORE == core, spot, -1)
        far = jnp.where(group % N_CORE == core, -1, spot)
        taken = product(picks(near, HALF_ATOMS, 0), mine_ref[...])
        taken = taken + product(picks(far, HALF_ATOMS, 0), other_ref[...])
        place = lax.rem(me + N_MP - k, N_MP) * ROWS
        out_ref[pl.ds(pl.multiple_of(place, ROWS), ROWS), :] = (
            hidden_ref[...].astype(F32) + taken
        ).astype(BF16)


def final(mp, core, edge_atom, hiddens, mine, other):
    return pl.pallas_call(
        final_kernel,
        grid=(1,),
        in_specs=[SCALAR, SCALAR, whole((1, EDGE_DEV))]
        + [whole((ROWS, COLS))] * N_MP
        + [whole((HALF_ATOMS, COLS))] * 2,
        out_specs=whole((EDGE_DEV, COLS)),
        out_shape=shape_of(EDGE_DEV, COLS),
        compiler_params=params(24),
        name="final",
        cost_estimate=pl.CostEstimate(
            flops=2 * ATOMS * EDGE_DEV * COLS, bytes_accessed=2400000, transcendentals=0
        ),
    )(mp, core, edge_atom, *hiddens, mine, other)


def turn(array, axis, count, shift):
    return lax.ppermute(array, axis, [(i, (i + shift) % count) for i in range(count)])


def turned(blocks, axis):
    count = len(blocks)
    return [blocks[0]] + [turn(blocks[k], axis, count, k) for k in range(1, count)]


def summed(blocks):
    return jnp.sum(blocks.astype(F32), axis=0)


def local(
    edge_state,
    down_weight,
    basis,
    basis_weight,
    up_weight,
    dense_weight,
    send_rows,
    trip_in,
    trip_out,
    trip_live,
    edge_atom,
):
    mp = jnp.full((1,), lax.axis_index("mp"), I32)
    core_index = lax.axis_index("graph_2")
    core = jnp.full((1,), core_index, I32)
    lists = send_rows.reshape(1, SLOTS)
    atom_row = edge_atom.reshape(1, EDGE_DEV)
    high = basis_weight.astype(BF16)
    low = (basis_weight - high.astype(F32)).astype(BF16)
    pad = ((0, BASIS_PAD - NSBF), (0, 0))
    high, low = jnp.pad(high, pad), jnp.pad(low, pad)
    coef_weight = jnp.concatenate([high, high, low], axis=0)
    half = jnp.concatenate(
        [
            lax.dynamic_slice_in_dim(
                dense_weight.reshape(MAPS * D, COLS), core_index * (HALF_MAPS * D), HALF_MAPS * D, 0
            ),
            lax.dynamic_slice_in_dim(up_weight, core_index * UP_HALF, UP_HALF, 0),
        ],
        axis=0,
    )

    partial, *state_blocks = project(mp, edge_state, down_weight)
    partials = turned([partial] * N_MP, "mp")
    outgoing = send(lists, partials)
    outgoing, half, *state_blocks = lax.optimization_barrier((outgoing, half, *state_blocks))
    gathered = lax.all_gather(half, ("graph_2", "mp"), axis=0, tiled=False)
    received = lax.all_to_all(
        outgoing.reshape(N_GRAPH, CAP, TRIP), GRAPH, split_axis=0, concat_axis=0, tiled=True
    )
    states = turned(state_blocks, "mp")
    slot_sums = triplets(
        trip_in.reshape(1, TRIPS),
        trip_live.reshape(1, TRIPS),
        trip_out.reshape(1, TRIPS),
        basis,
        coef_weight,
        received.reshape(SLOTS, TRIP),
    )
    returned = lax.all_to_all(
        slot_sums.reshape(N_GRAPH, CAP, TRIP), GRAPH, split_axis=0, concat_axis=0, tiled=True
    )
    updates = turned(edges(mp, lists, returned.reshape(SLOTS, TRIP)), "mp")
    hiddens = turned(layers(mp, updates, states, gathered), "mp")
    keep, give = atoms(mp, core, atom_row, hiddens)
    part = keep.astype(F32) + turn(give, "graph_2", N_CORE, 1).astype(F32)
    part = part.astype(BF16).reshape(N_X, HALF_ATOMS // N_X, COLS)
    part = summed(lax.all_to_all(part, "graph_0", 0, 0, tiled=True))
    part = part.astype(BF16).reshape(N_Z, ATOM_DEV, COLS)
    atom_sum = summed(lax.all_to_all(part, "graph_1", 0, 0, tiled=True))
    atom_out = jax.nn.silu(atom_scale * atom_sum).astype(BF16)
    table = lax.all_to_all(
        jnp.broadcast_to(atom_out[None], (N_Z, ATOM_DEV, COLS)), "graph_1", 0, 0, tiled=True
    ).reshape(N_Z * ATOM_DEV, COLS)
    table = lax.all_to_all(
        jnp.broadcast_to(table[None], (N_X, N_Z * ATOM_DEV, COLS)), "graph_0", 0, 0, tiled=True
    ).reshape(HALF_ATOMS, COLS)
    other = turn(table, "graph_2", N_CORE, 1)
    edge_out = final(mp, core, atom_row, hiddens, table, other)
    return (edge_out, atom_out)


def solution(mesh):
    split = Mesh(
        mesh.devices.reshape(N_X, N_Z, N_CORE, mesh.shape["mp"]),
        ("graph_0", "graph_1", "graph_2", "mp"),
    )
    return jax.shard_map(
        local,
        mesh=split,
        in_specs=(
            P(GRAPH, "mp"),
            P("mp", None),
            P(None, GRAPH_MP),
            P(),
            P(None, "mp"),
            P(None, None, None, "mp"),
            P(GRAPH, "mp", None),
            P(GRAPH_MP),
            P(GRAPH_MP),
            P(GRAPH_MP),
            P(GRAPH),
        ),
        out_specs=(P(GRAPH, "mp"), P(GRAPH, "mp")),
        check_vma=False,
    )
```

```python
import functools

import jax
import jax.numpy as jnp
from jax import lax
from jax.experimental import pallas as pl
from jax.experimental.pallas import tpu as pltpu
from jax.sharding import Mesh
from jax.sharding import PartitionSpec as P

ATOM_DEV = 32
GRAPH = ("graph_0", "graph_1", "graph_2")
GRAPH_MP = ("graph_0", "graph_1", "graph_2", "mp")
N_X, N_Z, N_CORE, N_MP = 4, 8, 2, 4
N_GRAPH = N_X * N_Z * N_CORE
CAP = 64
EDGE_DEV = 512
ROWS = EDGE_DEV // N_MP
SLOTS = N_GRAPH * CAP
TRIPS = 4096
NSBF = 42
BASIS_PAD = 48
D = 1536
COLS = D // N_MP
TRIP = 384
MAPS = 6
HALF_MAPS = MAPS // N_CORE
UP_HALF = TRIP // N_CORE
ATOMS = ATOM_DEV * N_GRAPH
HALF_ATOMS = ATOMS // N_CORE
BLOCK = 512

F32 = jnp.float32
BF16 = jnp.bfloat16
I32 = jnp.int32

inv_root_two = 0.7071067811865476
atom_scale = 0.2


def silu(v):
    return v / (1.0 + jnp.exp(-v))


def product(a, b):
    return jnp.dot(a, b, preferred_element_type=F32)


def ones_where(mask):
    return jnp.where(mask, jnp.ones((), F32), jnp.zeros((), F32)).astype(BF16)


def column_of(row):
    return jnp.broadcast_to(row, (128, row.shape[1])).T


def picks_of(column, count):
    lane = lax.broadcasted_iota(I32, column.shape, 1)
    return jnp.concatenate(
        [ones_where(column == lane + k) for k in range(0, count, 128)], axis=1
    )


def picks(row, count):
    return picks_of(column_of(row), count)


def members(row, count, first):
    place = lax.broadcasted_iota(I32, (count, 128), 0) + first
    return jnp.concatenate(
        [ones_where(place == row[:, k : k + 128]) for k in range(0, row.shape[1], 128)], axis=1
    )


def params(mib):
    return pltpu.CompilerParams(
        dimension_semantics=("arbitrary",), vmem_limit_bytes=mib * 1024 * 1024
    )


def whole(shape):
    return pl.BlockSpec(shape, lambda *_: (0,) * len(shape))


def shape_of(*shape, kind=BF16):
    return jax.ShapeDtypeStruct(shape, kind)


SCALAR = pl.BlockSpec(memory_space=pltpu.SMEM)


def project_kernel(mp_ref, state_ref, weight_ref, partial_ref, *turned_refs):
    partial_ref[...] = product(state_ref[...], weight_ref[...]).astype(BF16)
    for k, turned_ref in enumerate(turned_refs):
        place = lax.rem(mp_ref[0] + k, N_MP) * ROWS
        turned_ref[...] = state_ref[pl.ds(pl.multiple_of(place, ROWS), ROWS), :]


def project(mp, edge_state, down_weight):
    return pl.pallas_call(
        project_kernel,
        grid=(1,),
        in_specs=[SCALAR, whole((EDGE_DEV, COLS)), whole((COLS, TRIP))],
        out_specs=[whole((EDGE_DEV, TRIP))] + [whole((ROWS, COLS))] * N_MP,
        out_shape=[shape_of(EDGE_DEV, TRIP)] + [shape_of(ROWS, COLS)] * N_MP,
        compiler_params=params(24),
        name="project",
        cost_estimate=pl.CostEstimate(
            flops=2 * EDGE_DEV * COLS * TRIP, bytes_accessed=1500000, transcendentals=0
        ),
    )(mp, edge_state, down_weight)


def send_kernel(list_ref, a_ref, b_ref, c_ref, d_ref, out_ref, table):
    @pl.when(pl.program_id(0) == 0)
    def _():
        total = a_ref[...].astype(F32) + b_ref[...].astype(F32)
        total = total + (c_ref[...].astype(F32) + d_ref[...].astype(F32))
        table[...] = total.astype(BF16)

    out_ref[...] = product(picks(list_ref[...], EDGE_DEV), table[...]).astype(BF16)


def send(lists, partials):
    return pl.pallas_call(
        send_kernel,
        grid=(SLOTS // BLOCK,),
        in_specs=[pl.BlockSpec((1, BLOCK), lambda i: (0, i))] + [whole((EDGE_DEV, TRIP))] * N_MP,
        out_specs=pl.BlockSpec((BLOCK, TRIP), lambda i: (i, 0)),
        out_shape=shape_of(SLOTS, TRIP),
        scratch_shapes=[pltpu.VMEM((EDGE_DEV, TRIP), BF16)],
        compiler_params=params(24),
        name="send",
        cost_estimate=pl.CostEstimate(
            flops=2 * SLOTS * EDGE_DEV * TRIP, bytes_accessed=4700000, transcendentals=0
        ),
    )(lists, *partials)


TRIP_STEPS = TRIPS // BLOCK
HALF_SLOTS = SLOTS // 2
SLOT_BLOCK = 256
SLOT_STEPS = HALF_SLOTS // SLOT_BLOCK
FEATURE_BLOCKS = range(0, TRIP, 128)


def triplet_kernel(
    in_ref, live_ref, to_ref, basis_ref, weight_ref, table_ref, out_ref, table, values, padded
):
    step = pl.program_id(0)

    @pl.when(step == 0)
    def _():
        padded[...] = jnp.zeros_like(padded)
        table[:, :TRIP] = table_ref[:HALF_SLOTS, :]
        table[:, TRIP:] = table_ref[HALF_SLOTS:, :]

    @pl.when(step < TRIP_STEPS)
    def _():
        padded[0:NSBF, :] = basis_ref[...] * live_ref[...].astype(F32)
        basis = padded[...]
        high = basis.astype(BF16)
        low = (basis - high.astype(F32)).astype(BF16)
        stacked = jnp.concatenate([high, low, high], axis=0)
        coef = lax.dot_general(
            stacked, weight_ref[...], (((0,), (0,)), ((), ())), preferred_element_type=F32
        )
        place = pl.multiple_of(step * BLOCK, BLOCK)
        source = column_of(in_ref[...])
        target = column_of(to_ref[:, pl.ds(place, BLOCK)])
        near = source < HALF_SLOTS
        first = target < HALF_SLOTS
        both = product(picks_of(source & (HALF_SLOTS - 1), HALF_SLOTS), table[...])
        for k in FEATURE_BLOCKS:
            at, far = slice(k, k + 128), slice(TRIP + k, TRIP + k + 128)
            value = jnp.where(near, both[:, at], both[:, far]) * coef[:, at]
            values[pl.ds(place, BLOCK), at] = jnp.where(first, value, 0.0).astype(BF16)
            values[pl.ds(place, BLOCK), far] = jnp.where(first, 0.0, value).astype(BF16)

    @pl.when(step >= TRIP_STEPS)
    def _():
        row = to_ref[...] & (HALF_SLOTS - 1)
        chosen = members(row, SLOT_BLOCK, (step - TRIP_STEPS) * SLOT_BLOCK)
        total = product(chosen, values[...]).astype(BF16)
        out_ref[0] = total[:, :TRIP]
        out_ref[1] = total[:, TRIP:]


def triplets(trip_in, trip_live, trip_out, basis, weight, table):
    gather_step = lambda i: (0, jnp.minimum(i, TRIP_STEPS - 1))
    return pl.pallas_call(
        triplet_kernel,
        grid=(TRIP_STEPS + SLOT_STEPS,),
        in_specs=[
            pl.BlockSpec((1, BLOCK), gather_step),
            pl.BlockSpec((1, BLOCK), gather_step),
            whole((1, TRIPS)),
            pl.BlockSpec((NSBF, BLOCK), gather_step),
            whole((3 * BASIS_PAD, TRIP)),
            whole((SLOTS, TRIP)),
        ],
        out_specs=pl.BlockSpec(
            (2, SLOT_BLOCK, TRIP), lambda i: (0, jnp.maximum(i - TRIP_STEPS, 0), 0)
        ),
        out_shape=shape_of(2, HALF_SLOTS, TRIP),
        scratch_shapes=[
            pltpu.VMEM((HALF_SLOTS, 2 * TRIP), BF16),
            pltpu.VMEM((TRIPS, 2 * TRIP), BF16),
            pltpu.VMEM((BASIS_PAD, BLOCK), F32),
        ],
        compiler_params=params(60),
        name="triplets",
        cost_estimate=pl.CostEstimate(
            flops=4 * TRIPS * SLOTS * TRIP, bytes_accessed=7000000, transcendentals=0
        ),
    )(trip_in, trip_live, trip_out, basis, weight, table)


EDGE_CHUNK = 1024


def edges_kernel(mp_ref, list_ref, table_ref, *refs):
    outs, total = refs[:N_MP], refs[N_MP]
    step = pl.program_id(0)
    part = product(members(list_ref[...], EDGE_DEV, 0), table_ref[...])

    @pl.when(step == 0)
    def _():
        total[...] = part

    @pl.when(step > 0)
    def _():
        total[...] += part

    @pl.when(step == SLOTS // EDGE_CHUNK - 1)
    def _():
        for k, out_ref in enumerate(outs):
            place = lax.rem(mp_ref[0] + k, N_MP) * ROWS
            out_ref[...] = total[pl.ds(pl.multiple_of(place, ROWS), ROWS), :].astype(BF16)


def edges(mp, lists, returned):
    return pl.pallas_call(
        edges_kernel,
        grid=(SLOTS // EDGE_CHUNK,),
        in_specs=[
            SCALAR,
            pl.BlockSpec((1, EDGE_CHUNK), lambda i: (0, i)),
            pl.BlockSpec((EDGE_CHUNK, TRIP), lambda i: (i, 0)),
        ],
        out_specs=[whole((ROWS, TRIP))] * N_MP,
        out_shape=[shape_of(ROWS, TRIP)] * N_MP,
        scratch_shapes=[pltpu.VMEM((EDGE_DEV, TRIP), F32)],
        compiler_params=params(24),
        name="edges",
        cost_estimate=pl.CostEstimate(
            flops=2 * SLOTS * EDGE_DEV * TRIP, bytes_accessed=3500000, transcendentals=0
        ),
    )(mp, lists, returned)


SIDE = 4
MAP_STEPS = N_MP // SIDE


def layers_kernel(mp_ref, u0, u1, u2, u3, s0, s1, s2, s3, up_ref, weight_ref, *refs):
    outs = refs[:N_MP]
    hidden, given, inner = refs[N_MP:]
    step = pl.program_id(0)
    me = mp_ref[0]
    which = lax.div(step, MAP_STEPS)
    side = lax.rem(step, MAP_STEPS) * SIDE

    def columns(block):
        return pl.ds(pl.multiple_of(block * COLS, 128), COLS)

    @pl.when(step == 0)
    def _():
        total = u0[...].astype(F32) + u1[...].astype(F32)
        total = total + (u2[...].astype(F32) + u3[...].astype(F32))
        update = total.astype(BF16)
        for k, state_ref in enumerate((s0, s1, s2, s3)):
            hidden[:, columns(lax.rem(me + N_MP - k, N_MP))] = state_ref[...].astype(F32)
        for block in range(N_MP):
            added = product(update[:, :UP_HALF], up_ref[block])
            added = added + product(update[:, UP_HALF:], up_ref[N_MP + block])
            at = slice(block * COLS, (block + 1) * COLS)
            fresh = hidden[:, at] + added
            hidden[:, at] = fresh
            given[:, at] = fresh.astype(BF16)

    @pl.when(lax.rem(which, 2) == 0)
    def _():
        x = given[...]
        for j in range(SIDE):
            inner[:, columns(side + j)] = silu(product(x, weight_ref[j])).astype(BF16)

    @pl.when(lax.rem(which, 2) == 1)
    def _():
        x = inner[...]
        for j in range(SIDE):
            at = columns(side + j)
            fresh = (hidden[:, at] + silu(product(x, weight_ref[j]))) * inv_root_two
            hidden[:, at] = fresh
            given[:, at] = fresh.astype(BF16)

    @pl.when(step == MAPS * MAP_STEPS - 1)
    def _():
        for k, out_ref in enumerate(outs):
            out_ref[...] = given[:, columns(lax.rem(me + k, N_MP))]


def layers(mp, updates, states, gathered):
    def weight_block(i):
        which = i // MAP_STEPS
        side = i % MAP_STEPS
        return ((which // HALF_MAPS) * MAP_STEPS + side, which % HALF_MAPS, 0)

    return pl.pallas_call(
        layers_kernel,
        grid=(MAPS * MAP_STEPS,),
        in_specs=[SCALAR]
        + [whole((ROWS, TRIP))] * N_MP
        + [whole((ROWS, COLS))] * N_MP
        + [
            pl.BlockSpec(
                (N_CORE * N_MP, UP_HALF, COLS), lambda i: (0, HALF_MAPS * D // UP_HALF, 0)
            ),
            pl.BlockSpec((SIDE, D, COLS), weight_block),
        ],
        out_specs=[whole((ROWS, COLS))] * N_MP,
        out_shape=[shape_of(ROWS, COLS)] * N_MP,
        scratch_shapes=[
            pltpu.VMEM((ROWS, D), F32),
            pltpu.VMEM((ROWS, D), BF16),
            pltpu.VMEM((ROWS, D), BF16),
        ],
        compiler_params=params(40),
        name="layers",
        cost_estimate=pl.CostEstimate(
            flops=2 * ROWS * D * D * MAPS,
            bytes_accessed=2 * D * D * MAPS,
            transcendentals=ROWS * D * MAPS,
        ),
    )(mp, *updates, *states, gathered, gathered)


def at_block(ref, me, k):
    place = lax.rem(me + N_MP - k, N_MP) * ROWS
    return ref[:, pl.ds(pl.multiple_of(place, ROWS), ROWS)]


def atoms_kernel(mp_ref, core_ref, atom_ref, h0, h1, h2, h3, keep_ref, give_ref):
    me, core = mp_ref[0], core_ref[0]
    row = jnp.concatenate([at_block(atom_ref, me, k) for k in range(N_MP)], axis=1)
    hidden = jnp.concatenate([h0[...], h1[...], h2[...], h3[...]], axis=0)
    group = row // ATOM_DEV
    spot = (group // N_CORE) * ATOM_DEV + row % ATOM_DEV
    for out_ref, owner in ((keep_ref, core), (give_ref, 1 - core)):
        mine = jnp.where(group % N_CORE == owner, spot, -1)
        for first in range(0, HALF_ATOMS, BLOCK):
            part = product(members(mine, BLOCK, first), hidden)
            out_ref[first : first + BLOCK, :] = part.astype(BF16)


def atoms(mp, core, edge_atom, hiddens):
    return pl.pallas_call(
        atoms_kernel,
        grid=(1,),
        in_specs=[SCALAR, SCALAR, whole((1, EDGE_DEV))] + [whole((ROWS, COLS))] * N_MP,
        out_specs=[whole((HALF_ATOMS, COLS))] * 2,
        out_shape=[shape_of(HALF_ATOMS, COLS)] * 2,
        compiler_params=params(24),
        name="atoms",
        cost_estimate=pl.CostEstimate(
            flops=2 * ATOMS * EDGE_DEV * COLS, bytes_accessed=2000000, transcendentals=0
        ),
    )(mp, core, edge_atom, *hiddens)


def meet_kernel(x_ref, keep_ref, got_ref, *outs):
    for k, out_ref in enumerate(outs):
        place = lax.rem(x_ref[0] + k, N_X) * (HALF_ATOMS // N_X)
        rows = pl.ds(pl.multiple_of(place, HALF_ATOMS // N_X), HALF_ATOMS // N_X)
        out_ref[...] = (keep_ref[rows, :].astype(F32) + got_ref[rows, :].astype(F32)).astype(BF16)


def meet(x, keep, got):
    return pl.pallas_call(
        meet_kernel,
        grid=(1,),
        in_specs=[SCALAR] + [whole((HALF_ATOMS, COLS))] * 2,
        out_specs=[whole((HALF_ATOMS // N_X, COLS))] * N_X,
        out_shape=[shape_of(HALF_ATOMS // N_X, COLS)] * N_X,
        compiler_params=params(24),
        name="meet",
        cost_estimate=pl.CostEstimate(
            flops=HALF_ATOMS * COLS, bytes_accessed=2400000, transcendentals=0
        ),
    )(x, keep, got)


def final_kernel(mp_ref, core_ref, atom_ref, h0, h1, h2, h3, mine_ref, other_ref, out_ref):
    me, core = mp_ref[0], core_ref[0]
    for k, hidden_ref in enumerate((h0, h1, h2, h3)):
        row = at_block(atom_ref, me, k)
        group = row // ATOM_DEV
        spot = (group // N_CORE) * ATOM_DEV + row % ATOM_DEV
        near = jnp.where(group % N_CORE == core, spot, -1)
        far = jnp.where(group % N_CORE == core, -1, spot)
        taken = product(picks(near, HALF_ATOMS), mine_ref[...])
        taken = taken + product(picks(far, HALF_ATOMS), other_ref[...])
        place = lax.rem(me + N_MP - k, N_MP) * ROWS
        out_ref[pl.ds(pl.multiple_of(place, ROWS), ROWS), :] = (
            hidden_ref[...].astype(F32) + taken
        ).astype(BF16)


def final(mp, core, edge_atom, hiddens, mine, other):
    return pl.pallas_call(
        final_kernel,
        grid=(1,),
        in_specs=[SCALAR, SCALAR, whole((1, EDGE_DEV))]
        + [whole((ROWS, COLS))] * N_MP
        + [whole((HALF_ATOMS, COLS))] * 2,
        out_specs=whole((EDGE_DEV, COLS)),
        out_shape=shape_of(EDGE_DEV, COLS),
        compiler_params=params(24),
        name="final",
        cost_estimate=pl.CostEstimate(
            flops=2 * ATOMS * EDGE_DEV * COLS, bytes_accessed=2400000, transcendentals=0
        ),
    )(mp, core, edge_atom, *hiddens, mine, other)


def turn(array, axis, count, shift):
    return lax.ppermute(array, axis, [(i, (i + shift) % count) for i in range(count)])


def turned(blocks, axis):
    count = len(blocks)
    return [blocks[0]] + [turn(blocks[k], axis, count, k) for k in range(1, count)]


def summed(blocks):
    return jnp.sum(blocks.astype(F32), axis=0)


def local(
    edge_state,
    down_weight,
    basis,
    basis_weight,
    up_weight,
    dense_weight,
    send_rows,
    trip_in,
    trip_out,
    trip_live,
    edge_atom,
):
    mp = jnp.full((1,), lax.axis_index("mp"), I32)
    core_index = lax.axis_index("graph_2")
    core = jnp.full((1,), core_index, I32)
    lists = send_rows.reshape(1, SLOTS)
    atom_row = edge_atom.reshape(1, EDGE_DEV)
    high = basis_weight.astype(BF16)
    low = (basis_weight - high.astype(F32)).astype(BF16)
    pad = ((0, BASIS_PAD - NSBF), (0, 0))
    high, low = jnp.pad(high, pad), jnp.pad(low, pad)
    coef_weight = jnp.concatenate([high, high, low], axis=0)
    half = jnp.concatenate(
        [
            lax.dynamic_slice_in_dim(
                dense_weight.reshape(MAPS * D, COLS), core_index * (HALF_MAPS * D), HALF_MAPS * D, 0
            ),
            lax.dynamic_slice_in_dim(up_weight, core_index * UP_HALF, UP_HALF, 0),
        ],
        axis=0,
    )

    partial, *state_blocks = project(mp, edge_state, down_weight)
    partials = turned([partial] * N_MP, "mp")
    outgoing = send(lists, partials)
    outgoing, half, *state_blocks = lax.optimization_barrier((outgoing, half, *state_blocks))
    gathered = lax.all_gather(half, ("graph_2", "mp"), axis=0, tiled=False)
    received = lax.all_to_all(
        outgoing.reshape(N_GRAPH, CAP, TRIP), GRAPH, split_axis=0, concat_axis=0, tiled=True
    )
    states = turned(state_blocks, "mp")
    slot_sums = triplets(
        trip_in.reshape(1, TRIPS),
        trip_live.reshape(1, TRIPS),
        trip_out.reshape(1, TRIPS),
        basis,
        coef_weight,
        received.reshape(SLOTS, TRIP),
    )
    returned = lax.all_to_all(
        slot_sums.reshape(N_GRAPH, CAP, TRIP), GRAPH, split_axis=0, concat_axis=0, tiled=True
    )
    updates = turned(edges(mp, lists, returned.reshape(SLOTS, TRIP)), "mp")
    hiddens = turned(layers(mp, updates, states, gathered), "mp")
    keep, give = atoms(mp, core, atom_row, hiddens)
    x = jnp.full((1,), lax.axis_index("graph_0"), I32)
    parts = turned(meet(x, keep, turn(give, "graph_2", N_CORE, 1)), "graph_0")
    part = (parts[0].astype(F32) + parts[1].astype(F32)) + (
        parts[2].astype(F32) + parts[3].astype(F32)
    )
    part = part.astype(BF16).reshape(N_Z, ATOM_DEV, COLS)
    atom_sum = summed(lax.all_to_all(part, "graph_1", 0, 0, tiled=True))
    atom_out = jax.nn.silu(atom_scale * atom_sum).astype(BF16)
    table = lax.all_to_all(
        jnp.broadcast_to(atom_out[None], (N_Z, ATOM_DEV, COLS)), "graph_1", 0, 0, tiled=True
    ).reshape(N_Z * ATOM_DEV, COLS)
    table = lax.all_to_all(
        jnp.broadcast_to(table[None], (N_X, N_Z * ATOM_DEV, COLS)), "graph_0", 0, 0, tiled=True
    ).reshape(HALF_ATOMS, COLS)
    other = turn(table, "graph_2", N_CORE, 1)
    edge_out = final(mp, core, atom_row, hiddens, table, other)
    return (edge_out, atom_out)


def solution(mesh):
    split = Mesh(
        mesh.devices.reshape(N_X, N_Z, N_CORE, mesh.shape["mp"]),
        ("graph_0", "graph_1", "graph_2", "mp"),
    )
    return jax.shard_map(
        local,
        mesh=split,
        in_specs=(
            P(GRAPH, "mp"),
            P("mp", None),
            P(None, GRAPH_MP),
            P(),
            P(None, "mp"),
            P(None, None, None, "mp"),
            P(GRAPH, "mp", None),
            P(GRAPH_MP),
            P(GRAPH_MP),
            P(GRAPH_MP),
            P(GRAPH),
        ),
        out_specs=(P(GRAPH, "mp"), P(GRAPH, "mp")),
        check_vma=False,
    )
```

```python
import functools

import jax
import jax.numpy as jnp
from jax import lax
from jax.experimental import pallas as pl
from jax.experimental.pallas import tpu as pltpu
from jax.sharding import Mesh
from jax.sharding import PartitionSpec as P

ATOM_DEV = 32
GRAPH = ("graph_0", "graph_1", "graph_2")
GRAPH_MP = ("graph_0", "graph_1", "graph_2", "mp")
N_X, N_Z, N_CORE, N_MP = 4, 8, 2, 4
N_GRAPH = N_X * N_Z * N_CORE
CAP = 64
EDGE_DEV = 512
ROWS = EDGE_DEV // N_MP
SLOTS = N_GRAPH * CAP
TRIPS = 4096
NSBF = 42
BASIS_PAD = 48
D = 1536
COLS = D // N_MP
TRIP = 384
MAPS = 6
HALF_MAPS = MAPS // N_CORE
UP_HALF = TRIP // N_CORE
ATOMS = ATOM_DEV * N_GRAPH
HALF_ATOMS = ATOMS // N_CORE
BLOCK = 512
PARTS = ((0, 128), (128, 384))

F32 = jnp.float32
BF16 = jnp.bfloat16
I32 = jnp.int32

inv_root_two = 0.7071067811865476
atom_scale = 0.2


def silu(v):
    return v / (1.0 + jnp.exp(-v))


def product(a, b):
    return jnp.dot(a, b, preferred_element_type=F32)


def ones_where(mask):
    return jnp.where(mask, jnp.ones((), F32), jnp.zeros((), F32)).astype(BF16)


def column_of(row):
    return jnp.broadcast_to(row, (128, row.shape[1])).T


def picks_of(column, count):
    lane = lax.broadcasted_iota(I32, column.shape, 1)
    return jnp.concatenate(
        [ones_where(column == lane + k) for k in range(0, count, 128)], axis=1
    )


def picks(row, count):
    return picks_of(column_of(row), count)


def members(row, count, first):
    place = lax.broadcasted_iota(I32, (count, 128), 0) + first
    return jnp.concatenate(
        [ones_where(place == row[:, k : k + 128]) for k in range(0, row.shape[1], 128)], axis=1
    )


def params(mib):
    return pltpu.CompilerParams(
        dimension_semantics=("arbitrary",), vmem_limit_bytes=mib * 1024 * 1024
    )


def whole(shape):
    return pl.BlockSpec(shape, lambda *_: (0,) * len(shape))


def shape_of(*shape, kind=BF16):
    return jax.ShapeDtypeStruct(shape, kind)


SCALAR = pl.BlockSpec(memory_space=pltpu.SMEM)


def project_kernel(mp_ref, state_ref, weight_ref, *refs):
    partial = product(state_ref[...], weight_ref[...]).astype(BF16)
    for partial_ref, (low, high) in zip(refs, PARTS):
        partial_ref[...] = partial[:, low:high]
    for k, turned_ref in enumerate(refs[len(PARTS) :]):
        place = lax.rem(mp_ref[0] + k, N_MP) * ROWS
        turned_ref[...] = state_ref[pl.ds(pl.multiple_of(place, ROWS), ROWS), :]


def project(mp, edge_state, down_weight):
    widths = [high - low for low, high in PARTS]
    return pl.pallas_call(
        project_kernel,
        grid=(1,),
        in_specs=[SCALAR, whole((EDGE_DEV, COLS)), whole((COLS, TRIP))],
        out_specs=[whole((EDGE_DEV, w)) for w in widths] + [whole((ROWS, COLS))] * N_MP,
        out_shape=[shape_of(EDGE_DEV, w) for w in widths] + [shape_of(ROWS, COLS)] * N_MP,
        compiler_params=params(24),
        name="project",
        cost_estimate=pl.CostEstimate(
            flops=2 * EDGE_DEV * COLS * TRIP, bytes_accessed=1500000, transcendentals=0
        ),
    )(mp, edge_state, down_weight)


def send_kernel(list_ref, a_ref, b_ref, c_ref, d_ref, out_ref, table):
    @pl.when(pl.program_id(0) == 0)
    def _():
        total = a_ref[...].astype(F32) + b_ref[...].astype(F32)
        total = total + (c_ref[...].astype(F32) + d_ref[...].astype(F32))
        table[...] = total.astype(BF16)

    out_ref[...] = product(picks(list_ref[...], EDGE_DEV), table[...]).astype(BF16)


SEND_BLOCK = 256


def send(lists, partials):
    width = partials[0].shape[1]
    return pl.pallas_call(
        send_kernel,
        grid=(SLOTS // SEND_BLOCK,),
        in_specs=[pl.BlockSpec((1, SEND_BLOCK), lambda i: (0, i))] + [whole((EDGE_DEV, width))] * N_MP,
        out_specs=pl.BlockSpec((SEND_BLOCK, width), lambda i: (i, 0)),
        out_shape=shape_of(SLOTS, width),
        scratch_shapes=[pltpu.VMEM((EDGE_DEV, width), BF16)],
        compiler_params=params(24),
        name="send",
        cost_estimate=pl.CostEstimate(
            flops=2 * SLOTS * EDGE_DEV * width, bytes_accessed=12000 * width, transcendentals=0
        ),
    )(lists, *partials)


TRIP_BLOCK = 256
TRIP_STEPS = TRIPS // TRIP_BLOCK
SLOT_BLOCK = 256
SUM_CHUNK = 2048


def triplet_kernel(
    groups, in_ref, live_ref, to_ref, basis_ref, weight_ref, table_ref, out_ref, table, values, padded
):
    step = pl.program_id(0)
    width = table_ref.shape[1]
    deep = SLOTS // groups

    @pl.when(step == 0)
    def _():
        padded[...] = jnp.zeros_like(padded)
        for h in range(groups):
            table[:, h * width : (h + 1) * width] = table_ref[h * deep : (h + 1) * deep, :]

    @pl.when(step < TRIP_STEPS)
    def _():
        padded[0:NSBF, :] = basis_ref[...] * live_ref[...].astype(F32)
        basis = padded[...]
        high = basis.astype(BF16)
        low = (basis - high.astype(F32)).astype(BF16)
        stacked = jnp.concatenate([high, low, high], axis=0)
        coef = lax.dot_general(
            stacked, weight_ref[...], (((0,), (0,)), ((), ())), preferred_element_type=F32
        )
        place = pl.multiple_of(step * TRIP_BLOCK, TRIP_BLOCK)
        source = column_of(in_ref[...])
        target = column_of(to_ref[:, pl.ds(place, TRIP_BLOCK)])
        candidates = product(picks_of(source & (deep - 1), deep), table[...])
        for k in range(0, width, 128):
            value = candidates[:, k : k + 128]
            for h in range(1, groups):
                at = h * width + k
                value = jnp.where(source >= h * deep, candidates[:, at : at + 128], value)
            value = value * coef[:, k : k + 128]
            for h in range(groups):
                at = h * width + k
                here = (target >= h * deep) & (target < (h + 1) * deep)
                values[pl.ds(place, TRIP_BLOCK), at : at + 128] = jnp.where(here, value, 0.0).astype(
                    BF16
                )

    @pl.when(step >= TRIP_STEPS)
    def _():
        first = (step - TRIP_STEPS) * SLOT_BLOCK

        def more(i, total):
            rows = pl.ds(pl.multiple_of(i * SUM_CHUNK, SUM_CHUNK), SUM_CHUNK)
            chosen = members(to_ref[:, rows] & (deep - 1), SLOT_BLOCK, first)
            return total + product(chosen, values[rows, :])

        empty = jnp.zeros((SLOT_BLOCK, groups * width), F32)
        total = lax.fori_loop(0, TRIPS // SUM_CHUNK, more, empty).astype(BF16)
        for h in range(groups):
            out_ref[h] = total[:, h * width : (h + 1) * width]


def triplets(trip_in, trip_live, trip_out, basis, weight, table):
    width = table.shape[1]
    groups = 512 // width
    deep = SLOTS // groups
    gather_step = lambda i: (0, jnp.minimum(i, TRIP_STEPS - 1))
    return pl.pallas_call(
        functools.partial(triplet_kernel, groups),
        grid=(TRIP_STEPS + deep // SLOT_BLOCK,),
        in_specs=[
            pl.BlockSpec((1, TRIP_BLOCK), gather_step),
            pl.BlockSpec((1, TRIP_BLOCK), gather_step),
            whole((1, TRIPS)),
            pl.BlockSpec((NSBF, TRIP_BLOCK), gather_step),
            whole((3 * BASIS_PAD, width)),
            whole((SLOTS, width)),
        ],
        out_specs=pl.BlockSpec(
            (groups, SLOT_BLOCK, width), lambda i: (0, jnp.maximum(i - TRIP_STEPS, 0), 0)
        ),
        out_shape=shape_of(groups, deep, width),
        scratch_shapes=[
            pltpu.VMEM((deep, groups * width), BF16),
            pltpu.VMEM((TRIPS, groups * width), BF16),
            pltpu.VMEM((BASIS_PAD, TRIP_BLOCK), F32),
        ],
        compiler_params=params(48),
        name="triplets",
        cost_estimate=pl.CostEstimate(
            flops=4 * TRIPS * SLOTS * width, bytes_accessed=18000 * width, transcendentals=0
        ),
    )(trip_in, trip_live, trip_out, basis, weight, table)


EDGE_CHUNK = 1024


def edges_kernel(mp_ref, list_ref, table_ref, *refs):
    earlier, outs, total = refs[: -N_MP - 1], refs[-N_MP - 1 : -1], refs[-1]
    step = pl.program_id(0)
    part = product(members(list_ref[...], EDGE_DEV, 0), table_ref[...])

    @pl.when(step == 0)
    def _():
        total[...] = part

    @pl.when(step > 0)
    def _():
        total[...] += part

    @pl.when(step == SLOTS // EDGE_CHUNK - 1)
    def _():
        for k, out_ref in enumerate(outs):
            place = lax.rem(mp_ref[0] + k, N_MP) * ROWS
            low = 0
            if earlier:
                low = earlier[k].shape[1]
                out_ref[:, :low] = earlier[k][...]
            out_ref[:, low:] = total[pl.ds(pl.multiple_of(place, ROWS), ROWS), :].astype(BF16)


def edges(mp, lists, returned, earlier):
    width = returned.shape[1]
    before = [block.shape[1] for block in earlier]
    full = width + (before[0] if before else 0)
    return pl.pallas_call(
        edges_kernel,
        grid=(SLOTS // EDGE_CHUNK,),
        in_specs=[
            SCALAR,
            pl.BlockSpec((1, EDGE_CHUNK), lambda i: (0, i)),
            pl.BlockSpec((EDGE_CHUNK, width), lambda i: (i, 0)),
        ]
        + [whole((ROWS, w)) for w in before],
        out_specs=[whole((ROWS, full))] * N_MP,
        out_shape=[shape_of(ROWS, full)] * N_MP,
        scratch_shapes=[pltpu.VMEM((EDGE_DEV, width), F32)],
        compiler_params=params(24),
        name="edges",
        cost_estimate=pl.CostEstimate(
            flops=2 * SLOTS * EDGE_DEV * width, bytes_accessed=9000 * width, transcendentals=0
        ),
    )(mp, lists, returned, *earlier)


SIDE = 4
MAP_STEPS = N_MP // SIDE


def layers_kernel(mp_ref, *refs):
    updates, refs = refs[:N_MP], refs[N_MP:]
    states, (up_ref, weight_ref), refs = refs[:N_MP], refs[N_MP : N_MP + 2], refs[N_MP + 2 :]
    outs = refs[:N_MP]
    hidden, given, inner = refs[N_MP:]
    step = pl.program_id(0)
    me = mp_ref[0]
    which = lax.div(step, MAP_STEPS)
    side = lax.rem(step, MAP_STEPS) * SIDE

    def columns(block):
        return pl.ds(pl.multiple_of(block * COLS, 128), COLS)

    @pl.when(step == 0)
    def _():
        a, b, c, d = (ref[...].astype(F32) for ref in updates)
        update = ((a + b) + (c + d)).astype(BF16)
        for k, state_ref in enumerate(states):
            hidden[:, columns(lax.rem(me + N_MP - k, N_MP))] = state_ref[...].astype(F32)
        for block in range(N_MP):
            added = product(update[:, :UP_HALF], up_ref[block])
            added = added + product(update[:, UP_HALF:], up_ref[N_MP + block])
            at = slice(block * COLS, (block + 1) * COLS)
            fresh = hidden[:, at] + added
            hidden[:, at] = fresh
            given[:, at] = fresh.astype(BF16)

    @pl.when(lax.rem(which, 2) == 0)
    def _():
        x = given[...]

        def one(j, carry):
            inner[:, columns(side + j)] = silu(product(x, weight_ref[j])).astype(BF16)
            return carry

        lax.fori_loop(0, SIDE, one, 0)

    @pl.when(lax.rem(which, 2) == 1)
    def _():
        x = inner[...]

        def one(j, carry):
            at = columns(side + j)
            fresh = (hidden[:, at] + silu(product(x, weight_ref[j]))) * inv_root_two
            hidden[:, at] = fresh
            given[:, at] = fresh.astype(BF16)
            return carry

        lax.fori_loop(0, SIDE, one, 0)

    @pl.when(step == MAPS * MAP_STEPS - 1)
    def _():
        for k, out_ref in enumerate(outs):
            out_ref[...] = given[:, columns(lax.rem(me + k, N_MP))]


def layers(mp, updates, states, gathered):
    def weight_block(i):
        which = i // MAP_STEPS
        side = i % MAP_STEPS
        return ((which // HALF_MAPS) * MAP_STEPS + side, which % HALF_MAPS, 0)

    return pl.pallas_call(
        layers_kernel,
        grid=(MAPS * MAP_STEPS,),
        in_specs=[SCALAR]
        + [whole((ROWS, TRIP))] * N_MP
        + [whole((ROWS, COLS))] * N_MP
        + [
            pl.BlockSpec(
                (N_CORE * N_MP, UP_HALF, COLS), lambda i: (0, HALF_MAPS * D // UP_HALF, 0)
            ),
            pl.BlockSpec((SIDE, D, COLS), weight_block),
        ],
        out_specs=[whole((ROWS, COLS))] * N_MP,
        out_shape=[shape_of(ROWS, COLS)] * N_MP,
        scratch_shapes=[
            pltpu.VMEM((ROWS, D), F32),
            pltpu.VMEM((ROWS, D), BF16),
            pltpu.VMEM((ROWS, D), BF16),
        ],
        compiler_params=params(40),
        name="layers",
        cost_estimate=pl.CostEstimate(
            flops=2 * ROWS * D * D * MAPS,
            bytes_accessed=2 * D * D * MAPS,
            transcendentals=ROWS * D * MAPS,
        ),
    )(mp, *updates, *states, gathered, gathered)


def at_block(ref, me, k):
    place = lax.rem(me + N_MP - k, N_MP) * ROWS
    return ref[:, pl.ds(pl.multiple_of(place, ROWS), ROWS)]


def atoms_kernel(mp_ref, core_ref, atom_ref, h0, h1, h2, h3, keep_ref, give_ref):
    me, core = mp_ref[0], core_ref[0]
    row = jnp.concatenate([at_block(atom_ref, me, k) for k in range(N_MP)], axis=1)
    hidden = jnp.concatenate([h0[...], h1[...], h2[...], h3[...]], axis=0)
    group = row // ATOM_DEV
    spot = (group // N_CORE) * ATOM_DEV + row % ATOM_DEV
    for out_ref, owner in ((keep_ref, core), (give_ref, 1 - core)):
        mine = jnp.where(group % N_CORE == owner, spot, -1)
        for first in range(0, HALF_ATOMS, BLOCK):
            part = product(members(mine, BLOCK, first), hidden)
            out_ref[first : first + BLOCK, :] = part.astype(BF16)


def atoms(mp, core, edge_atom, hiddens):
    return pl.pallas_call(
        atoms_kernel,
        grid=(1,),
        in_specs=[SCALAR, SCALAR, whole((1, EDGE_DEV))] + [whole((ROWS, COLS))] * N_MP,
        out_specs=[whole((HALF_ATOMS, COLS))] * 2,
        out_shape=[shape_of(HALF_ATOMS, COLS)] * 2,
        compiler_params=params(24),
        name="atoms",
        cost_estimate=pl.CostEstimate(
            flops=2 * ATOMS * EDGE_DEV * COLS, bytes_accessed=2000000, transcendentals=0
        ),
    )(mp, core, edge_atom, *hiddens)


def meet_kernel(x_ref, keep_ref, got_ref, *outs):
    for k, out_ref in enumerate(outs):
        place = lax.rem(x_ref[0] + k, N_X) * (HALF_ATOMS // N_X)
        rows = pl.ds(pl.multiple_of(place, HALF_ATOMS // N_X), HALF_ATOMS // N_X)
        out_ref[...] = (keep_ref[rows, :].astype(F32) + got_ref[rows, :].astype(F32)).astype(BF16)


def meet(x, keep, got):
    return pl.pallas_call(
        meet_kernel,
        grid=(1,),
        in_specs=[SCALAR] + [whole((HALF_ATOMS, COLS))] * 2,
        out_specs=[whole((HALF_ATOMS // N_X, COLS))] * N_X,
        out_shape=[shape_of(HALF_ATOMS // N_X, COLS)] * N_X,
        compiler_params=params(24),
        name="meet",
        cost_estimate=pl.CostEstimate(
            flops=HALF_ATOMS * COLS, bytes_accessed=2400000, transcendentals=0
        ),
    )(x, keep, got)


def final_kernel(mp_ref, core_ref, atom_ref, h0, h1, h2, h3, mine_ref, other_ref, out_ref):
    me, core = mp_ref[0], core_ref[0]
    for k, hidden_ref in enumerate((h0, h1, h2, h3)):
        row = at_block(atom_ref, me, k)
        group = row // ATOM_DEV
        spot = (group // N_CORE) * ATOM_DEV + row % ATOM_DEV
        near = jnp.where(group % N_CORE == core, spot, -1)
        far = jnp.where(group % N_CORE == core, -1, spot)
        taken = product(picks(near, HALF_ATOMS), mine_ref[...])
        taken = taken + product(picks(far, HALF_ATOMS), other_ref[...])
        place = lax.rem(me + N_MP - k, N_MP) * ROWS
        out_ref[pl.ds(pl.multiple_of(place, ROWS), ROWS), :] = (
            hidden_ref[...].astype(F32) + taken
        ).astype(BF16)


def final(mp, core, edge_atom, hiddens, mine, other):
    return pl.pallas_call(
        final_kernel,
        grid=(1,),
        in_specs=[SCALAR, SCALAR, whole((1, EDGE_DEV))]
        + [whole((ROWS, COLS))] * N_MP
        + [whole((HALF_ATOMS, COLS))] * 2,
        out_specs=whole((EDGE_DEV, COLS)),
        out_shape=shape_of(EDGE_DEV, COLS),
        compiler_params=params(24),
        name="final",
        cost_estimate=pl.CostEstimate(
            flops=2 * ATOMS * EDGE_DEV * COLS, bytes_accessed=2400000, transcendentals=0
        ),
    )(mp, core, edge_atom, *hiddens, mine, other)


def turn(array, axis, count, shift):
    return lax.ppermute(array, axis, [(i, (i + shift) % count) for i in range(count)])


def turned(blocks, axis):
    count = len(blocks)
    return [blocks[0]] + [turn(blocks[k], axis, count, k) for k in range(1, count)]


def summed(blocks):
    return jnp.sum(blocks.astype(F32), axis=0)


def local(
    edge_state,
    down_weight,
    basis,
    basis_weight,
    up_weight,
    dense_weight,
    send_rows,
    trip_in,
    trip_out,
    trip_live,
    edge_atom,
):
    mp = jnp.full((1,), lax.axis_index("mp"), I32)
    core_index = lax.axis_index("graph_2")
    core = jnp.full((1,), core_index, I32)
    lists = send_rows.reshape(1, SLOTS)
    atom_row = edge_atom.reshape(1, EDGE_DEV)
    high = basis_weight.astype(BF16)
    low = (basis_weight - high.astype(F32)).astype(BF16)
    pad = ((0, BASIS_PAD - NSBF), (0, 0))
    high, low = jnp.pad(high, pad), jnp.pad(low, pad)
    coef_weight = jnp.concatenate([high, high, low], axis=0)
    half = jnp.concatenate(
        [
            lax.dynamic_slice_in_dim(
                dense_weight.reshape(MAPS * D, COLS), core_index * (HALF_MAPS * D), HALF_MAPS * D, 0
            ),
            lax.dynamic_slice_in_dim(up_weight, core_index * UP_HALF, UP_HALF, 0),
        ],
        axis=0,
    )

    trip_in = trip_in.reshape(1, TRIPS)
    trip_live = trip_live.reshape(1, TRIPS)
    trip_out = trip_out.reshape(1, TRIPS)
    first, second, *state_blocks = project(mp, edge_state, down_weight)
    exchange = functools.partial(
        lax.all_to_all, axis_name=GRAPH, split_axis=0, concat_axis=0, tiled=True
    )

    def sums(received, part):
        low, high = part
        table = received.reshape(SLOTS, high - low)
        weight = coef_weight[:, low:high]
        total = triplets(trip_in, trip_live, trip_out, basis, weight, table)
        return total.reshape(N_GRAPH, CAP, high - low)

    first = send(lists, turned([first] * N_MP, "mp")).reshape(N_GRAPH, CAP, -1)
    first, second = lax.optimization_barrier((first, second))
    partials = turned([second] * N_MP, "mp")
    first = exchange(first)
    first, half, *partials = lax.optimization_barrier((first, half, *partials))
    second = exchange(send(lists, partials).reshape(N_GRAPH, CAP, -1))
    gathered = lax.all_gather(half, ("graph_2", "mp"), axis=0, tiled=False)
    states = turned(state_blocks, "mp")
    first = exchange(sums(first, PARTS[0]))
    second = exchange(sums(second, PARTS[1]))
    blocks = edges(mp, lists, first.reshape(SLOTS, -1), [])
    blocks = edges(mp, lists, second.reshape(SLOTS, -1), blocks)
    updates = turned(blocks, "mp")
    hiddens = turned(layers(mp, updates, states, gathered), "mp")
    keep, give = atoms(mp, core, atom_row, hiddens)
    x = jnp.full((1,), lax.axis_index("graph_0"), I32)
    parts = turned(meet(x, keep, turn(give, "graph_2", N_CORE, 1)), "graph_0")
    part = (parts[0].astype(F32) + parts[1].astype(F32)) + (
        parts[2].astype(F32) + parts[3].astype(F32)
    )
    part = part.astype(BF16).reshape(N_Z, ATOM_DEV, COLS)
    atom_sum = summed(lax.all_to_all(part, "graph_1", 0, 0, tiled=True))
    atom_out = jax.nn.silu(atom_scale * atom_sum).astype(BF16)
    table = lax.all_to_all(
        jnp.broadcast_to(atom_out[None], (N_Z, ATOM_DEV, COLS)), "graph_1", 0, 0, tiled=True
    ).reshape(N_Z * ATOM_DEV, COLS)
    table = lax.all_to_all(
        jnp.broadcast_to(table[None], (N_X, N_Z * ATOM_DEV, COLS)), "graph_0", 0, 0, tiled=True
    ).reshape(HALF_ATOMS, COLS)
    other = turn(table, "graph_2", N_CORE, 1)
    edge_out = final(mp, core, atom_row, hiddens, table, other)
    return (edge_out, atom_out)


def solution(mesh):
    split = Mesh(
        mesh.devices.reshape(N_X, N_Z, N_CORE, mesh.shape["mp"]),
        ("graph_0", "graph_1", "graph_2", "mp"),
    )
    return jax.shard_map(
        local,
        mesh=split,
        in_specs=(
            P(GRAPH, "mp"),
            P("mp", None),
            P(None, GRAPH_MP),
            P(),
            P(None, "mp"),
            P(None, None, None, "mp"),
            P(GRAPH, "mp", None),
            P(GRAPH_MP),
            P(GRAPH_MP),
            P(GRAPH_MP),
            P(GRAPH),
        ),
        out_specs=(P(GRAPH, "mp"), P(GRAPH, "mp")),
        check_vma=False,
    )
```

```python
import functools

import jax
import jax.numpy as jnp
from jax import lax
from jax.experimental import pallas as pl
from jax.experimental.pallas import tpu as pltpu
from jax.sharding import Mesh
from jax.sharding import PartitionSpec as P

ATOM_DEV = 32
GRAPH = ("graph_0", "graph_1", "graph_2")
GRAPH_MP = ("graph_0", "graph_1", "graph_2", "mp")
N_X, N_Z, N_CORE, N_MP = 4, 8, 2, 4
N_GRAPH = N_X * N_Z * N_CORE
CAP = 64
EDGE_DEV = 512
ROWS = EDGE_DEV // N_MP
SLOTS = N_GRAPH * CAP
TRIPS = 4096
NSBF = 42
BASIS_PAD = 48
D = 1536
COLS = D // N_MP
TRIP = 384
MAPS = 6
HALF_MAPS = MAPS // N_CORE
UP_HALF = TRIP // N_CORE
ATOMS = ATOM_DEV * N_GRAPH
HALF_ATOMS = ATOMS // N_CORE
ATOM_BLOCK = 256
PARTS = ((0, 128), (128, 384))

F32 = jnp.float32
BF16 = jnp.bfloat16
I32 = jnp.int32

inv_root_two = 0.7071067811865476
atom_scale = 0.2


def silu(v):
    return v / (1.0 + jnp.exp(-v))


def product(a, b):
    return jnp.dot(a, b, preferred_element_type=F32)


def ones_where(mask):
    return jnp.where(mask, jnp.ones((), F32), jnp.zeros((), F32)).astype(BF16)


def column_of(row):
    return jnp.broadcast_to(row, (128, row.shape[1])).T


def picks_of(column, count):
    lane = lax.broadcasted_iota(I32, column.shape, 1)
    return jnp.concatenate(
        [ones_where(column == lane + k) for k in range(0, count, 128)], axis=1
    )


def picks(row, count):
    return picks_of(column_of(row), count)


def members(row, count, first):
    place = lax.broadcasted_iota(I32, (count, 128), 0) + first
    return jnp.concatenate(
        [ones_where(place == row[:, k : k + 128]) for k in range(0, row.shape[1], 128)], axis=1
    )


def params(mib):
    return pltpu.CompilerParams(
        dimension_semantics=("arbitrary",), vmem_limit_bytes=mib * 1024 * 1024
    )


def whole(shape):
    return pl.BlockSpec(shape, lambda *_: (0,) * len(shape))


def shape_of(*shape, kind=BF16):
    return jax.ShapeDtypeStruct(shape, kind)


SCALAR = pl.BlockSpec(memory_space=pltpu.SMEM)


def project_kernel(mp_ref, state_ref, weight_ref, *refs):
    partial = product(state_ref[...], weight_ref[...]).astype(BF16)
    for partial_ref, (low, high) in zip(refs, PARTS):
        partial_ref[...] = partial[:, low:high]
    for k, turned_ref in enumerate(refs[len(PARTS) :]):
        place = lax.rem(mp_ref[0] + k, N_MP) * ROWS
        turned_ref[...] = state_ref[pl.ds(pl.multiple_of(place, ROWS), ROWS), :]


def project(mp, edge_state, down_weight):
    widths = [high - low for low, high in PARTS]
    return pl.pallas_call(
        project_kernel,
        grid=(1,),
        in_specs=[SCALAR, whole((EDGE_DEV, COLS)), whole((COLS, TRIP))],
        out_specs=[whole((EDGE_DEV, w)) for w in widths] + [whole((ROWS, COLS))] * N_MP,
        out_shape=[shape_of(EDGE_DEV, w) for w in widths] + [shape_of(ROWS, COLS)] * N_MP,
        compiler_params=params(62),
        name="project",
        cost_estimate=pl.CostEstimate(
            flops=2 * EDGE_DEV * COLS * TRIP, bytes_accessed=1500000, transcendentals=0
        ),
    )(mp, edge_state, down_weight)


def send_kernel(list_ref, a_ref, b_ref, c_ref, d_ref, out_ref, table):
    @pl.when(pl.program_id(0) == 0)
    def _():
        total = a_ref[...].astype(F32) + b_ref[...].astype(F32)
        total = total + (c_ref[...].astype(F32) + d_ref[...].astype(F32))
        table[...] = total.astype(BF16)

    out_ref[...] = product(picks(list_ref[...], EDGE_DEV), table[...]).astype(BF16)


SEND_BLOCK = 1024


def send(lists, partials):
    width = partials[0].shape[1]
    return pl.pallas_call(
        send_kernel,
        grid=(SLOTS // SEND_BLOCK,),
        in_specs=[pl.BlockSpec((1, SEND_BLOCK), lambda i: (0, i))] + [whole((EDGE_DEV, width))] * N_MP,
        out_specs=pl.BlockSpec((SEND_BLOCK, width), lambda i: (i, 0)),
        out_shape=shape_of(SLOTS, width),
        scratch_shapes=[pltpu.VMEM((EDGE_DEV, width), BF16)],
        compiler_params=params(24),
        name="send",
        cost_estimate=pl.CostEstimate(
            flops=2 * SLOTS * EDGE_DEV * width, bytes_accessed=12000 * width, transcendentals=0
        ),
    )(lists, *partials)


TRIP_BLOCK = 256
TRIP_STEPS = TRIPS // TRIP_BLOCK
SLOT_BLOCK = 256
SUM_CHUNK = 2048


def triplet_kernel(
    groups, in_ref, live_ref, to_ref, basis_ref, weight_ref, table_ref, out_ref, table, values, padded
):
    step = pl.program_id(0)
    width = table_ref.shape[1]
    deep = SLOTS // groups

    @pl.when(step == 0)
    def _():
        padded[...] = jnp.zeros_like(padded)
        for h in range(groups):
            table[:, h * width : (h + 1) * width] = table_ref[h * deep : (h + 1) * deep, :]

    @pl.when(step < TRIP_STEPS)
    def _():
        padded[0:NSBF, :] = basis_ref[...] * live_ref[...].astype(F32)
        basis = padded[...]
        high = basis.astype(BF16)
        low = (basis - high.astype(F32)).astype(BF16)
        stacked = jnp.concatenate([high, low, high], axis=0)
        coef = lax.dot_general(
            stacked, weight_ref[...], (((0,), (0,)), ((), ())), preferred_element_type=F32
        )
        place = pl.multiple_of(step * TRIP_BLOCK, TRIP_BLOCK)
        source = column_of(in_ref[...])
        target = column_of(to_ref[:, pl.ds(place, TRIP_BLOCK)])
        candidates = product(picks_of(source & (deep - 1), deep), table[...])
        for k in range(0, width, 128):
            value = candidates[:, k : k + 128]
            for h in range(1, groups):
                at = h * width + k
                value = jnp.where(source >= h * deep, candidates[:, at : at + 128], value)
            value = value * coef[:, k : k + 128]
            for h in range(groups):
                at = h * width + k
                here = (target >= h * deep) & (target < (h + 1) * deep)
                values[pl.ds(place, TRIP_BLOCK), at : at + 128] = jnp.where(here, value, 0.0).astype(
                    BF16
                )

    @pl.when(step >= TRIP_STEPS)
    def _():
        first = (step - TRIP_STEPS) * SLOT_BLOCK

        def more(i, total):
            rows = pl.ds(pl.multiple_of(i * SUM_CHUNK, SUM_CHUNK), SUM_CHUNK)
            chosen = members(to_ref[:, rows] & (deep - 1), SLOT_BLOCK, first)
            return total + product(chosen, values[rows, :])

        empty = jnp.zeros((SLOT_BLOCK, groups * width), F32)
        total = lax.fori_loop(0, TRIPS // SUM_CHUNK, more, empty).astype(BF16)
        for h in range(groups):
            out_ref[h] = total[:, h * width : (h + 1) * width]


def triplets(trip_in, trip_live, trip_out, basis, weight, table):
    width = table.shape[1]
    groups = 512 // width
    deep = SLOTS // groups
    gather_step = lambda i: (0, jnp.minimum(i, TRIP_STEPS - 1))
    return pl.pallas_call(
        functools.partial(triplet_kernel, groups),
        grid=(TRIP_STEPS + deep // SLOT_BLOCK,),
        in_specs=[
            pl.BlockSpec((1, TRIP_BLOCK), gather_step),
            pl.BlockSpec((1, TRIP_BLOCK), gather_step),
            whole((1, TRIPS)),
            pl.BlockSpec((NSBF, TRIP_BLOCK), gather_step),
            whole((3 * BASIS_PAD, width)),
            whole((SLOTS, width)),
        ],
        out_specs=pl.BlockSpec(
            (groups, SLOT_BLOCK, width), lambda i: (0, jnp.maximum(i - TRIP_STEPS, 0), 0)
        ),
        out_shape=shape_of(groups, deep, width),
        scratch_shapes=[
            pltpu.VMEM((deep, groups * width), BF16),
            pltpu.VMEM((TRIPS, groups * width), BF16),
            pltpu.VMEM((BASIS_PAD, TRIP_BLOCK), F32),
        ],
        compiler_params=params(48),
        name="triplets",
        cost_estimate=pl.CostEstimate(
            flops=4 * TRIPS * SLOTS * width, bytes_accessed=18000 * width, transcendentals=0
        ),
    )(trip_in, trip_live, trip_out, basis, weight, table)


EDGE_CHUNK = 1024


def edges_kernel(mp_ref, list_ref, table_ref, *refs):
    earlier, outs, total = refs[: -N_MP - 1], refs[-N_MP - 1 : -1], refs[-1]
    step = pl.program_id(0)
    part = product(members(list_ref[...], EDGE_DEV, 0), table_ref[...])

    @pl.when(step == 0)
    def _():
        total[...] = part

    @pl.when(step > 0)
    def _():
        total[...] += part

    @pl.when(step == SLOTS // EDGE_CHUNK - 1)
    def _():
        for k, out_ref in enumerate(outs):
            place = lax.rem(mp_ref[0] + k, N_MP) * ROWS
            low = 0
            if earlier:
                low = earlier[k].shape[1]
                out_ref[:, :low] = earlier[k][...]
            out_ref[:, low:] = total[pl.ds(pl.multiple_of(place, ROWS), ROWS), :].astype(BF16)


def edges(mp, lists, returned, earlier):
    width = returned.shape[1]
    before = [block.shape[1] for block in earlier]
    full = width + (before[0] if before else 0)
    return pl.pallas_call(
        edges_kernel,
        grid=(SLOTS // EDGE_CHUNK,),
        in_specs=[
            SCALAR,
            pl.BlockSpec((1, EDGE_CHUNK), lambda i: (0, i)),
            pl.BlockSpec((EDGE_CHUNK, width), lambda i: (i, 0)),
        ]
        + [whole((ROWS, w)) for w in before],
        out_specs=[whole((ROWS, full))] * N_MP,
        out_shape=[shape_of(ROWS, full)] * N_MP,
        scratch_shapes=[pltpu.VMEM((EDGE_DEV, width), F32)],
        compiler_params=params(24),
        name="edges",
        cost_estimate=pl.CostEstimate(
            flops=2 * SLOTS * EDGE_DEV * width, bytes_accessed=9000 * width, transcendentals=0
        ),
    )(mp, lists, returned, *earlier)


SIDE = 4
MAP_STEPS = N_MP // SIDE


def layers_kernel(mp_ref, *refs):
    updates, refs = refs[:N_MP], refs[N_MP:]
    states, (up_ref, weight_ref), refs = refs[:N_MP], refs[N_MP : N_MP + 2], refs[N_MP + 2 :]
    outs = refs[:N_MP]
    hidden, given, inner = refs[N_MP:]
    step = pl.program_id(0)
    me = mp_ref[0]
    which = lax.div(step, MAP_STEPS)
    side = lax.rem(step, MAP_STEPS) * SIDE

    def columns(block):
        return pl.ds(pl.multiple_of(block * COLS, 128), COLS)

    @pl.when(step == 0)
    def _():
        a, b, c, d = (ref[...].astype(F32) for ref in updates)
        update = ((a + b) + (c + d)).astype(BF16)
        for k, state_ref in enumerate(states):
            hidden[:, columns(lax.rem(me + N_MP - k, N_MP))] = state_ref[...].astype(F32)
        for block in range(N_MP):
            added = product(update[:, :UP_HALF], up_ref[block])
            added = added + product(update[:, UP_HALF:], up_ref[N_MP + block])
            at = slice(block * COLS, (block + 1) * COLS)
            fresh = hidden[:, at] + added
            hidden[:, at] = fresh
            given[:, at] = fresh.astype(BF16)

    @pl.when(lax.rem(which, 2) == 0)
    def _():
        x = given[...]

        def one(j, carry):
            inner[:, columns(side + j)] = silu(product(x, weight_ref[j])).astype(BF16)
            return carry

        lax.fori_loop(0, SIDE, one, 0, unroll=True)

    @pl.when(lax.rem(which, 2) == 1)
    def _():
        x = inner[...]

        def one(j, carry):
            at = columns(side + j)
            fresh = (hidden[:, at] + silu(product(x, weight_ref[j]))) * inv_root_two
            hidden[:, at] = fresh
            given[:, at] = fresh.astype(BF16)
            return carry

        lax.fori_loop(0, SIDE, one, 0, unroll=True)

    @pl.when(step == MAPS * MAP_STEPS - 1)
    def _():
        for k, out_ref in enumerate(outs):
            out_ref[...] = given[:, columns(lax.rem(me + k, N_MP))]


def layers(mp, updates, states, gathered):
    def weight_block(i):
        which = i // MAP_STEPS
        side = i % MAP_STEPS
        return ((which // HALF_MAPS) * MAP_STEPS + side, which % HALF_MAPS, 0)

    return pl.pallas_call(
        layers_kernel,
        grid=(MAPS * MAP_STEPS,),
        in_specs=[SCALAR]
        + [whole((ROWS, TRIP))] * N_MP
        + [whole((ROWS, COLS))] * N_MP
        + [
            pl.BlockSpec(
                (N_CORE * N_MP, UP_HALF, COLS), lambda i: (0, HALF_MAPS * D // UP_HALF, 0)
            ),
            pl.BlockSpec((SIDE, D, COLS), weight_block),
        ],
        out_specs=[whole((ROWS, COLS))] * N_MP,
        out_shape=[shape_of(ROWS, COLS)] * N_MP,
        scratch_shapes=[
            pltpu.VMEM((ROWS, D), F32),
            pltpu.VMEM((ROWS, D), BF16),
            pltpu.VMEM((ROWS, D), BF16),
        ],
        compiler_params=params(40),
        name="layers",
        cost_estimate=pl.CostEstimate(
            flops=2 * ROWS * D * D * MAPS,
            bytes_accessed=2 * D * D * MAPS,
            transcendentals=ROWS * D * MAPS,
        ),
    )(mp, *updates, *states, gathered, gathered)


def at_block(ref, me, k):
    place = lax.rem(me + N_MP - k, N_MP) * ROWS
    return ref[:, pl.ds(pl.multiple_of(place, ROWS), ROWS)]


def atoms_kernel(mp_ref, core_ref, atom_ref, h0, h1, h2, h3, keep_ref, give_ref):
    me, core = mp_ref[0], core_ref[0]
    row = jnp.concatenate([at_block(atom_ref, me, k) for k in range(N_MP)], axis=1)
    hidden = jnp.concatenate([h0[...], h1[...], h2[...], h3[...]], axis=0)
    group = row // ATOM_DEV
    spot = (group // N_CORE) * ATOM_DEV + row % ATOM_DEV
    for out_ref, owner in ((keep_ref, core), (give_ref, 1 - core)):
        mine = jnp.where(group % N_CORE == owner, spot, -1)

        def one(i, carry):
            first = pl.multiple_of(i * ATOM_BLOCK, ATOM_BLOCK)
            part = product(members(mine, ATOM_BLOCK, first), hidden)
            out_ref[pl.ds(first, ATOM_BLOCK), :] = part.astype(BF16)
            return carry

        lax.fori_loop(0, HALF_ATOMS // ATOM_BLOCK, one, 0)


def atoms(mp, core, edge_atom, hiddens):
    return pl.pallas_call(
        atoms_kernel,
        grid=(1,),
        in_specs=[SCALAR, SCALAR, whole((1, EDGE_DEV))] + [whole((ROWS, COLS))] * N_MP,
        out_specs=[whole((HALF_ATOMS, COLS))] * 2,
        out_shape=[shape_of(HALF_ATOMS, COLS)] * 2,
        compiler_params=params(24),
        name="atoms",
        cost_estimate=pl.CostEstimate(
            flops=2 * ATOMS * EDGE_DEV * COLS, bytes_accessed=2000000, transcendentals=0
        ),
    )(mp, core, edge_atom, *hiddens)


def meet_kernel(x_ref, keep_ref, got_ref, *outs):
    for k, out_ref in enumerate(outs):
        place = lax.rem(x_ref[0] + k, N_X) * (HALF_ATOMS // N_X)
        rows = pl.ds(pl.multiple_of(place, HALF_ATOMS // N_X), HALF_ATOMS // N_X)
        out_ref[...] = (keep_ref[rows, :].astype(F32) + got_ref[rows, :].astype(F32)).astype(BF16)


def meet(x, keep, got):
    return pl.pallas_call(
        meet_kernel,
        grid=(1,),
        in_specs=[SCALAR] + [whole((HALF_ATOMS, COLS))] * 2,
        out_specs=[whole((HALF_ATOMS // N_X, COLS))] * N_X,
        out_shape=[shape_of(HALF_ATOMS // N_X, COLS)] * N_X,
        compiler_params=params(24),
        name="meet",
        cost_estimate=pl.CostEstimate(
            flops=HALF_ATOMS * COLS, bytes_accessed=2400000, transcendentals=0
        ),
    )(x, keep, got)


def final_kernel(mp_ref, core_ref, atom_ref, h0, h1, h2, h3, mine_ref, other_ref, out_ref):
    me, core = mp_ref[0], core_ref[0]
    for k, hidden_ref in enumerate((h0, h1, h2, h3)):
        row = at_block(atom_ref, me, k)
        group = row // ATOM_DEV
        spot = (group // N_CORE) * ATOM_DEV + row % ATOM_DEV
        near = jnp.where(group % N_CORE == core, spot, -1)
        far = jnp.where(group % N_CORE == core, -1, spot)
        taken = product(picks(near, HALF_ATOMS), mine_ref[...])
        taken = taken + product(picks(far, HALF_ATOMS), other_ref[...])
        place = lax.rem(me + N_MP - k, N_MP) * ROWS
        out_ref[pl.ds(pl.multiple_of(place, ROWS), ROWS), :] = (
            hidden_ref[...].astype(F32) + taken
        ).astype(BF16)


def final(mp, core, edge_atom, hiddens, mine, other):
    return pl.pallas_call(
        final_kernel,
        grid=(1,),
        in_specs=[SCALAR, SCALAR, whole((1, EDGE_DEV))]
        + [whole((ROWS, COLS))] * N_MP
        + [whole((HALF_ATOMS, COLS))] * 2,
        out_specs=whole((EDGE_DEV, COLS)),
        out_shape=shape_of(EDGE_DEV, COLS),
        compiler_params=params(24),
        name="final",
        cost_estimate=pl.CostEstimate(
            flops=2 * ATOMS * EDGE_DEV * COLS, bytes_accessed=2400000, transcendentals=0
        ),
    )(mp, core, edge_atom, *hiddens, mine, other)


def turn(array, axis, count, shift):
    return lax.ppermute(array, axis, [(i, (i + shift) % count) for i in range(count)])


def turned(blocks, axis):
    count = len(blocks)
    return [blocks[0]] + [turn(blocks[k], axis, count, k) for k in range(1, count)]


def summed(blocks):
    return jnp.sum(blocks.astype(F32), axis=0)


def local(
    edge_state,
    down_weight,
    basis,
    basis_weight,
    up_weight,
    dense_weight,
    send_rows,
    trip_in,
    trip_out,
    trip_live,
    edge_atom,
):
    mp = jnp.full((1,), lax.axis_index("mp"), I32)
    core_index = lax.axis_index("graph_2")
    core = jnp.full((1,), core_index, I32)
    lists = send_rows.reshape(1, SLOTS)
    atom_row = edge_atom.reshape(1, EDGE_DEV)
    high = basis_weight.astype(BF16)
    low = (basis_weight - high.astype(F32)).astype(BF16)
    pad = ((0, BASIS_PAD - NSBF), (0, 0))
    high, low = jnp.pad(high, pad), jnp.pad(low, pad)
    coef_weight = jnp.concatenate([high, high, low], axis=0)
    half = jnp.concatenate(
        [
            lax.dynamic_slice_in_dim(
                dense_weight.reshape(MAPS * D, COLS), core_index * (HALF_MAPS * D), HALF_MAPS * D, 0
            ),
            lax.dynamic_slice_in_dim(up_weight, core_index * UP_HALF, UP_HALF, 0),
        ],
        axis=0,
    )

    trip_in = trip_in.reshape(1, TRIPS)
    trip_live = trip_live.reshape(1, TRIPS)
    trip_out = trip_out.reshape(1, TRIPS)
    first, second, *state_blocks = project(mp, edge_state, down_weight)
    exchange = functools.partial(
        lax.all_to_all, axis_name=GRAPH, split_axis=0, concat_axis=0, tiled=True
    )

    def sums(received, part):
        low, high = part
        table = received.reshape(SLOTS, high - low)
        weight = coef_weight[:, low:high]
        total = triplets(trip_in, trip_live, trip_out, basis, weight, table)
        return total.reshape(N_GRAPH, CAP, high - low)

    first = send(lists, turned([first] * N_MP, "mp")).reshape(N_GRAPH, CAP, -1)
    first, second = lax.optimization_barrier((first, second))
    partials = turned([second] * N_MP, "mp")
    first = exchange(first)
    second = send(lists, partials).reshape(N_GRAPH, CAP, -1)
    first, second, half = lax.optimization_barrier((first, second, half))
    second = exchange(second)
    gathered = lax.all_gather(half, ("graph_2", "mp"), axis=0, tiled=False)
    states = turned(state_blocks, "mp")
    first = exchange(sums(first, PARTS[0]))
    second = exchange(sums(second, PARTS[1]))
    blocks = edges(mp, lists, first.reshape(SLOTS, -1), [])
    blocks = edges(mp, lists, second.reshape(SLOTS, -1), blocks)
    updates = turned(blocks, "mp")
    hiddens = turned(layers(mp, updates, states, gathered), "mp")
    keep, give = atoms(mp, core, atom_row, hiddens)
    x = jnp.full((1,), lax.axis_index("graph_0"), I32)
    parts = turned(meet(x, keep, turn(give, "graph_2", N_CORE, 1)), "graph_0")
    part = (parts[0].astype(F32) + parts[1].astype(F32)) + (
        parts[2].astype(F32) + parts[3].astype(F32)
    )
    part = part.astype(BF16).reshape(N_Z, ATOM_DEV, COLS)
    atom_sum = summed(lax.all_to_all(part, "graph_1", 0, 0, tiled=True))
    atom_out = jax.nn.silu(atom_scale * atom_sum).astype(BF16)
    table = lax.all_to_all(
        jnp.broadcast_to(atom_out[None], (N_Z, ATOM_DEV, COLS)), "graph_1", 0, 0, tiled=True
    ).reshape(N_Z * ATOM_DEV, COLS)
    table = lax.all_to_all(
        jnp.broadcast_to(table[None], (N_X, N_Z * ATOM_DEV, COLS)), "graph_0", 0, 0, tiled=True
    ).reshape(HALF_ATOMS, COLS)
    other = turn(table, "graph_2", N_CORE, 1)
    edge_out = final(mp, core, atom_row, hiddens, table, other)
    return (edge_out, atom_out)


def solution(mesh):
    split = Mesh(
        mesh.devices.reshape(N_X, N_Z, N_CORE, mesh.shape["mp"]),
        ("graph_0", "graph_1", "graph_2", "mp"),
    )
    return jax.shard_map(
        local,
        mesh=split,
        in_specs=(
            P(GRAPH, "mp"),
            P("mp", None),
            P(None, GRAPH_MP),
            P(),
            P(None, "mp"),
            P(None, None, None, "mp"),
            P(GRAPH, "mp", None),
            P(GRAPH_MP),
            P(GRAPH_MP),
            P(GRAPH_MP),
            P(GRAPH),
        ),
        out_specs=(P(GRAPH, "mp"), P(GRAPH, "mp")),
        check_vma=False,
    )
```

```python
import functools

import jax
import jax.numpy as jnp
from jax import lax
from jax.experimental import pallas as pl
from jax.experimental.pallas import tpu as pltpu
from jax.sharding import Mesh
from jax.sharding import PartitionSpec as P

ATOM_DEV = 32
GRAPH = ("graph_0", "graph_1", "graph_2")
GRAPH_MP = ("graph_0", "graph_1", "graph_2", "mp")
N_X, N_Z, N_CORE, N_MP = 4, 8, 2, 4
N_GRAPH = N_X * N_Z * N_CORE
CAP = 64
EDGE_DEV = 512
ROWS = EDGE_DEV // N_MP
SLOTS = N_GRAPH * CAP
TRIPS = 4096
NSBF = 42
BASIS_PAD = 48
D = 1536
COLS = D // N_MP
TRIP = 384
MAPS = 6
HALF_MAPS = MAPS // N_CORE
UP_HALF = TRIP // N_CORE
ATOMS = ATOM_DEV * N_GRAPH
HALF_ATOMS = ATOMS // N_CORE
BLOCK = 512
ATOM_BLOCK = 256
PARTS = ((0, 128), (128, 384))

F32 = jnp.float32
BF16 = jnp.bfloat16
I32 = jnp.int32

inv_root_two = 0.7071067811865476
atom_scale = 0.2


def silu(v):
    return v / (1.0 + jnp.exp(-v))


def product(a, b):
    return jnp.dot(a, b, preferred_element_type=F32)


def ones_where(mask):
    return jnp.where(mask, jnp.ones((), F32), jnp.zeros((), F32)).astype(BF16)


def column_of(row):
    return jnp.broadcast_to(row, (128, row.shape[1])).T


def picks_of(column, count):
    lane = lax.broadcasted_iota(I32, column.shape, 1)
    return jnp.concatenate(
        [ones_where(column == lane + k) for k in range(0, count, 128)], axis=1
    )


def picks(row, count):
    return picks_of(column_of(row), count)


def members(row, count, first):
    place = lax.broadcasted_iota(I32, (count, 128), 0) + first
    return jnp.concatenate(
        [ones_where(place == row[:, k : k + 128]) for k in range(0, row.shape[1], 128)], axis=1
    )


def params(mib):
    return pltpu.CompilerParams(
        dimension_semantics=("arbitrary",), vmem_limit_bytes=mib * 1024 * 1024
    )


def whole(shape):
    return pl.BlockSpec(shape, lambda *_: (0,) * len(shape))


def shape_of(*shape, kind=BF16):
    return jax.ShapeDtypeStruct(shape, kind)


SCALAR = pl.BlockSpec(memory_space=pltpu.SMEM)


def project_kernel(mp_ref, state_ref, weight_ref, *refs):
    partial = product(state_ref[...], weight_ref[...]).astype(BF16)
    for partial_ref, (low, high) in zip(refs, PARTS):
        partial_ref[...] = partial[:, low:high]
    for k, turned_ref in enumerate(refs[len(PARTS) :]):
        place = lax.rem(mp_ref[0] + k, N_MP) * ROWS
        turned_ref[...] = state_ref[pl.ds(pl.multiple_of(place, ROWS), ROWS), :]


def project(mp, edge_state, down_weight):
    widths = [high - low for low, high in PARTS]
    return pl.pallas_call(
        project_kernel,
        grid=(1,),
        in_specs=[SCALAR, whole((EDGE_DEV, COLS)), whole((COLS, TRIP))],
        out_specs=[whole((EDGE_DEV, w)) for w in widths] + [whole((ROWS, COLS))] * N_MP,
        out_shape=[shape_of(EDGE_DEV, w) for w in widths] + [shape_of(ROWS, COLS)] * N_MP,
        compiler_params=params(62),
        name="project",
        cost_estimate=pl.CostEstimate(
            flops=2 * EDGE_DEV * COLS * TRIP, bytes_accessed=1500000, transcendentals=0
        ),
    )(mp, edge_state, down_weight)


def send_kernel(list_ref, a_ref, b_ref, c_ref, d_ref, out_ref, table):
    @pl.when(pl.program_id(0) == 0)
    def _():
        total = a_ref[...].astype(F32) + b_ref[...].astype(F32)
        total = total + (c_ref[...].astype(F32) + d_ref[...].astype(F32))
        table[...] = total.astype(BF16)

    out_ref[...] = product(picks(list_ref[...], EDGE_DEV), table[...]).astype(BF16)


SEND_BLOCK = 1024


def send(lists, partials):
    width = partials[0].shape[1]
    return pl.pallas_call(
        send_kernel,
        grid=(SLOTS // SEND_BLOCK,),
        in_specs=[pl.BlockSpec((1, SEND_BLOCK), lambda i: (0, i))] + [whole((EDGE_DEV, width))] * N_MP,
        out_specs=pl.BlockSpec((SEND_BLOCK, width), lambda i: (i, 0)),
        out_shape=shape_of(SLOTS, width),
        scratch_shapes=[pltpu.VMEM((EDGE_DEV, width), BF16)],
        compiler_params=params(24),
        name="send",
        cost_estimate=pl.CostEstimate(
            flops=2 * SLOTS * EDGE_DEV * width, bytes_accessed=12000 * width, transcendentals=0
        ),
    )(lists, *partials)


TRIP_BLOCK = 512
TRIP_STEPS = TRIPS // TRIP_BLOCK
SLOT_BLOCK = 512
SUM_CHUNK = 1024


def triplet_kernel(
    groups, in_ref, live_ref, to_ref, basis_ref, weight_ref, table_ref, out_ref, table, values, padded
):
    step = pl.program_id(0)
    width = table_ref.shape[1]
    deep = SLOTS // groups

    @pl.when(step == 0)
    def _():
        padded[...] = jnp.zeros_like(padded)
        for h in range(groups):
            table[:, h * width : (h + 1) * width] = table_ref[h * deep : (h + 1) * deep, :]

    @pl.when(step < TRIP_STEPS)
    def _():
        padded[0:NSBF, :] = basis_ref[...] * live_ref[...].astype(F32)
        basis = padded[...]
        high = basis.astype(BF16)
        low = (basis - high.astype(F32)).astype(BF16)
        stacked = jnp.concatenate([high, low, high], axis=0)
        coef = lax.dot_general(
            stacked, weight_ref[...], (((0,), (0,)), ((), ())), preferred_element_type=F32
        )
        place = pl.multiple_of(step * TRIP_BLOCK, TRIP_BLOCK)
        source = column_of(in_ref[...])
        target = column_of(to_ref[:, pl.ds(place, TRIP_BLOCK)])
        spot = source & (deep - 1)

        def more(i, total):
            first = pl.multiple_of(i * SUM_CHUNK, SUM_CHUNK)
            return total + product(
                picks_of(spot - first, SUM_CHUNK), table[pl.ds(first, SUM_CHUNK), :]
            )

        candidates = product(picks_of(spot, SUM_CHUNK), table[:SUM_CHUNK, :])
        if deep > SUM_CHUNK:
            candidates = lax.fori_loop(1, deep // SUM_CHUNK, more, candidates)
        for k in range(0, width, 128):
            value = candidates[:, k : k + 128]
            for h in range(1, groups):
                at = h * width + k
                value = jnp.where(source >= h * deep, candidates[:, at : at + 128], value)
            value = value * coef[:, k : k + 128]
            for h in range(groups):
                at = h * width + k
                here = (target >= h * deep) & (target < (h + 1) * deep)
                values[pl.ds(place, TRIP_BLOCK), at : at + 128] = jnp.where(here, value, 0.0).astype(
                    BF16
                )

    @pl.when(step >= TRIP_STEPS)
    def _():
        first = (step - TRIP_STEPS) * SLOT_BLOCK

        def more(i, total):
            rows = pl.ds(pl.multiple_of(i * SUM_CHUNK, SUM_CHUNK), SUM_CHUNK)
            chosen = members(to_ref[:, rows] & (deep - 1), SLOT_BLOCK, first)
            return total + product(chosen, values[rows, :])

        empty = jnp.zeros((SLOT_BLOCK, groups * width), F32)
        total = lax.fori_loop(0, TRIPS // SUM_CHUNK, more, empty).astype(BF16)
        for h in range(groups):
            out_ref[h] = total[:, h * width : (h + 1) * width]


def triplets(trip_in, trip_live, trip_out, basis, weight, table):
    width = table.shape[1]
    groups = 512 // width
    deep = SLOTS // groups
    gather_step = lambda i: (0, jnp.minimum(i, TRIP_STEPS - 1))
    return pl.pallas_call(
        functools.partial(triplet_kernel, groups),
        grid=(TRIP_STEPS + deep // SLOT_BLOCK,),
        in_specs=[
            pl.BlockSpec((1, TRIP_BLOCK), gather_step),
            pl.BlockSpec((1, TRIP_BLOCK), gather_step),
            whole((1, TRIPS)),
            pl.BlockSpec((NSBF, TRIP_BLOCK), gather_step),
            whole((3 * BASIS_PAD, width)),
            whole((SLOTS, width)),
        ],
        out_specs=pl.BlockSpec(
            (groups, SLOT_BLOCK, width), lambda i: (0, jnp.maximum(i - TRIP_STEPS, 0), 0)
        ),
        out_shape=shape_of(groups, deep, width),
        scratch_shapes=[
            pltpu.VMEM((deep, groups * width), BF16),
            pltpu.VMEM((TRIPS, groups * width), BF16),
            pltpu.VMEM((BASIS_PAD, TRIP_BLOCK), F32),
        ],
        compiler_params=params(48),
        name="triplets",
        cost_estimate=pl.CostEstimate(
            flops=4 * TRIPS * SLOTS * width, bytes_accessed=18000 * width, transcendentals=0
        ),
    )(trip_in, trip_live, trip_out, basis, weight, table)


EDGE_CHUNK = 2048


def edges_kernel(mp_ref, list_ref, table_ref, *refs):
    earlier, outs, total = refs[: -N_MP - 1], refs[-N_MP - 1 : -1], refs[-1]
    step = pl.program_id(0)

    @pl.when(step == 0)
    def _():
        total[...] = jnp.zeros_like(total)

    def more(i, carry):
        rows = pl.ds(pl.multiple_of(i * BLOCK, BLOCK), BLOCK)
        total[...] += product(members(list_ref[:, rows], EDGE_DEV, 0), table_ref[rows, :])
        return carry

    lax.fori_loop(0, EDGE_CHUNK // BLOCK, more, 0)

    @pl.when(step == SLOTS // EDGE_CHUNK - 1)
    def _():
        for k, out_ref in enumerate(outs):
            place = lax.rem(mp_ref[0] + k, N_MP) * ROWS
            low = 0
            if earlier:
                low = earlier[k].shape[1]
                out_ref[:, :low] = earlier[k][...]
            out_ref[:, low:] = total[pl.ds(pl.multiple_of(place, ROWS), ROWS), :].astype(BF16)


def edges(mp, lists, returned, earlier):
    width = returned.shape[1]
    before = [block.shape[1] for block in earlier]
    full = width + (before[0] if before else 0)
    return pl.pallas_call(
        edges_kernel,
        grid=(SLOTS // EDGE_CHUNK,),
        in_specs=[
            SCALAR,
            pl.BlockSpec((1, EDGE_CHUNK), lambda i: (0, i)),
            pl.BlockSpec((EDGE_CHUNK, width), lambda i: (i, 0)),
        ]
        + [whole((ROWS, w)) for w in before],
        out_specs=[whole((ROWS, full))] * N_MP,
        out_shape=[shape_of(ROWS, full)] * N_MP,
        scratch_shapes=[pltpu.VMEM((EDGE_DEV, width), F32)],
        compiler_params=params(24),
        name="edges",
        cost_estimate=pl.CostEstimate(
            flops=2 * SLOTS * EDGE_DEV * width, bytes_accessed=9000 * width, transcendentals=0
        ),
    )(mp, lists, returned, *earlier)


WIDE = 2 * COLS


def layers_kernel(mp_ref, *refs):
    updates, states, weight_ref = refs[:N_MP], refs[N_MP : 2 * N_MP], refs[2 * N_MP]
    refs = refs[2 * N_MP + 1 :]
    outs, (hidden, given, inner, up, weights, up_sem, sems) = refs[:N_MP], refs[N_MP:]
    me = mp_ref[0]

    def fetch(i):
        which, block = i // N_MP, i % N_MP
        return pltpu.make_async_copy(
            weight_ref.at[
                (which // HALF_MAPS) * N_MP + block, pl.ds((which % HALF_MAPS) * D, D), :
            ],
            weights.at[which, :, pl.ds(block * COLS, COLS)],
            sems.at[i],
        )

    up_fetch = pltpu.make_async_copy(
        weight_ref.at[:, pl.ds(HALF_MAPS * D, UP_HALF), :], up, up_sem
    )
    up_fetch.start()
    for i in range(MAPS * N_MP):
        fetch(i).start()

    a, b, c, d = (ref[...].astype(F32) for ref in updates)
    update = ((a + b) + (c + d)).astype(BF16)
    for k, state_ref in enumerate(states):
        place = pl.multiple_of(lax.rem(me + N_MP - k, N_MP) * COLS, 128)
        hidden[:, pl.ds(place, COLS)] = state_ref[...].astype(F32)
    up_fetch.wait()
    for block in range(N_MP):
        added = product(update[:, :UP_HALF], up[block])
        added = added + product(update[:, UP_HALF:], up[N_MP + block])
        at = slice(block * COLS, (block + 1) * COLS)
        fresh = hidden[:, at] + added
        hidden[:, at] = fresh
        given[:, at] = fresh.astype(BF16)

    def arrived(which, side):
        for j in range(2):
            i = which * N_MP + side * 2 + j
            pltpu.make_async_copy(
                weight_ref.at[0, pl.ds(0, D), :],
                weights.at[which, :, pl.ds((side * 2 + j) * COLS, COLS)],
                sems.at[i],
            ).wait()
        return weights[which, :, pl.ds(pl.multiple_of(side * WIDE, 128), WIDE)]

    def layer(index, carry):
        def one(side, carry):
            at = pl.ds(pl.multiple_of(side * WIDE, 128), WIDE)
            inner[:, at] = silu(product(given[...], arrived(2 * index, side))).astype(BF16)
            return carry

        lax.fori_loop(0, 2, one, 0)
        for side in range(2):
            at = slice(side * WIDE, (side + 1) * WIDE)
            outer = silu(product(inner[...], arrived(2 * index + 1, side)))
            fresh = (hidden[:, at] + outer) * inv_root_two
            hidden[:, at] = fresh
            given[:, at] = fresh.astype(BF16)
        return carry

    lax.fori_loop(0, MAPS // 2, layer, 0)
    for k, out_ref in enumerate(outs):
        place = pl.multiple_of(lax.rem(me + k, N_MP) * COLS, 128)
        out_ref[...] = given[:, pl.ds(place, COLS)]


def layers(mp, updates, states, gathered):
    vmem = pl.BlockSpec(memory_space=pltpu.VMEM)
    return pl.pallas_call(
        layers_kernel,
        in_specs=[SCALAR] + [vmem] * (2 * N_MP) + [pl.BlockSpec(memory_space=pl.ANY)],
        out_specs=[vmem] * N_MP,
        out_shape=[shape_of(ROWS, COLS)] * N_MP,
        scratch_shapes=[
            pltpu.VMEM((ROWS, D), F32),
            pltpu.VMEM((ROWS, D), BF16),
            pltpu.VMEM((ROWS, D), BF16),
            pltpu.VMEM((N_CORE * N_MP, UP_HALF, COLS), BF16),
            pltpu.VMEM((MAPS, D, D), BF16),
            pltpu.SemaphoreType.DMA,
            pltpu.SemaphoreType.DMA((MAPS * N_MP,)),
        ],
        compiler_params=pltpu.CompilerParams(vmem_limit_bytes=48 * 1024 * 1024),
        name="layers",
        cost_estimate=pl.CostEstimate(
            flops=2 * ROWS * D * D * MAPS,
            bytes_accessed=2 * D * D * MAPS,
            transcendentals=ROWS * D * MAPS,
        ),
    )(mp, *updates, *states, gathered)


def at_block(ref, me, k):
    place = lax.rem(me + N_MP - k, N_MP) * ROWS
    return ref[:, pl.ds(pl.multiple_of(place, ROWS), ROWS)]


def atoms_kernel(mp_ref, core_ref, atom_ref, h0, h1, h2, h3, keep_ref, give_ref):
    me, core = mp_ref[0], core_ref[0]
    row = jnp.concatenate([at_block(atom_ref, me, k) for k in range(N_MP)], axis=1)
    hidden = jnp.concatenate([h0[...], h1[...], h2[...], h3[...]], axis=0)
    group = row // ATOM_DEV
    spot = (group // N_CORE) * ATOM_DEV + row % ATOM_DEV
    for out_ref, owner in ((keep_ref, core), (give_ref, 1 - core)):
        mine = jnp.where(group % N_CORE == owner, spot, -1)

        def one(i, carry):
            first = pl.multiple_of(i * ATOM_BLOCK, ATOM_BLOCK)
            part = product(members(mine, ATOM_BLOCK, first), hidden)
            out_ref[pl.ds(first, ATOM_BLOCK), :] = part.astype(BF16)
            return carry

        lax.fori_loop(0, HALF_ATOMS // ATOM_BLOCK, one, 0)


def atoms(mp, core, edge_atom, hiddens):
    return pl.pallas_call(
        atoms_kernel,
        grid=(1,),
        in_specs=[SCALAR, SCALAR, whole((1, EDGE_DEV))] + [whole((ROWS, COLS))] * N_MP,
        out_specs=[whole((HALF_ATOMS, COLS))] * 2,
        out_shape=[shape_of(HALF_ATOMS, COLS)] * 2,
        compiler_params=params(24),
        name="atoms",
        cost_estimate=pl.CostEstimate(
            flops=2 * ATOMS * EDGE_DEV * COLS, bytes_accessed=2000000, transcendentals=0
        ),
    )(mp, core, edge_atom, *hiddens)


def meet_kernel(x_ref, keep_ref, got_ref, *outs):
    for k, out_ref in enumerate(outs):
        place = lax.rem(x_ref[0] + k, N_X) * (HALF_ATOMS // N_X)
        rows = pl.ds(pl.multiple_of(place, HALF_ATOMS // N_X), HALF_ATOMS // N_X)
        out_ref[...] = (keep_ref[rows, :].astype(F32) + got_ref[rows, :].astype(F32)).astype(BF16)


def meet(x, keep, got):
    return pl.pallas_call(
        meet_kernel,
        grid=(1,),
        in_specs=[SCALAR] + [whole((HALF_ATOMS, COLS))] * 2,
        out_specs=[whole((HALF_ATOMS // N_X, COLS))] * N_X,
        out_shape=[shape_of(HALF_ATOMS // N_X, COLS)] * N_X,
        compiler_params=params(24),
        name="meet",
        cost_estimate=pl.CostEstimate(
            flops=HALF_ATOMS * COLS, bytes_accessed=2400000, transcendentals=0
        ),
    )(x, keep, got)


def final_kernel(mp_ref, core_ref, atom_ref, h0, h1, h2, h3, mine_ref, other_ref, out_ref):
    me, core = mp_ref[0], core_ref[0]
    for k, hidden_ref in enumerate((h0, h1, h2, h3)):
        place = lax.rem(me + N_MP - k, N_MP) * ROWS
        out_ref[pl.ds(pl.multiple_of(place, ROWS), ROWS), :] = hidden_ref[...]

    def one(i, carry):
        rows = pl.ds(pl.multiple_of(i * ROWS, ROWS), ROWS)
        row = atom_ref[:, rows]
        group = row // ATOM_DEV
        spot = (group // N_CORE) * ATOM_DEV + row % ATOM_DEV
        near = jnp.where(group % N_CORE == core, spot, -1)
        far = jnp.where(group % N_CORE == core, -1, spot)
        taken = product(picks(near, HALF_ATOMS), mine_ref[...])
        taken = taken + product(picks(far, HALF_ATOMS), other_ref[...])
        out_ref[rows, :] = (out_ref[rows, :].astype(F32) + taken).astype(BF16)
        return carry

    lax.fori_loop(0, N_MP, one, 0)


def final(mp, core, edge_atom, hiddens, mine, other):
    return pl.pallas_call(
        final_kernel,
        grid=(1,),
        in_specs=[SCALAR, SCALAR, whole((1, EDGE_DEV))]
        + [whole((ROWS, COLS))] * N_MP
        + [whole((HALF_ATOMS, COLS))] * 2,
        out_specs=whole((EDGE_DEV, COLS)),
        out_shape=shape_of(EDGE_DEV, COLS),
        compiler_params=params(24),
        name="final",
        cost_estimate=pl.CostEstimate(
            flops=2 * ATOMS * EDGE_DEV * COLS, bytes_accessed=2400000, transcendentals=0
        ),
    )(mp, core, edge_atom, *hiddens, mine, other)


def turn(array, axis, count, shift):
    return lax.ppermute(array, axis, [(i, (i + shift) % count) for i in range(count)])


def turned(blocks, axis):
    count = len(blocks)
    return [blocks[0]] + [turn(blocks[k], axis, count, k) for k in range(1, count)]


def summed(blocks):
    return jnp.sum(blocks.astype(F32), axis=0)


def local(
    edge_state,
    down_weight,
    basis,
    basis_weight,
    up_weight,
    dense_weight,
    send_rows,
    trip_in,
    trip_out,
    trip_live,
    edge_atom,
):
    mp = jnp.full((1,), lax.axis_index("mp"), I32)
    core_index = lax.axis_index("graph_2")
    core = jnp.full((1,), core_index, I32)
    lists = send_rows.reshape(1, SLOTS)
    atom_row = edge_atom.reshape(1, EDGE_DEV)
    high = basis_weight.astype(BF16)
    low = (basis_weight - high.astype(F32)).astype(BF16)
    pad = ((0, BASIS_PAD - NSBF), (0, 0))
    high, low = jnp.pad(high, pad), jnp.pad(low, pad)
    coef_weight = jnp.concatenate([high, high, low], axis=0)
    half = jnp.concatenate(
        [
            lax.dynamic_slice_in_dim(
                dense_weight.reshape(MAPS * D, COLS), core_index * (HALF_MAPS * D), HALF_MAPS * D, 0
            ),
            lax.dynamic_slice_in_dim(up_weight, core_index * UP_HALF, UP_HALF, 0),
        ],
        axis=0,
    )

    trip_in = trip_in.reshape(1, TRIPS)
    trip_live = trip_live.reshape(1, TRIPS)
    trip_out = trip_out.reshape(1, TRIPS)
    first, second, *state_blocks = project(mp, edge_state, down_weight)
    exchange = functools.partial(
        lax.all_to_all, axis_name=GRAPH, split_axis=0, concat_axis=0, tiled=True
    )

    def sums(received, part):
        low, high = part
        table = received.reshape(SLOTS, high - low)
        weight = coef_weight[:, low:high]
        total = triplets(trip_in, trip_live, trip_out, basis, weight, table)
        return total.reshape(N_GRAPH, CAP, high - low)

    first = send(lists, turned([first] * N_MP, "mp")).reshape(N_GRAPH, CAP, -1)
    first, second = lax.optimization_barrier((first, second))
    partials = turned([second] * N_MP, "mp")
    first = exchange(first)
    second = send(lists, partials).reshape(N_GRAPH, CAP, -1)
    first, second, half = lax.optimization_barrier((first, second, half))
    second = exchange(second)
    gathered = lax.all_gather(half, ("graph_2", "mp"), axis=0, tiled=False)
    states = turned(state_blocks, "mp")
    first = exchange(sums(first, PARTS[0]))
    second = exchange(sums(second, PARTS[1]))
    blocks = edges(mp, lists, first.reshape(SLOTS, -1), [])
    blocks = edges(mp, lists, second.reshape(SLOTS, -1), blocks)
    updates = turned(blocks, "mp")
    hiddens = turned(layers(mp, updates, states, gathered), "mp")
    keep, give = atoms(mp, core, atom_row, hiddens)
    x = jnp.full((1,), lax.axis_index("graph_0"), I32)
    parts = turned(meet(x, keep, turn(give, "graph_2", N_CORE, 1)), "graph_0")
    part = (parts[0].astype(F32) + parts[1].astype(F32)) + (
        parts[2].astype(F32) + parts[3].astype(F32)
    )
    part = part.astype(BF16).reshape(N_Z, ATOM_DEV, COLS)
    atom_sum = summed(lax.all_to_all(part, "graph_1", 0, 0, tiled=True))
    atom_out = jax.nn.silu(atom_scale * atom_sum).astype(BF16)
    table = lax.all_to_all(
        jnp.broadcast_to(atom_out[None], (N_Z, ATOM_DEV, COLS)), "graph_1", 0, 0, tiled=True
    ).reshape(N_Z * ATOM_DEV, COLS)
    table = lax.all_to_all(
        jnp.broadcast_to(table[None], (N_X, N_Z * ATOM_DEV, COLS)), "graph_0", 0, 0, tiled=True
    ).reshape(HALF_ATOMS, COLS)
    other = turn(table, "graph_2", N_CORE, 1)
    edge_out = final(mp, core, atom_row, hiddens, table, other)
    return (edge_out, atom_out)


def solution(mesh):
    split = Mesh(
        mesh.devices.reshape(N_X, N_Z, N_CORE, mesh.shape["mp"]),
        ("graph_0", "graph_1", "graph_2", "mp"),
    )
    return jax.shard_map(
        local,
        mesh=split,
        in_specs=(
            P(GRAPH, "mp"),
            P("mp", None),
            P(None, GRAPH_MP),
            P(),
            P(None, "mp"),
            P(None, None, None, "mp"),
            P(GRAPH, "mp", None),
            P(GRAPH_MP),
            P(GRAPH_MP),
            P(GRAPH_MP),
            P(GRAPH),
        ),
        out_specs=(P(GRAPH, "mp"), P(GRAPH, "mp")),
        check_vma=False,
    )
```

```python
import functools

import jax
import jax.numpy as jnp
from jax import lax
from jax.experimental import pallas as pl
from jax.experimental.pallas import tpu as pltpu
from jax.sharding import Mesh
from jax.sharding import PartitionSpec as P

ATOM_DEV = 32
GRAPH = ("graph_0", "graph_1", "graph_2")
GRAPH_MP = ("graph_0", "graph_1", "graph_2", "mp")
N_X, N_Z, N_CORE, N_MP = 4, 8, 2, 4
N_GRAPH = N_X * N_Z * N_CORE
CAP = 64
EDGE_DEV = 512
ROWS = EDGE_DEV // N_MP
SLOTS = N_GRAPH * CAP
TRIPS = 4096
NSBF = 42
BASIS_PAD = 48
D = 1536
COLS = D // N_MP
TRIP = 384
MAPS = 6
HALF_MAPS = MAPS // N_CORE
UP_HALF = TRIP // N_CORE
ATOMS = ATOM_DEV * N_GRAPH
HALF_ATOMS = ATOMS // N_CORE
BLOCK = 512
ATOM_BLOCK = 256
PARTS = ((0, 128), (128, 384))

F32 = jnp.float32
BF16 = jnp.bfloat16
I32 = jnp.int32

inv_root_two = 0.7071067811865476
atom_scale = 0.2


def silu(v):
    return v / (1.0 + jnp.exp(-v))


def product(a, b):
    return jnp.dot(a, b, preferred_element_type=F32)


def ones_where(mask):
    return jnp.where(mask, jnp.ones((), F32), jnp.zeros((), F32)).astype(BF16)


def column_of(row):
    return jnp.broadcast_to(row, (128, row.shape[1])).T


def picks_of(column, count):
    lane = lax.broadcasted_iota(I32, column.shape, 1)
    return jnp.concatenate(
        [ones_where(column == lane + k) for k in range(0, count, 128)], axis=1
    )


def picks(row, count):
    return picks_of(column_of(row), count)


def members(row, count, first):
    place = lax.broadcasted_iota(I32, (count, 128), 0) + first
    return jnp.concatenate(
        [ones_where(place == row[:, k : k + 128]) for k in range(0, row.shape[1], 128)], axis=1
    )


def params(mib):
    return pltpu.CompilerParams(
        dimension_semantics=("arbitrary",), vmem_limit_bytes=mib * 1024 * 1024
    )


def whole(shape):
    return pl.BlockSpec(shape, lambda *_: (0,) * len(shape))


def shape_of(*shape, kind=BF16):
    return jax.ShapeDtypeStruct(shape, kind)


SCALAR = pl.BlockSpec(memory_space=pltpu.SMEM)


def project_kernel(mp_ref, state_ref, weight_ref, *refs):
    partial = product(state_ref[...], weight_ref[...]).astype(BF16)
    for partial_ref, (low, high) in zip(refs, PARTS):
        partial_ref[...] = partial[:, low:high]
    for k, turned_ref in enumerate(refs[len(PARTS) :]):
        place = lax.rem(mp_ref[0] + k, N_MP) * ROWS
        turned_ref[...] = state_ref[pl.ds(pl.multiple_of(place, ROWS), ROWS), :]


def project(mp, edge_state, down_weight):
    widths = [high - low for low, high in PARTS]
    return pl.pallas_call(
        project_kernel,
        grid=(1,),
        in_specs=[SCALAR, whole((EDGE_DEV, COLS)), whole((COLS, TRIP))],
        out_specs=[whole((EDGE_DEV, w)) for w in widths] + [whole((ROWS, COLS))] * N_MP,
        out_shape=[shape_of(EDGE_DEV, w) for w in widths] + [shape_of(ROWS, COLS)] * N_MP,
        compiler_params=params(62),
        name="project",
        cost_estimate=pl.CostEstimate(
            flops=2 * EDGE_DEV * COLS * TRIP, bytes_accessed=1500000, transcendentals=0
        ),
    )(mp, edge_state, down_weight)


def send_kernel(list_ref, a_ref, b_ref, c_ref, d_ref, out_ref, table):
    @pl.when(pl.program_id(0) == 0)
    def _():
        total = a_ref[...].astype(F32) + b_ref[...].astype(F32)
        total = total + (c_ref[...].astype(F32) + d_ref[...].astype(F32))
        table[...] = total.astype(BF16)

    out_ref[...] = product(picks(list_ref[...], EDGE_DEV), table[...]).astype(BF16)


SEND_BLOCK = 1024


def send(lists, partials):
    width = partials[0].shape[1]
    return pl.pallas_call(
        send_kernel,
        grid=(SLOTS // SEND_BLOCK,),
        in_specs=[pl.BlockSpec((1, SEND_BLOCK), lambda i: (0, i))] + [whole((EDGE_DEV, width))] * N_MP,
        out_specs=pl.BlockSpec((SEND_BLOCK, width), lambda i: (i, 0)),
        out_shape=shape_of(SLOTS, width),
        scratch_shapes=[pltpu.VMEM((EDGE_DEV, width), BF16)],
        compiler_params=params(24),
        name="send",
        cost_estimate=pl.CostEstimate(
            flops=2 * SLOTS * EDGE_DEV * width, bytes_accessed=12000 * width, transcendentals=0
        ),
    )(lists, *partials)


TRIP_BLOCK = 512
TRIP_STEPS = TRIPS // TRIP_BLOCK
SLOT_BLOCK = 512
SUM_CHUNK = 1024


def triplet_kernel(
    groups, in_ref, live_ref, to_ref, basis_ref, weight_ref, table_ref, out_ref, table, values, padded
):
    step = pl.program_id(0)
    width = table_ref.shape[1]
    deep = SLOTS // groups

    @pl.when(step == 0)
    def _():
        padded[...] = jnp.zeros_like(padded)
        for h in range(groups):
            table[:, h * width : (h + 1) * width] = table_ref[h * deep : (h + 1) * deep, :]

    @pl.when(step < TRIP_STEPS)
    def _():
        padded[0:NSBF, :] = basis_ref[...] * live_ref[...].astype(F32)
        basis = padded[...]
        high = basis.astype(BF16)
        low = (basis - high.astype(F32)).astype(BF16)
        stacked = jnp.concatenate([high, low, high], axis=0)
        coef = lax.dot_general(
            stacked, weight_ref[...], (((0,), (0,)), ((), ())), preferred_element_type=F32
        )
        place = pl.multiple_of(step * TRIP_BLOCK, TRIP_BLOCK)
        source = column_of(in_ref[...])
        target = column_of(to_ref[:, pl.ds(place, TRIP_BLOCK)])
        spot = source & (deep - 1)

        def more(i, total):
            first = pl.multiple_of(i * SUM_CHUNK, SUM_CHUNK)
            return total + product(
                picks_of(spot - first, SUM_CHUNK), table[pl.ds(first, SUM_CHUNK), :]
            )

        candidates = product(picks_of(spot, SUM_CHUNK), table[:SUM_CHUNK, :])
        if deep > SUM_CHUNK:
            candidates = lax.fori_loop(1, deep // SUM_CHUNK, more, candidates)
        for k in range(0, width, 128):
            value = candidates[:, k : k + 128]
            for h in range(1, groups):
                at = h * width + k
                value = jnp.where(source >= h * deep, candidates[:, at : at + 128], value)
            value = value * coef[:, k : k + 128]
            for h in range(groups):
                at = h * width + k
                here = (target >= h * deep) & (target < (h + 1) * deep)
                values[pl.ds(place, TRIP_BLOCK), at : at + 128] = jnp.where(here, value, 0.0).astype(
                    BF16
                )

    @pl.when(step >= TRIP_STEPS)
    def _():
        first = (step - TRIP_STEPS) * SLOT_BLOCK

        def more(i, total):
            rows = pl.ds(pl.multiple_of(i * SUM_CHUNK, SUM_CHUNK), SUM_CHUNK)
            chosen = members(to_ref[:, rows] & (deep - 1), SLOT_BLOCK, first)
            return total + product(chosen, values[rows, :])

        empty = jnp.zeros((SLOT_BLOCK, groups * width), F32)
        total = lax.fori_loop(0, TRIPS // SUM_CHUNK, more, empty).astype(BF16)
        for h in range(groups):
            out_ref[h] = total[:, h * width : (h + 1) * width]


def triplets(trip_in, trip_live, trip_out, basis, weight, table):
    width = table.shape[1]
    groups = 512 // width
    deep = SLOTS // groups
    gather_step = lambda i: (0, jnp.minimum(i, TRIP_STEPS - 1))
    return pl.pallas_call(
        functools.partial(triplet_kernel, groups),
        grid=(TRIP_STEPS + deep // SLOT_BLOCK,),
        in_specs=[
            pl.BlockSpec((1, TRIP_BLOCK), gather_step),
            pl.BlockSpec((1, TRIP_BLOCK), gather_step),
            whole((1, TRIPS)),
            pl.BlockSpec((NSBF, TRIP_BLOCK), gather_step),
            whole((3 * BASIS_PAD, width)),
            whole((SLOTS, width)),
        ],
        out_specs=pl.BlockSpec(
            (groups, SLOT_BLOCK, width), lambda i: (0, jnp.maximum(i - TRIP_STEPS, 0), 0)
        ),
        out_shape=shape_of(groups, deep, width),
        scratch_shapes=[
            pltpu.VMEM((deep, groups * width), BF16),
            pltpu.VMEM((TRIPS, groups * width), BF16),
            pltpu.VMEM((BASIS_PAD, TRIP_BLOCK), F32),
        ],
        compiler_params=params(48),
        name="triplets",
        cost_estimate=pl.CostEstimate(
            flops=4 * TRIPS * SLOTS * width, bytes_accessed=18000 * width, transcendentals=0
        ),
    )(trip_in, trip_live, trip_out, basis, weight, table)


EDGE_CHUNK = 1024


def edges_kernel(mp_ref, list_ref, table_ref, *refs):
    earlier, outs, total = refs[: -N_MP - 1], refs[-N_MP - 1 : -1], refs[-1]
    step = pl.program_id(0)
    part = product(members(list_ref[...], EDGE_DEV, 0), table_ref[...])

    @pl.when(step == 0)
    def _():
        total[...] = part

    @pl.when(step > 0)
    def _():
        total[...] += part

    @pl.when(step == SLOTS // EDGE_CHUNK - 1)
    def _():
        for k, out_ref in enumerate(outs):
            place = lax.rem(mp_ref[0] + k, N_MP) * ROWS
            low = 0
            if earlier:
                low = earlier[k].shape[1]
                out_ref[:, :low] = earlier[k][...]
            out_ref[:, low:] = total[pl.ds(pl.multiple_of(place, ROWS), ROWS), :].astype(BF16)


def edges(mp, lists, returned, earlier):
    width = returned.shape[1]
    before = [block.shape[1] for block in earlier]
    full = width + (before[0] if before else 0)
    return pl.pallas_call(
        edges_kernel,
        grid=(SLOTS // EDGE_CHUNK,),
        in_specs=[
            SCALAR,
            pl.BlockSpec((1, EDGE_CHUNK), lambda i: (0, i)),
            pl.BlockSpec((EDGE_CHUNK, width), lambda i: (i, 0)),
        ]
        + [whole((ROWS, w)) for w in before],
        out_specs=[whole((ROWS, full))] * N_MP,
        out_shape=[shape_of(ROWS, full)] * N_MP,
        scratch_shapes=[pltpu.VMEM((EDGE_DEV, width), F32)],
        compiler_params=params(24),
        name="edges",
        cost_estimate=pl.CostEstimate(
            flops=2 * SLOTS * EDGE_DEV * width, bytes_accessed=9000 * width, transcendentals=0
        ),
    )(mp, lists, returned, *earlier)


WIDE = 2 * COLS
AHEAD = 6


def layers_kernel(mp_ref, *refs):
    updates, states, weight_ref = refs[:N_MP], refs[N_MP : 2 * N_MP], refs[2 * N_MP]
    refs = refs[2 * N_MP + 1 :]
    outs, (hidden, given, inner, up, weights, up_sem, sems) = refs[:N_MP], refs[N_MP:]
    me = mp_ref[0]

    def fetch(i):
        which, block = lax.div(i, N_MP), lax.rem(i, N_MP)
        rows = pl.multiple_of(lax.rem(which, HALF_MAPS) * D, D)
        return pltpu.make_async_copy(
            weight_ref.at[lax.div(which, HALF_MAPS) * N_MP + block, pl.ds(rows, D), :],
            weights.at[which, :, pl.ds(pl.multiple_of(block * COLS, 128), COLS)],
            sems.at[i],
        )

    up_fetch = pltpu.make_async_copy(
        weight_ref.at[:, pl.ds(HALF_MAPS * D, UP_HALF), :], up, up_sem
    )
    up_fetch.start()
    for i in range(AHEAD):
        fetch(i).start()

    a, b, c, d = (ref[...].astype(F32) for ref in updates)
    update = ((a + b) + (c + d)).astype(BF16)
    for k, state_ref in enumerate(states):
        place = pl.multiple_of(lax.rem(me + N_MP - k, N_MP) * COLS, 128)
        hidden[:, pl.ds(place, COLS)] = state_ref[...].astype(F32)
    up_fetch.wait()
    for block in range(N_MP):
        added = product(update[:, :UP_HALF], up[block])
        added = added + product(update[:, UP_HALF:], up[N_MP + block])
        at = slice(block * COLS, (block + 1) * COLS)
        fresh = hidden[:, at] + added
        hidden[:, at] = fresh
        given[:, at] = fresh.astype(BF16)

    def arrived(which, side):
        for j in range(2):
            i = which * N_MP + side * 2 + j
            fetch(i).wait()

            @pl.when(i + AHEAD < MAPS * N_MP)
            def _():
                fetch(i + AHEAD).start()

        return weights[which, :, pl.ds(pl.multiple_of(side * WIDE, 128), WIDE)]

    def layer(index, carry):
        def one(side, carry):
            at = pl.ds(pl.multiple_of(side * WIDE, 128), WIDE)
            inner[:, at] = silu(product(given[...], arrived(2 * index, side))).astype(BF16)
            return carry

        lax.fori_loop(0, 2, one, 0)
        for side in range(2):
            at = slice(side * WIDE, (side + 1) * WIDE)
            outer = silu(product(inner[...], arrived(2 * index + 1, side)))
            fresh = (hidden[:, at] + outer) * inv_root_two
            hidden[:, at] = fresh
            given[:, at] = fresh.astype(BF16)
        return carry

    lax.fori_loop(0, MAPS // 2, layer, 0)
    for k, out_ref in enumerate(outs):
        place = pl.multiple_of(lax.rem(me + k, N_MP) * COLS, 128)
        out_ref[...] = given[:, pl.ds(place, COLS)]


def layers(mp, updates, states, gathered):
    vmem = pl.BlockSpec(memory_space=pltpu.VMEM)
    return pl.pallas_call(
        layers_kernel,
        in_specs=[SCALAR] + [vmem] * (2 * N_MP) + [pl.BlockSpec(memory_space=pl.ANY)],
        out_specs=[vmem] * N_MP,
        out_shape=[shape_of(ROWS, COLS)] * N_MP,
        scratch_shapes=[
            pltpu.VMEM((ROWS, D), F32),
            pltpu.VMEM((ROWS, D), BF16),
            pltpu.VMEM((ROWS, D), BF16),
            pltpu.VMEM((N_CORE * N_MP, UP_HALF, COLS), BF16),
            pltpu.VMEM((MAPS, D, D), BF16),
            pltpu.SemaphoreType.DMA,
            pltpu.SemaphoreType.DMA((MAPS * N_MP,)),
        ],
        compiler_params=pltpu.CompilerParams(vmem_limit_bytes=48 * 1024 * 1024),
        name="layers",
        cost_estimate=pl.CostEstimate(
            flops=2 * ROWS * D * D * MAPS,
            bytes_accessed=2 * D * D * MAPS,
            transcendentals=ROWS * D * MAPS,
        ),
    )(mp, *updates, *states, gathered)


def at_block(ref, me, k):
    place = lax.rem(me + N_MP - k, N_MP) * ROWS
    return ref[:, pl.ds(pl.multiple_of(place, ROWS), ROWS)]


def atoms_kernel(mp_ref, core_ref, atom_ref, h0, h1, h2, h3, keep_ref, give_ref):
    me, core = mp_ref[0], core_ref[0]
    row = jnp.concatenate([at_block(atom_ref, me, k) for k in range(N_MP)], axis=1)
    hidden = jnp.concatenate([h0[...], h1[...], h2[...], h3[...]], axis=0)
    group = row // ATOM_DEV
    spot = (group // N_CORE) * ATOM_DEV + row % ATOM_DEV
    for out_ref, owner in ((keep_ref, core), (give_ref, 1 - core)):
        mine = jnp.where(group % N_CORE == owner, spot, -1)

        def one(i, carry):
            first = pl.multiple_of(i * ATOM_BLOCK, ATOM_BLOCK)
            part = product(members(mine, ATOM_BLOCK, first), hidden)
            out_ref[pl.ds(first, ATOM_BLOCK), :] = part.astype(BF16)
            return carry

        lax.fori_loop(0, HALF_ATOMS // ATOM_BLOCK, one, 0)


def atoms(mp, core, edge_atom, hiddens):
    return pl.pallas_call(
        atoms_kernel,
        grid=(1,),
        in_specs=[SCALAR, SCALAR, whole((1, EDGE_DEV))] + [whole((ROWS, COLS))] * N_MP,
        out_specs=[whole((HALF_ATOMS, COLS))] * 2,
        out_shape=[shape_of(HALF_ATOMS, COLS)] * 2,
        compiler_params=params(24),
        name="atoms",
        cost_estimate=pl.CostEstimate(
            flops=2 * ATOMS * EDGE_DEV * COLS, bytes_accessed=2000000, transcendentals=0
        ),
    )(mp, core, edge_atom, *hiddens)


def meet_kernel(x_ref, keep_ref, got_ref, *outs):
    for k, out_ref in enumerate(outs):
        place = lax.rem(x_ref[0] + k, N_X) * (HALF_ATOMS // N_X)
        rows = pl.ds(pl.multiple_of(place, HALF_ATOMS // N_X), HALF_ATOMS // N_X)
        out_ref[...] = (keep_ref[rows, :].astype(F32) + got_ref[rows, :].astype(F32)).astype(BF16)


def meet(x, keep, got):
    return pl.pallas_call(
        meet_kernel,
        grid=(1,),
        in_specs=[SCALAR] + [whole((HALF_ATOMS, COLS))] * 2,
        out_specs=[whole((HALF_ATOMS // N_X, COLS))] * N_X,
        out_shape=[shape_of(HALF_ATOMS // N_X, COLS)] * N_X,
        compiler_params=params(24),
        name="meet",
        cost_estimate=pl.CostEstimate(
            flops=HALF_ATOMS * COLS, bytes_accessed=2400000, transcendentals=0
        ),
    )(x, keep, got)


def final_kernel(mp_ref, core_ref, atom_ref, h0, h1, h2, h3, mine_ref, other_ref, out_ref):
    me, core = mp_ref[0], core_ref[0]
    for k, hidden_ref in enumerate((h0, h1, h2, h3)):
        place = lax.rem(me + N_MP - k, N_MP) * ROWS
        out_ref[pl.ds(pl.multiple_of(place, ROWS), ROWS), :] = hidden_ref[...]

    def one(i, carry):
        rows = pl.ds(pl.multiple_of(i * ROWS, ROWS), ROWS)
        row = atom_ref[:, rows]
        group = row // ATOM_DEV
        spot = (group // N_CORE) * ATOM_DEV + row % ATOM_DEV
        near = jnp.where(group % N_CORE == core, spot, -1)
        far = jnp.where(group % N_CORE == core, -1, spot)
        taken = product(picks(near, HALF_ATOMS), mine_ref[...])
        taken = taken + product(picks(far, HALF_ATOMS), other_ref[...])
        out_ref[rows, :] = (out_ref[rows, :].astype(F32) + taken).astype(BF16)
        return carry

    lax.fori_loop(0, N_MP, one, 0, unroll=2)


def final(mp, core, edge_atom, hiddens, mine, other):
    return pl.pallas_call(
        final_kernel,
        grid=(1,),
        in_specs=[SCALAR, SCALAR, whole((1, EDGE_DEV))]
        + [whole((ROWS, COLS))] * N_MP
        + [whole((HALF_ATOMS, COLS))] * 2,
        out_specs=whole((EDGE_DEV, COLS)),
        out_shape=shape_of(EDGE_DEV, COLS),
        compiler_params=params(24),
        name="final",
        cost_estimate=pl.CostEstimate(
            flops=2 * ATOMS * EDGE_DEV * COLS, bytes_accessed=2400000, transcendentals=0
        ),
    )(mp, core, edge_atom, *hiddens, mine, other)


def turn(array, axis, count, shift):
    return lax.ppermute(array, axis, [(i, (i + shift) % count) for i in range(count)])


def turned(blocks, axis):
    count = len(blocks)
    return [blocks[0]] + [turn(blocks[k], axis, count, k) for k in range(1, count)]


def summed(blocks):
    return jnp.sum(blocks.astype(F32), axis=0)


def local(
    edge_state,
    down_weight,
    basis,
    basis_weight,
    up_weight,
    dense_weight,
    send_rows,
    trip_in,
    trip_out,
    trip_live,
    edge_atom,
):
    mp = jnp.full((1,), lax.axis_index("mp"), I32)
    core_index = lax.axis_index("graph_2")
    core = jnp.full((1,), core_index, I32)
    lists = send_rows.reshape(1, SLOTS)
    atom_row = edge_atom.reshape(1, EDGE_DEV)
    high = basis_weight.astype(BF16)
    low = (basis_weight - high.astype(F32)).astype(BF16)
    pad = ((0, BASIS_PAD - NSBF), (0, 0))
    high, low = jnp.pad(high, pad), jnp.pad(low, pad)
    coef_weight = jnp.concatenate([high, high, low], axis=0)
    half = jnp.concatenate(
        [
            lax.dynamic_slice_in_dim(
                dense_weight.reshape(MAPS * D, COLS), core_index * (HALF_MAPS * D), HALF_MAPS * D, 0
            ),
            lax.dynamic_slice_in_dim(up_weight, core_index * UP_HALF, UP_HALF, 0),
        ],
        axis=0,
    )

    trip_in = trip_in.reshape(1, TRIPS)
    trip_live = trip_live.reshape(1, TRIPS)
    trip_out = trip_out.reshape(1, TRIPS)
    first, second, *state_blocks = project(mp, edge_state, down_weight)
    exchange = functools.partial(
        lax.all_to_all, axis_name=GRAPH, split_axis=0, concat_axis=0, tiled=True
    )

    def sums(received, part):
        low, high = part
        table = received.reshape(SLOTS, high - low)
        weight = coef_weight[:, low:high]
        total = triplets(trip_in, trip_live, trip_out, basis, weight, table)
        return total.reshape(N_GRAPH, CAP, high - low)

    first = send(lists, turned([first] * N_MP, "mp")).reshape(N_GRAPH, CAP, -1)
    first, second = lax.optimization_barrier((first, second))
    partials = turned([second] * N_MP, "mp")
    first = exchange(first)
    second = send(lists, partials).reshape(N_GRAPH, CAP, -1)
    first, second, half = lax.optimization_barrier((first, second, half))
    second = exchange(second)
    gathered = lax.all_gather(half, ("graph_2", "mp"), axis=0, tiled=False)
    states = turned(state_blocks, "mp")
    first = exchange(sums(first, PARTS[0]))
    second = exchange(sums(second, PARTS[1]))
    blocks = edges(mp, lists, first.reshape(SLOTS, -1), [])
    blocks = edges(mp, lists, second.reshape(SLOTS, -1), blocks)
    updates = turned(blocks, "mp")
    hiddens = turned(layers(mp, updates, states, gathered), "mp")
    keep, give = atoms(mp, core, atom_row, hiddens)
    x = jnp.full((1,), lax.axis_index("graph_0"), I32)
    parts = turned(meet(x, keep, turn(give, "graph_2", N_CORE, 1)), "graph_0")
    part = (parts[0].astype(F32) + parts[1].astype(F32)) + (
        parts[2].astype(F32) + parts[3].astype(F32)
    )
    part = part.astype(BF16).reshape(N_Z, ATOM_DEV, COLS)
    atom_sum = summed(lax.all_to_all(part, "graph_1", 0, 0, tiled=True))
    atom_out = jax.nn.silu(atom_scale * atom_sum).astype(BF16)
    table = lax.all_to_all(
        jnp.broadcast_to(atom_out[None], (N_Z, ATOM_DEV, COLS)), "graph_1", 0, 0, tiled=True
    ).reshape(N_Z * ATOM_DEV, COLS)
    table = lax.all_to_all(
        jnp.broadcast_to(table[None], (N_X, N_Z * ATOM_DEV, COLS)), "graph_0", 0, 0, tiled=True
    ).reshape(HALF_ATOMS, COLS)
    other = turn(table, "graph_2", N_CORE, 1)
    edge_out = final(mp, core, atom_row, hiddens, table, other)
    return (edge_out, atom_out)


def solution(mesh):
    split = Mesh(
        mesh.devices.reshape(N_X, N_Z, N_CORE, mesh.shape["mp"]),
        ("graph_0", "graph_1", "graph_2", "mp"),
    )
    return jax.shard_map(
        local,
        mesh=split,
        in_specs=(
            P(GRAPH, "mp"),
            P("mp", None),
            P(None, GRAPH_MP),
            P(),
            P(None, "mp"),
            P(None, None, None, "mp"),
            P(GRAPH, "mp", None),
            P(GRAPH_MP),
            P(GRAPH_MP),
            P(GRAPH_MP),
            P(GRAPH),
        ),
        out_specs=(P(GRAPH, "mp"), P(GRAPH, "mp")),
        check_vma=False,
    )
```

```python
import functools

import jax
import jax.numpy as jnp
from jax import lax
from jax.experimental import pallas as pl
from jax.experimental.pallas import tpu as pltpu
from jax.sharding import Mesh
from jax.sharding import PartitionSpec as P

ATOM_DEV = 32
GRAPH = ("graph_0", "graph_1", "graph_2")
GRAPH_MP = ("graph_0", "graph_1", "graph_2", "mp")
N_X, N_Z, N_CORE, N_MP = 4, 8, 2, 4
N_GRAPH = N_X * N_Z * N_CORE
CAP = 64
EDGE_DEV = 512
ROWS = EDGE_DEV // N_MP
SLOTS = N_GRAPH * CAP
TRIPS = 4096
NSBF = 42
BASIS_PAD = 48
D = 1536
COLS = D // N_MP
TRIP = 384
MAPS = 6
HALF_MAPS = MAPS // N_CORE
UP_HALF = TRIP // N_CORE
ATOMS = ATOM_DEV * N_GRAPH
HALF_ATOMS = ATOMS // N_CORE
BLOCK = 512
ATOM_BLOCK = 512
PARTS = ((0, 128), (128, 384))

F32 = jnp.float32
BF16 = jnp.bfloat16
I32 = jnp.int32

inv_root_two = 0.7071067811865476
atom_scale = 0.2


def silu(v):
    return v / (1.0 + jnp.exp(-v))


def product(a, b):
    return jnp.dot(a, b, preferred_element_type=F32)


def ones_where(mask):
    return jnp.where(mask, jnp.ones((), F32), jnp.zeros((), F32)).astype(BF16)


def column_of(row):
    return jnp.broadcast_to(row, (128, row.shape[1])).T


def picks_of(column, count):
    lane = lax.broadcasted_iota(I32, column.shape, 1)
    low = ones_where((column & 127) == lane)
    high = (column >> 7).astype(F32).astype(BF16)
    none = jnp.zeros_like(low)
    return jnp.concatenate(
        [jnp.where(high == k, low, none) for k in range(count // 128)], axis=1
    )


def picks(row, count):
    return picks_of(column_of(row), count)


def members(row, count, first):
    shape = (128, row.shape[1])
    local = jnp.broadcast_to(row - first, shape)
    low = ones_where((local & 127) == lax.broadcasted_iota(I32, shape, 0))
    high = local >> 7
    return jnp.concatenate(
        [low * ones_where(high == k) for k in range(count // 128)], axis=0
    )


def params(mib):
    return pltpu.CompilerParams(
        dimension_semantics=("arbitrary",), vmem_limit_bytes=mib * 1024 * 1024
    )


def whole(shape):
    return pl.BlockSpec(shape, lambda *_: (0,) * len(shape))


def shape_of(*shape, kind=BF16):
    return jax.ShapeDtypeStruct(shape, kind)


SCALAR = pl.BlockSpec(memory_space=pltpu.SMEM)


def project_kernel(mp_ref, state_ref, weight_ref, *refs):
    partial = product(state_ref[...], weight_ref[...]).astype(BF16)
    for partial_ref, (low, high) in zip(refs, PARTS):
        partial_ref[...] = partial[:, low:high]
    for k, turned_ref in enumerate(refs[len(PARTS) :]):
        place = lax.rem(mp_ref[0] + k, N_MP) * ROWS
        turned_ref[...] = state_ref[pl.ds(pl.multiple_of(place, ROWS), ROWS), :]


def project(mp, edge_state, down_weight):
    widths = [high - low for low, high in PARTS]
    return pl.pallas_call(
        project_kernel,
        grid=(1,),
        in_specs=[SCALAR, whole((EDGE_DEV, COLS)), whole((COLS, TRIP))],
        out_specs=[whole((EDGE_DEV, w)) for w in widths] + [whole((ROWS, COLS))] * N_MP,
        out_shape=[shape_of(EDGE_DEV, w) for w in widths] + [shape_of(ROWS, COLS)] * N_MP,
        compiler_params=params(62),
        name="project",
        cost_estimate=pl.CostEstimate(
            flops=2 * EDGE_DEV * COLS * TRIP, bytes_accessed=1500000, transcendentals=0
        ),
    )(mp, edge_state, down_weight)


def send_kernel(list_ref, a_ref, b_ref, c_ref, d_ref, out_ref, table):
    @pl.when(pl.program_id(0) == 0)
    def _():
        total = a_ref[...].astype(F32) + b_ref[...].astype(F32)
        total = total + (c_ref[...].astype(F32) + d_ref[...].astype(F32))
        table[...] = total.astype(BF16)

    out_ref[...] = product(picks(list_ref[...], EDGE_DEV), table[...]).astype(BF16)


SEND_BLOCK = 1024


def send(lists, partials):
    width = partials[0].shape[1]
    return pl.pallas_call(
        send_kernel,
        grid=(SLOTS // SEND_BLOCK,),
        in_specs=[pl.BlockSpec((1, SEND_BLOCK), lambda i: (0, i))] + [whole((EDGE_DEV, width))] * N_MP,
        out_specs=pl.BlockSpec((SEND_BLOCK, width), lambda i: (i, 0)),
        out_shape=shape_of(SLOTS, width),
        scratch_shapes=[pltpu.VMEM((EDGE_DEV, width), BF16)],
        compiler_params=params(24),
        name="send",
        cost_estimate=pl.CostEstimate(
            flops=2 * SLOTS * EDGE_DEV * width, bytes_accessed=12000 * width, transcendentals=0
        ),
    )(lists, *partials)


TRIP_BLOCK = 512
TRIP_STEPS = TRIPS // TRIP_BLOCK
SLOT_BLOCK = 512
SUM_CHUNK = 1024


def triplet_kernel(
    groups, in_ref, live_ref, to_ref, basis_ref, weight_ref, table_ref, out_ref, table, values, padded
):
    step = pl.program_id(0)
    width = table_ref.shape[1]
    deep = SLOTS // groups

    @pl.when(step == 0)
    def _():
        padded[...] = jnp.zeros_like(padded)
        for h in range(groups):
            table[:, h * width : (h + 1) * width] = table_ref[h * deep : (h + 1) * deep, :]

    @pl.when(step < TRIP_STEPS)
    def _():
        padded[0:NSBF, :] = basis_ref[...] * live_ref[...].astype(F32)
        basis = padded[...]
        high = basis.astype(BF16)
        low = (basis - high.astype(F32)).astype(BF16)
        stacked = jnp.concatenate([high, low, high], axis=0)
        coef = lax.dot_general(
            stacked, weight_ref[...], (((0,), (0,)), ((), ())), preferred_element_type=F32
        )
        place = pl.multiple_of(step * TRIP_BLOCK, TRIP_BLOCK)
        source = column_of(in_ref[...])
        target = column_of(to_ref[:, pl.ds(place, TRIP_BLOCK)])
        spot = source & (deep - 1)

        def more(i, total):
            first = pl.multiple_of(i * SUM_CHUNK, SUM_CHUNK)
            return total + product(
                picks_of(spot - first, SUM_CHUNK), table[pl.ds(first, SUM_CHUNK), :]
            )

        candidates = product(picks_of(spot, SUM_CHUNK), table[:SUM_CHUNK, :])
        if deep > SUM_CHUNK:
            candidates = lax.fori_loop(1, deep // SUM_CHUNK, more, candidates)
        for k in range(0, width, 128):
            value = candidates[:, k : k + 128]
            for h in range(1, groups):
                at = h * width + k
                value = jnp.where(source >= h * deep, candidates[:, at : at + 128], value)
            value = value * coef[:, k : k + 128]
            for h in range(groups):
                at = h * width + k
                here = (target >= h * deep) & (target < (h + 1) * deep)
                values[pl.ds(place, TRIP_BLOCK), at : at + 128] = jnp.where(here, value, 0.0).astype(
                    BF16
                )

    @pl.when(step >= TRIP_STEPS)
    def _():
        first = (step - TRIP_STEPS) * SLOT_BLOCK

        def more(i, total):
            rows = pl.ds(pl.multiple_of(i * SUM_CHUNK, SUM_CHUNK), SUM_CHUNK)
            chosen = members(to_ref[:, rows] & (deep - 1), SLOT_BLOCK, first)
            return total + product(chosen, values[rows, :])

        empty = jnp.zeros((SLOT_BLOCK, groups * width), F32)
        total = lax.fori_loop(0, TRIPS // SUM_CHUNK, more, empty).astype(BF16)
        for h in range(groups):
            out_ref[h] = total[:, h * width : (h + 1) * width]


def triplets(trip_in, trip_live, trip_out, basis, weight, table):
    width = table.shape[1]
    groups = 512 // width
    deep = SLOTS // groups
    gather_step = lambda i: (0, jnp.minimum(i, TRIP_STEPS - 1))
    return pl.pallas_call(
        functools.partial(triplet_kernel, groups),
        grid=(TRIP_STEPS + deep // SLOT_BLOCK,),
        in_specs=[
            pl.BlockSpec((1, TRIP_BLOCK), gather_step),
            pl.BlockSpec((1, TRIP_BLOCK), gather_step),
            whole((1, TRIPS)),
            pl.BlockSpec((NSBF, TRIP_BLOCK), gather_step),
            whole((3 * BASIS_PAD, width)),
            whole((SLOTS, width)),
        ],
        out_specs=pl.BlockSpec(
            (groups, SLOT_BLOCK, width), lambda i: (0, jnp.maximum(i - TRIP_STEPS, 0), 0)
        ),
        out_shape=shape_of(groups, deep, width),
        scratch_shapes=[
            pltpu.VMEM((deep, groups * width), BF16),
            pltpu.VMEM((TRIPS, groups * width), BF16),
            pltpu.VMEM((BASIS_PAD, TRIP_BLOCK), F32),
        ],
        compiler_params=params(48),
        name="triplets",
        cost_estimate=pl.CostEstimate(
            flops=4 * TRIPS * SLOTS * width, bytes_accessed=18000 * width, transcendentals=0
        ),
    )(trip_in, trip_live, trip_out, basis, weight, table)


EDGE_CHUNK = 1024


def edges_kernel(mp_ref, list_ref, table_ref, *refs):
    earlier, outs, total = refs[: -N_MP - 1], refs[-N_MP - 1 : -1], refs[-1]
    step = pl.program_id(0)
    part = product(members(list_ref[...], EDGE_DEV, 0), table_ref[...])

    @pl.when(step == 0)
    def _():
        total[...] = part

    @pl.when(step > 0)
    def _():
        total[...] += part

    @pl.when(step == SLOTS // EDGE_CHUNK - 1)
    def _():
        for k, out_ref in enumerate(outs):
            place = lax.rem(mp_ref[0] + k, N_MP) * ROWS
            low = 0
            if earlier:
                low = earlier[k].shape[1]
                out_ref[:, :low] = earlier[k][...]
            out_ref[:, low:] = total[pl.ds(pl.multiple_of(place, ROWS), ROWS), :].astype(BF16)


def edges(mp, lists, returned, earlier):
    width = returned.shape[1]
    before = [block.shape[1] for block in earlier]
    full = width + (before[0] if before else 0)
    return pl.pallas_call(
        edges_kernel,
        grid=(SLOTS // EDGE_CHUNK,),
        in_specs=[
            SCALAR,
            pl.BlockSpec((1, EDGE_CHUNK), lambda i: (0, i)),
            pl.BlockSpec((EDGE_CHUNK, width), lambda i: (i, 0)),
        ]
        + [whole((ROWS, w)) for w in before],
        out_specs=[whole((ROWS, full))] * N_MP,
        out_shape=[shape_of(ROWS, full)] * N_MP,
        scratch_shapes=[pltpu.VMEM((EDGE_DEV, width), F32)],
        compiler_params=params(24),
        name="edges",
        cost_estimate=pl.CostEstimate(
            flops=2 * SLOTS * EDGE_DEV * width, bytes_accessed=9000 * width, transcendentals=0
        ),
    )(mp, lists, returned, *earlier)


WIDE = 2 * COLS
AHEAD = 6
AHEAD = 6


def layers_kernel(mp_ref, *refs):
    updates, states, weight_ref = refs[:N_MP], refs[N_MP : 2 * N_MP], refs[2 * N_MP]
    refs = refs[2 * N_MP + 1 :]
    outs, (hidden, given, inner, up, weights, up_sem, sems) = refs[:N_MP], refs[N_MP:]
    me = mp_ref[0]

    def fetch(i):
        which, block = lax.div(i, N_MP), lax.rem(i, N_MP)
        rows = pl.multiple_of(lax.rem(which, HALF_MAPS) * D, D)
        return pltpu.make_async_copy(
            weight_ref.at[lax.div(which, HALF_MAPS) * N_MP + block, pl.ds(rows, D), :],
            weights.at[which, :, pl.ds(pl.multiple_of(block * COLS, 128), COLS)],
            sems.at[i],
        )

    up_fetch = pltpu.make_async_copy(
        weight_ref.at[:, pl.ds(HALF_MAPS * D, UP_HALF), :], up, up_sem
    )
    up_fetch.start()
    for i in range(AHEAD):
        fetch(i).start()

    a, b, c, d = (ref[...].astype(F32) for ref in updates)
    update = ((a + b) + (c + d)).astype(BF16)
    for k, state_ref in enumerate(states):
        place = pl.multiple_of(lax.rem(me + N_MP - k, N_MP) * COLS, 128)
        hidden[:, pl.ds(place, COLS)] = state_ref[...].astype(F32)
    up_fetch.wait()
    for block in range(N_MP):
        added = product(update[:, :UP_HALF], up[block])
        added = added + product(update[:, UP_HALF:], up[N_MP + block])
        at = slice(block * COLS, (block + 1) * COLS)
        fresh = hidden[:, at] + added
        hidden[:, at] = fresh
        given[:, at] = fresh.astype(BF16)

    def arrived(which, side):
        for j in range(2):
            i = which * N_MP + side * 2 + j
            fetch(i).wait()

            @pl.when(i + AHEAD < MAPS * N_MP)
            def _():
                fetch(i + AHEAD).start()

        return weights[which, :, pl.ds(pl.multiple_of(side * WIDE, 128), WIDE)]

    def layer(index, carry):
        def one(side, carry):
            at = pl.ds(pl.multiple_of(side * WIDE, 128), WIDE)
            inner[:, at] = silu(product(given[...], arrived(2 * index, side))).astype(BF16)
            return carry

        lax.fori_loop(0, 2, one, 0)
        for side in range(2):
            at = slice(side * WIDE, (side + 1) * WIDE)
            outer = silu(product(inner[...], arrived(2 * index + 1, side)))
            fresh = (hidden[:, at] + outer) * inv_root_two
            hidden[:, at] = fresh
            given[:, at] = fresh.astype(BF16)
        return carry

    lax.fori_loop(0, MAPS // 2, layer, 0)
    for k, out_ref in enumerate(outs):
        place = pl.multiple_of(lax.rem(me + k, N_MP) * COLS, 128)
        out_ref[...] = given[:, pl.ds(place, COLS)]


def layers(mp, updates, states, gathered):
    vmem = pl.BlockSpec(memory_space=pltpu.VMEM)
    return pl.pallas_call(
        layers_kernel,
        in_specs=[SCALAR] + [vmem] * (2 * N_MP) + [pl.BlockSpec(memory_space=pl.ANY)],
        out_specs=[vmem] * N_MP,
        out_shape=[shape_of(ROWS, COLS)] * N_MP,
        scratch_shapes=[
            pltpu.VMEM((ROWS, D), F32),
            pltpu.VMEM((ROWS, D), BF16),
            pltpu.VMEM((ROWS, D), BF16),
            pltpu.VMEM((N_CORE * N_MP, UP_HALF, COLS), BF16),
            pltpu.VMEM((MAPS, D, D), BF16),
            pltpu.SemaphoreType.DMA,
            pltpu.SemaphoreType.DMA((MAPS * N_MP,)),
        ],
        compiler_params=pltpu.CompilerParams(vmem_limit_bytes=48 * 1024 * 1024),
        name="layers",
        cost_estimate=pl.CostEstimate(
            flops=2 * ROWS * D * D * MAPS,
            bytes_accessed=2 * D * D * MAPS,
            transcendentals=ROWS * D * MAPS,
        ),
    )(mp, *updates, *states, gathered)


def at_block(ref, me, k):
    place = lax.rem(me + N_MP - k, N_MP) * ROWS
    return ref[:, pl.ds(pl.multiple_of(place, ROWS), ROWS)]


def atoms_kernel(mp_ref, core_ref, atom_ref, h0, h1, h2, h3, keep_ref, give_ref):
    me, core = mp_ref[0], core_ref[0]
    row = jnp.concatenate([at_block(atom_ref, me, k) for k in range(N_MP)], axis=1)
    hidden = jnp.concatenate([h0[...], h1[...], h2[...], h3[...]], axis=0)
    group = row // ATOM_DEV
    spot = (group // N_CORE) * ATOM_DEV + row % ATOM_DEV
    for out_ref, owner in ((keep_ref, core), (give_ref, 1 - core)):
        mine = jnp.where(group % N_CORE == owner, spot, -1)

        def one(i, carry):
            first = pl.multiple_of(i * ATOM_BLOCK, ATOM_BLOCK)
            part = product(members(mine, ATOM_BLOCK, first), hidden)
            out_ref[pl.ds(first, ATOM_BLOCK), :] = part.astype(BF16)
            return carry

        lax.fori_loop(0, HALF_ATOMS // ATOM_BLOCK, one, 0, unroll=True)


def atoms(mp, core, edge_atom, hiddens):
    return pl.pallas_call(
        atoms_kernel,
        grid=(1,),
        in_specs=[SCALAR, SCALAR, whole((1, EDGE_DEV))] + [whole((ROWS, COLS))] * N_MP,
        out_specs=[whole((HALF_ATOMS, COLS))] * 2,
        out_shape=[shape_of(HALF_ATOMS, COLS)] * 2,
        compiler_params=params(24),
        name="atoms",
        cost_estimate=pl.CostEstimate(
            flops=2 * ATOMS * EDGE_DEV * COLS, bytes_accessed=2000000, transcendentals=0
        ),
    )(mp, core, edge_atom, *hiddens)


def meet_kernel(x_ref, keep_ref, got_ref, *outs):
    for k, out_ref in enumerate(outs):
        place = lax.rem(x_ref[0] + k, N_X) * (HALF_ATOMS // N_X)
        rows = pl.ds(pl.multiple_of(place, HALF_ATOMS // N_X), HALF_ATOMS // N_X)
        out_ref[...] = (keep_ref[rows, :].astype(F32) + got_ref[rows, :].astype(F32)).astype(BF16)


def meet(x, keep, got):
    return pl.pallas_call(
        meet_kernel,
        grid=(1,),
        in_specs=[SCALAR] + [whole((HALF_ATOMS, COLS))] * 2,
        out_specs=[whole((HALF_ATOMS // N_X, COLS))] * N_X,
        out_shape=[shape_of(HALF_ATOMS // N_X, COLS)] * N_X,
        compiler_params=params(24),
        name="meet",
        cost_estimate=pl.CostEstimate(
            flops=HALF_ATOMS * COLS, bytes_accessed=2400000, transcendentals=0
        ),
    )(x, keep, got)


def final_kernel(mp_ref, core_ref, atom_ref, h0, h1, h2, h3, mine_ref, other_ref, out_ref):
    me, core = mp_ref[0], core_ref[0]
    for k, hidden_ref in enumerate((h0, h1, h2, h3)):
        row = at_block(atom_ref, me, k)
        group = row // ATOM_DEV
        spot = (group // N_CORE) * ATOM_DEV + row % ATOM_DEV
        near = jnp.where(group % N_CORE == core, spot, -1)
        far = jnp.where(group % N_CORE == core, -1, spot)
        taken = product(picks(near, HALF_ATOMS), mine_ref[...])
        taken = taken + product(picks(far, HALF_ATOMS), other_ref[...])
        place = lax.rem(me + N_MP - k, N_MP) * ROWS
        out_ref[pl.ds(pl.multiple_of(place, ROWS), ROWS), :] = (
            hidden_ref[...].astype(F32) + taken
        ).astype(BF16)


def final(mp, core, edge_atom, hiddens, mine, other):
    return pl.pallas_call(
        final_kernel,
        grid=(1,),
        in_specs=[SCALAR, SCALAR, whole((1, EDGE_DEV))]
        + [whole((ROWS, COLS))] * N_MP
        + [whole((HALF_ATOMS, COLS))] * 2,
        out_specs=whole((EDGE_DEV, COLS)),
        out_shape=shape_of(EDGE_DEV, COLS),
        compiler_params=params(24),
        name="final",
        cost_estimate=pl.CostEstimate(
            flops=2 * ATOMS * EDGE_DEV * COLS, bytes_accessed=2400000, transcendentals=0
        ),
    )(mp, core, edge_atom, *hiddens, mine, other)


def turn(array, axis, count, shift):
    return lax.ppermute(array, axis, [(i, (i + shift) % count) for i in range(count)])


def turned(blocks, axis):
    count = len(blocks)
    return [blocks[0]] + [turn(blocks[k], axis, count, k) for k in range(1, count)]


def summed(blocks):
    return jnp.sum(blocks.astype(F32), axis=0)


def local(
    edge_state,
    down_weight,
    basis,
    basis_weight,
    up_weight,
    dense_weight,
    send_rows,
    trip_in,
    trip_out,
    trip_live,
    edge_atom,
):
    mp = jnp.full((1,), lax.axis_index("mp"), I32)
    core_index = lax.axis_index("graph_2")
    core = jnp.full((1,), core_index, I32)
    lists = send_rows.reshape(1, SLOTS)
    atom_row = edge_atom.reshape(1, EDGE_DEV)
    high = basis_weight.astype(BF16)
    low = (basis_weight - high.astype(F32)).astype(BF16)
    pad = ((0, BASIS_PAD - NSBF), (0, 0))
    high, low = jnp.pad(high, pad), jnp.pad(low, pad)
    coef_weight = jnp.concatenate([high, high, low], axis=0)
    half = jnp.concatenate(
        [
            lax.dynamic_slice_in_dim(
                dense_weight.reshape(MAPS * D, COLS), core_index * (HALF_MAPS * D), HALF_MAPS * D, 0
            ),
            lax.dynamic_slice_in_dim(up_weight, core_index * UP_HALF, UP_HALF, 0),
        ],
        axis=0,
    )

    trip_in = trip_in.reshape(1, TRIPS)
    trip_live = trip_live.reshape(1, TRIPS)
    trip_out = trip_out.reshape(1, TRIPS)
    first, second, *state_blocks = project(mp, edge_state, down_weight)
    exchange = functools.partial(
        lax.all_to_all, axis_name=GRAPH, split_axis=0, concat_axis=0, tiled=True
    )

    def sums(received, part):
        low, high = part
        table = received.reshape(SLOTS, high - low)
        weight = coef_weight[:, low:high]
        total = triplets(trip_in, trip_live, trip_out, basis, weight, table)
        return total.reshape(N_GRAPH, CAP, high - low)

    first = send(lists, turned([first] * N_MP, "mp")).reshape(N_GRAPH, CAP, -1)
    first, second = lax.optimization_barrier((first, second))
    partials = turned([second] * N_MP, "mp")
    first = exchange(first)
    second = send(lists, partials).reshape(N_GRAPH, CAP, -1)
    first, second, half = lax.optimization_barrier((first, second, half))
    second = exchange(second)
    gathered = lax.all_gather(half, ("graph_2", "mp"), axis=0, tiled=False)
    states = turned(state_blocks, "mp")
    first = exchange(sums(first, PARTS[0]))
    second = exchange(sums(second, PARTS[1]))
    blocks = edges(mp, lists, first.reshape(SLOTS, -1), [])
    blocks = edges(mp, lists, second.reshape(SLOTS, -1), blocks)
    updates = turned(blocks, "mp")
    hiddens = turned(layers(mp, updates, states, gathered), "mp")
    keep, give = atoms(mp, core, atom_row, hiddens)
    x = jnp.full((1,), lax.axis_index("graph_0"), I32)
    parts = turned(meet(x, keep, turn(give, "graph_2", N_CORE, 1)), "graph_0")
    part = (parts[0].astype(F32) + parts[1].astype(F32)) + (
        parts[2].astype(F32) + parts[3].astype(F32)
    )
    part = part.astype(BF16).reshape(N_Z, ATOM_DEV, COLS)
    atom_sum = summed(lax.all_to_all(part, "graph_1", 0, 0, tiled=True))
    atom_out = jax.nn.silu(atom_scale * atom_sum).astype(BF16)
    table = lax.all_to_all(
        jnp.broadcast_to(atom_out[None], (N_Z, ATOM_DEV, COLS)), "graph_1", 0, 0, tiled=True
    ).reshape(N_Z * ATOM_DEV, COLS)
    table = lax.all_to_all(
        jnp.broadcast_to(table[None], (N_X, N_Z * ATOM_DEV, COLS)), "graph_0", 0, 0, tiled=True
    ).reshape(HALF_ATOMS, COLS)
    other = turn(table, "graph_2", N_CORE, 1)
    edge_out = final(mp, core, atom_row, hiddens, table, other)
    return (edge_out, atom_out)


def solution(mesh):
    split = Mesh(
        mesh.devices.reshape(N_X, N_Z, N_CORE, mesh.shape["mp"]),
        ("graph_0", "graph_1", "graph_2", "mp"),
    )
    return jax.shard_map(
        local,
        mesh=split,
        in_specs=(
            P(GRAPH, "mp"),
            P("mp", None),
            P(None, GRAPH_MP),
            P(),
            P(None, "mp"),
            P(None, None, None, "mp"),
            P(GRAPH, "mp", None),
            P(GRAPH_MP),
            P(GRAPH_MP),
            P(GRAPH_MP),
            P(GRAPH),
        ),
        out_specs=(P(GRAPH, "mp"), P(GRAPH, "mp")),
        check_vma=False,
    )
```

```python
import functools

import jax
import jax.numpy as jnp
from jax import lax
from jax.experimental import pallas as pl
from jax.experimental.pallas import tpu as pltpu
from jax.sharding import Mesh
from jax.sharding import PartitionSpec as P

ATOM_DEV = 32
GRAPH = ("graph_0", "graph_1", "graph_2")
GRAPH_MP = ("graph_0", "graph_1", "graph_2", "mp")
N_X, N_Z, N_CORE, N_MP = 4, 8, 2, 4
N_GRAPH = N_X * N_Z * N_CORE
CAP = 64
EDGE_DEV = 512
ROWS = EDGE_DEV // N_MP
SLOTS = N_GRAPH * CAP
TRIPS = 4096
NSBF = 42
BASIS_PAD = 48
D = 1536
COLS = D // N_MP
TRIP = 384
MAPS = 6
HALF_MAPS = MAPS // N_CORE
UP_HALF = TRIP // N_CORE
ATOMS = ATOM_DEV * N_GRAPH
HALF_ATOMS = ATOMS // N_CORE
BLOCK = 512
ATOM_BLOCK = 512
PARTS = ((0, 128), (128, 384))

F32 = jnp.float32
BF16 = jnp.bfloat16
I32 = jnp.int32

inv_root_two = 0.7071067811865476
atom_scale = 0.2


def silu(v):
    return v / (1.0 + jnp.exp(-v))


def product(a, b):
    return jnp.dot(a, b, preferred_element_type=F32)


def ones_where(mask):
    return jnp.where(mask, jnp.ones((), F32), jnp.zeros((), F32)).astype(BF16)


def column_of(row):
    return jnp.broadcast_to(row, (128, row.shape[1])).T


def picks_of(column, count):
    lane = lax.broadcasted_iota(I32, column.shape, 1)
    low = ones_where((column & 127) == lane)
    high = (column >> 7).astype(F32).astype(BF16)
    none = jnp.zeros_like(low)
    return jnp.concatenate(
        [jnp.where(high == k, low, none) for k in range(count // 128)], axis=1
    )


def picks(row, count):
    return picks_of(column_of(row), count)


def members(row, count, first):
    shape = (128, row.shape[1])
    local = jnp.broadcast_to(row - first, shape)
    low = ones_where((local & 127) == lax.broadcasted_iota(I32, shape, 0))
    high = local >> 7
    return jnp.concatenate(
        [low * ones_where(high == k) for k in range(count // 128)], axis=0
    )


def params(mib):
    return pltpu.CompilerParams(
        dimension_semantics=("arbitrary",), vmem_limit_bytes=mib * 1024 * 1024
    )


def whole(shape):
    return pl.BlockSpec(shape, lambda *_: (0,) * len(shape))


def shape_of(*shape, kind=BF16):
    return jax.ShapeDtypeStruct(shape, kind)


SCALAR = pl.BlockSpec(memory_space=pltpu.SMEM)


def project_kernel(mp_ref, state_ref, weight_ref, *refs):
    partial = product(state_ref[...], weight_ref[...]).astype(BF16)
    for partial_ref, (low, high) in zip(refs, PARTS):
        partial_ref[...] = partial[:, low:high]
    for k, turned_ref in enumerate(refs[len(PARTS) :]):
        place = lax.rem(mp_ref[0] + k, N_MP) * ROWS
        turned_ref[...] = state_ref[pl.ds(pl.multiple_of(place, ROWS), ROWS), :]


def project(mp, edge_state, down_weight):
    widths = [high - low for low, high in PARTS]
    return pl.pallas_call(
        project_kernel,
        grid=(1,),
        in_specs=[SCALAR, whole((EDGE_DEV, COLS)), whole((COLS, TRIP))],
        out_specs=[whole((EDGE_DEV, w)) for w in widths] + [whole((ROWS, COLS))] * N_MP,
        out_shape=[shape_of(EDGE_DEV, w) for w in widths] + [shape_of(ROWS, COLS)] * N_MP,
        compiler_params=params(62),
        name="project",
        cost_estimate=pl.CostEstimate(
            flops=2 * EDGE_DEV * COLS * TRIP, bytes_accessed=1500000, transcendentals=0
        ),
    )(mp, edge_state, down_weight)


def send_kernel(list_ref, a_ref, b_ref, c_ref, d_ref, out_ref, table):
    @pl.when(pl.program_id(0) == 0)
    def _():
        total = a_ref[...].astype(F32) + b_ref[...].astype(F32)
        total = total + (c_ref[...].astype(F32) + d_ref[...].astype(F32))
        table[...] = total.astype(BF16)

    out_ref[...] = product(picks(list_ref[...], EDGE_DEV), table[...]).astype(BF16)


SEND_BLOCK = 1024


def send(lists, partials):
    width = partials[0].shape[1]
    return pl.pallas_call(
        send_kernel,
        grid=(SLOTS // SEND_BLOCK,),
        in_specs=[pl.BlockSpec((1, SEND_BLOCK), lambda i: (0, i))] + [whole((EDGE_DEV, width))] * N_MP,
        out_specs=pl.BlockSpec((SEND_BLOCK, width), lambda i: (i, 0)),
        out_shape=shape_of(SLOTS, width),
        scratch_shapes=[pltpu.VMEM((EDGE_DEV, width), BF16)],
        compiler_params=params(24),
        name="send",
        cost_estimate=pl.CostEstimate(
            flops=2 * SLOTS * EDGE_DEV * width, bytes_accessed=12000 * width, transcendentals=0
        ),
    )(lists, *partials)


TRIP_BLOCKS = {128: (512, 512, 1024, 48), 256: (1024, 512, TRIPS, 62)}


def triplet_kernel(
    groups, blocks, in_ref, live_ref, to_ref, basis_ref, weight_ref, table_ref, out_ref, table, values, padded
):
    step = pl.program_id(0)
    trip_block, slot_block, sum_chunk = blocks
    trip_steps = TRIPS // trip_block
    width = table_ref.shape[1]
    deep = SLOTS // groups

    @pl.when(step == 0)
    def _():
        padded[...] = jnp.zeros_like(padded)
        for h in range(groups):
            table[:, h * width : (h + 1) * width] = table_ref[h * deep : (h + 1) * deep, :]

    @pl.when(step < trip_steps)
    def _():
        padded[0:NSBF, :] = basis_ref[...] * live_ref[...].astype(F32)
        basis = padded[...]
        high = basis.astype(BF16)
        low = (basis - high.astype(F32)).astype(BF16)
        stacked = jnp.concatenate([high, low, high], axis=0)
        coef = lax.dot_general(
            stacked, weight_ref[...], (((0,), (0,)), ((), ())), preferred_element_type=F32
        )
        place = pl.multiple_of(step * trip_block, trip_block)
        source = column_of(in_ref[...])
        target = column_of(to_ref[:, pl.ds(place, trip_block)])
        spot = source & (deep - 1)

        candidates = product(picks_of(spot, deep), table[...])
        for k in range(0, width, 128):
            value = candidates[:, k : k + 128]
            for h in range(1, groups):
                at = h * width + k
                value = jnp.where(source >= h * deep, candidates[:, at : at + 128], value)
            value = value * coef[:, k : k + 128]
            for h in range(groups):
                at = h * width + k
                here = (target >= h * deep) & (target < (h + 1) * deep)
                values[pl.ds(place, trip_block), at : at + 128] = jnp.where(here, value, 0.0).astype(
                    BF16
                )

    @pl.when(step >= trip_steps)
    def _():
        first = (step - trip_steps) * slot_block

        def part(rows):
            chosen = members(to_ref[:, rows] & (deep - 1), slot_block, first)
            return product(chosen, values[rows, :])

        def more(i, total):
            return total + part(pl.ds(pl.multiple_of(i * sum_chunk, sum_chunk), sum_chunk))

        if sum_chunk == TRIPS:
            total = part(slice(0, TRIPS))
        else:
            empty = jnp.zeros((slot_block, groups * width), F32)
            total = lax.fori_loop(0, TRIPS // sum_chunk, more, empty)
        total = total.astype(BF16)
        for h in range(groups):
            out_ref[h] = total[:, h * width : (h + 1) * width]


def triplets(trip_in, trip_live, trip_out, basis, weight, table):
    width = table.shape[1]
    groups = 512 // width
    deep = SLOTS // groups
    trip_block, slot_block, sum_chunk, mib = TRIP_BLOCKS[width]
    trip_steps = TRIPS // trip_block
    gather_step = lambda i: (0, jnp.minimum(i, trip_steps - 1))
    return pl.pallas_call(
        functools.partial(triplet_kernel, groups, (trip_block, slot_block, sum_chunk)),
        grid=(trip_steps + deep // slot_block,),
        in_specs=[
            pl.BlockSpec((1, trip_block), gather_step),
            pl.BlockSpec((1, trip_block), gather_step),
            whole((1, TRIPS)),
            pl.BlockSpec((NSBF, trip_block), gather_step),
            whole((3 * BASIS_PAD, width)),
            whole((SLOTS, width)),
        ],
        out_specs=pl.BlockSpec(
            (groups, slot_block, width), lambda i: (0, jnp.maximum(i - trip_steps, 0), 0)
        ),
        out_shape=shape_of(groups, deep, width),
        scratch_shapes=[
            pltpu.VMEM((deep, groups * width), BF16),
            pltpu.VMEM((TRIPS, groups * width), BF16),
            pltpu.VMEM((BASIS_PAD, trip_block), F32),
        ],
        compiler_params=params(mib),
        name="triplets",
        cost_estimate=pl.CostEstimate(
            flops=4 * TRIPS * SLOTS * width, bytes_accessed=18000 * width, transcendentals=0
        ),
    )(trip_in, trip_live, trip_out, basis, weight, table)


EDGE_CHUNK = 1024


def edges_kernel(has_earlier, mp_ref, list_ref, table_ref, *refs):
    earlier, outs, total = refs[:has_earlier], refs[has_earlier:-1], refs[-1]
    step = pl.program_id(0)
    part = product(members(list_ref[...], EDGE_DEV, 0), table_ref[...])

    @pl.when(step == 0)
    def _():
        total[...] = part

    @pl.when(step > 0)
    def _():
        total[...] += part

    @pl.when(step == SLOTS // EDGE_CHUNK - 1)
    def _():
        for k in range(N_MP):
            place = lax.rem(mp_ref[0] + k, N_MP) * ROWS
            block = total[pl.ds(pl.multiple_of(place, ROWS), ROWS), :].astype(BF16)
            if earlier:
                low = earlier[0].shape[2]
                outs[k][:, :low] = earlier[0][k]
                outs[k][:, low:] = block
            else:
                outs[0][k] = block


def edges(mp, lists, returned, earlier):
    width = returned.shape[1]
    if earlier:
        shapes = [(ROWS, width + earlier[0].shape[2])] * N_MP
    else:
        shapes = [(N_MP, ROWS, width)]
    return pl.pallas_call(
        functools.partial(edges_kernel, len(earlier)),
        grid=(SLOTS // EDGE_CHUNK,),
        in_specs=[
            SCALAR,
            pl.BlockSpec((1, EDGE_CHUNK), lambda i: (0, i)),
            pl.BlockSpec((EDGE_CHUNK, width), lambda i: (i, 0)),
        ]
        + [whole(block.shape) for block in earlier],
        out_specs=[whole(shape) for shape in shapes],
        out_shape=[shape_of(*shape) for shape in shapes],
        scratch_shapes=[pltpu.VMEM((EDGE_DEV, width), F32)],
        compiler_params=params(24),
        name="edges",
        cost_estimate=pl.CostEstimate(
            flops=2 * SLOTS * EDGE_DEV * width, bytes_accessed=9000 * width, transcendentals=0
        ),
    )(mp, lists, returned, *earlier)


WIDE = 2 * COLS
AHEAD = 6
AHEAD = 6


def layers_kernel(mp_ref, *refs):
    updates, states, weight_ref = refs[:N_MP], refs[N_MP : 2 * N_MP], refs[2 * N_MP]
    refs = refs[2 * N_MP + 1 :]
    outs, (hidden, given, inner, up, weights, up_sem, sems) = refs[:N_MP], refs[N_MP:]
    me = mp_ref[0]

    def fetch(i):
        which, block = lax.div(i, N_MP), lax.rem(i, N_MP)
        rows = pl.multiple_of(lax.rem(which, HALF_MAPS) * D, D)
        return pltpu.make_async_copy(
            weight_ref.at[lax.div(which, HALF_MAPS) * N_MP + block, pl.ds(rows, D), :],
            weights.at[which, :, pl.ds(pl.multiple_of(block * COLS, 128), COLS)],
            sems.at[i],
        )

    up_fetch = pltpu.make_async_copy(
        weight_ref.at[:, pl.ds(HALF_MAPS * D, UP_HALF), :], up, up_sem
    )
    up_fetch.start()
    for i in range(AHEAD):
        fetch(i).start()

    a, b, c, d = (ref[...].astype(F32) for ref in updates)
    update = ((a + b) + (c + d)).astype(BF16)
    for k, state_ref in enumerate(states):
        place = pl.multiple_of(lax.rem(me + N_MP - k, N_MP) * COLS, 128)
        hidden[:, pl.ds(place, COLS)] = state_ref[...].astype(F32)
    up_fetch.wait()
    for block in range(N_MP):
        added = product(update[:, :UP_HALF], up[block])
        added = added + product(update[:, UP_HALF:], up[N_MP + block])
        at = slice(block * COLS, (block + 1) * COLS)
        fresh = hidden[:, at] + added
        hidden[:, at] = fresh
        given[:, at] = fresh.astype(BF16)

    def arrived(which, side):
        for j in range(2):
            i = which * N_MP + side * 2 + j
            fetch(i).wait()

            @pl.when(i + AHEAD < MAPS * N_MP)
            def _():
                fetch(i + AHEAD).start()

        return weights[which, :, pl.ds(pl.multiple_of(side * WIDE, 128), WIDE)]

    def layer(index, carry):
        def one(side, carry):
            at = pl.ds(pl.multiple_of(side * WIDE, 128), WIDE)
            inner[:, at] = silu(product(given[...], arrived(2 * index, side))).astype(BF16)
            return carry

        lax.fori_loop(0, 2, one, 0)
        for side in range(2):
            at = slice(side * WIDE, (side + 1) * WIDE)
            outer = silu(product(inner[...], arrived(2 * index + 1, side)))
            fresh = (hidden[:, at] + outer) * inv_root_two
            hidden[:, at] = fresh
            given[:, at] = fresh.astype(BF16)
        return carry

    lax.fori_loop(0, MAPS // 2, layer, 0)
    for k, out_ref in enumerate(outs):
        place = pl.multiple_of(lax.rem(me + k, N_MP) * COLS, 128)
        out_ref[...] = given[:, pl.ds(place, COLS)]


def layers(mp, updates, states, gathered):
    vmem = pl.BlockSpec(memory_space=pltpu.VMEM)
    return pl.pallas_call(
        layers_kernel,
        in_specs=[SCALAR] + [vmem] * (2 * N_MP) + [pl.BlockSpec(memory_space=pl.ANY)],
        out_specs=[vmem] * N_MP,
        out_shape=[shape_of(ROWS, COLS)] * N_MP,
        scratch_shapes=[
            pltpu.VMEM((ROWS, D), F32),
            pltpu.VMEM((ROWS, D), BF16),
            pltpu.VMEM((ROWS, D), BF16),
            pltpu.VMEM((N_CORE * N_MP, UP_HALF, COLS), BF16),
            pltpu.VMEM((MAPS, D, D), BF16),
            pltpu.SemaphoreType.DMA,
            pltpu.SemaphoreType.DMA((MAPS * N_MP,)),
        ],
        compiler_params=pltpu.CompilerParams(vmem_limit_bytes=48 * 1024 * 1024),
        name="layers",
        cost_estimate=pl.CostEstimate(
            flops=2 * ROWS * D * D * MAPS,
            bytes_accessed=2 * D * D * MAPS,
            transcendentals=ROWS * D * MAPS,
        ),
    )(mp, *updates, *states, gathered)


def at_block(ref, me, k):
    place = lax.rem(me + N_MP - k, N_MP) * ROWS
    return ref[:, pl.ds(pl.multiple_of(place, ROWS), ROWS)]


def atoms_kernel(mp_ref, core_ref, atom_ref, h0, h1, h2, h3, keep_ref, give_ref):
    me, core = mp_ref[0], core_ref[0]
    row = jnp.concatenate([at_block(atom_ref, me, k) for k in range(N_MP)], axis=1)
    hidden = jnp.concatenate([h0[...], h1[...], h2[...], h3[...]], axis=0)
    group = row // ATOM_DEV
    spot = (group // N_CORE) * ATOM_DEV + row % ATOM_DEV
    for out_ref, owner in ((keep_ref, core), (give_ref, 1 - core)):
        mine = jnp.where(group % N_CORE == owner, spot, -1)

        def one(i, carry):
            first = pl.multiple_of(i * ATOM_BLOCK, ATOM_BLOCK)
            part = product(members(mine, ATOM_BLOCK, first), hidden)
            out_ref[pl.ds(first, ATOM_BLOCK), :] = part.astype(BF16)
            return carry

        lax.fori_loop(0, HALF_ATOMS // ATOM_BLOCK, one, 0, unroll=True)


def atoms(mp, core, edge_atom, hiddens):
    return pl.pallas_call(
        atoms_kernel,
        grid=(1,),
        in_specs=[SCALAR, SCALAR, whole((1, EDGE_DEV))] + [whole((ROWS, COLS))] * N_MP,
        out_specs=[whole((HALF_ATOMS, COLS))] * 2,
        out_shape=[shape_of(HALF_ATOMS, COLS)] * 2,
        compiler_params=params(24),
        name="atoms",
        cost_estimate=pl.CostEstimate(
            flops=2 * ATOMS * EDGE_DEV * COLS, bytes_accessed=2000000, transcendentals=0
        ),
    )(mp, core, edge_atom, *hiddens)


def meet_kernel(x_ref, keep_ref, got_ref, *outs):
    for k, out_ref in enumerate(outs):
        place = lax.rem(x_ref[0] + k, N_X) * (HALF_ATOMS // N_X)
        rows = pl.ds(pl.multiple_of(place, HALF_ATOMS // N_X), HALF_ATOMS // N_X)
        out_ref[...] = (keep_ref[rows, :].astype(F32) + got_ref[rows, :].astype(F32)).astype(BF16)


def meet(x, keep, got):
    return pl.pallas_call(
        meet_kernel,
        grid=(1,),
        in_specs=[SCALAR] + [whole((HALF_ATOMS, COLS))] * 2,
        out_specs=[whole((HALF_ATOMS // N_X, COLS))] * N_X,
        out_shape=[shape_of(HALF_ATOMS // N_X, COLS)] * N_X,
        compiler_params=params(24),
        name="meet",
        cost_estimate=pl.CostEstimate(
            flops=HALF_ATOMS * COLS, bytes_accessed=2400000, transcendentals=0
        ),
    )(x, keep, got)


def final_kernel(mp_ref, core_ref, atom_ref, h0, h1, h2, h3, mine_ref, other_ref, out_ref):
    me, core = mp_ref[0], core_ref[0]
    for k, hidden_ref in enumerate((h0, h1, h2, h3)):
        row = at_block(atom_ref, me, k)
        group = row // ATOM_DEV
        spot = (group // N_CORE) * ATOM_DEV + row % ATOM_DEV
        near = jnp.where(group % N_CORE == core, spot, -1)
        far = jnp.where(group % N_CORE == core, -1, spot)
        taken = product(picks(near, HALF_ATOMS), mine_ref[...])
        taken = taken + product(picks(far, HALF_ATOMS), other_ref[...])
        place = lax.rem(me + N_MP - k, N_MP) * ROWS
        out_ref[pl.ds(pl.multiple_of(place, ROWS), ROWS), :] = (
            hidden_ref[...].astype(F32) + taken
        ).astype(BF16)


def final(mp, core, edge_atom, hiddens, mine, other):
    return pl.pallas_call(
        final_kernel,
        grid=(1,),
        in_specs=[SCALAR, SCALAR, whole((1, EDGE_DEV))]
        + [whole((ROWS, COLS))] * N_MP
        + [whole((HALF_ATOMS, COLS))] * 2,
        out_specs=whole((EDGE_DEV, COLS)),
        out_shape=shape_of(EDGE_DEV, COLS),
        compiler_params=params(24),
        name="final",
        cost_estimate=pl.CostEstimate(
            flops=2 * ATOMS * EDGE_DEV * COLS, bytes_accessed=2400000, transcendentals=0
        ),
    )(mp, core, edge_atom, *hiddens, mine, other)


def turn(array, axis, count, shift):
    return lax.ppermute(array, axis, [(i, (i + shift) % count) for i in range(count)])


def turned(blocks, axis):
    count = len(blocks)
    return [blocks[0]] + [turn(blocks[k], axis, count, k) for k in range(1, count)]


def summed(blocks):
    return jnp.sum(blocks.astype(F32), axis=0)


def local(
    edge_state,
    down_weight,
    basis,
    basis_weight,
    up_weight,
    dense_weight,
    send_rows,
    trip_in,
    trip_out,
    trip_live,
    edge_atom,
):
    mp = jnp.full((1,), lax.axis_index("mp"), I32)
    core_index = lax.axis_index("graph_2")
    core = jnp.full((1,), core_index, I32)
    lists = send_rows.reshape(1, SLOTS)
    atom_row = edge_atom.reshape(1, EDGE_DEV)
    high = basis_weight.astype(BF16)
    low = (basis_weight - high.astype(F32)).astype(BF16)
    pad = ((0, BASIS_PAD - NSBF), (0, 0))
    high, low = jnp.pad(high, pad), jnp.pad(low, pad)
    coef_weight = jnp.concatenate([high, high, low], axis=0)
    half = jnp.concatenate(
        [
            lax.dynamic_slice_in_dim(
                dense_weight.reshape(MAPS * D, COLS), core_index * (HALF_MAPS * D), HALF_MAPS * D, 0
            ),
            lax.dynamic_slice_in_dim(up_weight, core_index * UP_HALF, UP_HALF, 0),
        ],
        axis=0,
    )

    trip_in = trip_in.reshape(1, TRIPS)
    trip_live = trip_live.reshape(1, TRIPS)
    trip_out = trip_out.reshape(1, TRIPS)
    first, second, *state_blocks = project(mp, edge_state, down_weight)
    exchange = functools.partial(
        lax.all_to_all, axis_name=GRAPH, split_axis=0, concat_axis=0, tiled=True
    )

    def sums(received, part):
        low, high = part
        table = received.reshape(SLOTS, high - low)
        weight = coef_weight[:, low:high]
        total = triplets(trip_in, trip_live, trip_out, basis, weight, table)
        return total.reshape(N_GRAPH, CAP, high - low)

    first = send(lists, turned([first] * N_MP, "mp")).reshape(N_GRAPH, CAP, -1)
    first, second = lax.optimization_barrier((first, second))
    partials = turned([second] * N_MP, "mp")
    first = exchange(first)
    second = send(lists, partials).reshape(N_GRAPH, CAP, -1)
    first, second, half = lax.optimization_barrier((first, second, half))
    second = exchange(second)
    gathered = lax.all_gather(half, ("graph_2", "mp"), axis=0, tiled=False)
    states = turned(state_blocks, "mp")
    first = exchange(sums(first, PARTS[0]))
    second = exchange(sums(second, PARTS[1]))
    blocks = edges(mp, lists, first.reshape(SLOTS, -1), [])
    blocks = edges(mp, lists, second.reshape(SLOTS, -1), blocks)
    updates = turned(blocks, "mp")
    hiddens = turned(layers(mp, updates, states, gathered), "mp")
    keep, give = atoms(mp, core, atom_row, hiddens)
    x = jnp.full((1,), lax.axis_index("graph_0"), I32)
    parts = turned(meet(x, keep, turn(give, "graph_2", N_CORE, 1)), "graph_0")
    part = (parts[0].astype(F32) + parts[1].astype(F32)) + (
        parts[2].astype(F32) + parts[3].astype(F32)
    )
    part = part.astype(BF16).reshape(N_Z, ATOM_DEV, COLS)
    atom_sum = summed(lax.all_to_all(part, "graph_1", 0, 0, tiled=True))
    atom_out = jax.nn.silu(atom_scale * atom_sum).astype(BF16)
    table = lax.all_to_all(
        jnp.broadcast_to(atom_out[None], (N_Z, ATOM_DEV, COLS)), "graph_1", 0, 0, tiled=True
    ).reshape(N_Z * ATOM_DEV, COLS)
    table = lax.all_to_all(
        jnp.broadcast_to(table[None], (N_X, N_Z * ATOM_DEV, COLS)), "graph_0", 0, 0, tiled=True
    ).reshape(HALF_ATOMS, COLS)
    other = turn(table, "graph_2", N_CORE, 1)
    edge_out = final(mp, core, atom_row, hiddens, table, other)
    return (edge_out, atom_out)


def solution(mesh):
    split = Mesh(
        mesh.devices.reshape(N_X, N_Z, N_CORE, mesh.shape["mp"]),
        ("graph_0", "graph_1", "graph_2", "mp"),
    )
    return jax.shard_map(
        local,
        mesh=split,
        in_specs=(
            P(GRAPH, "mp"),
            P("mp", None),
            P(None, GRAPH_MP),
            P(),
            P(None, "mp"),
            P(None, None, None, "mp"),
            P(GRAPH, "mp", None),
            P(GRAPH_MP),
            P(GRAPH_MP),
            P(GRAPH_MP),
            P(GRAPH),
        ),
        out_specs=(P(GRAPH, "mp"), P(GRAPH, "mp")),
        check_vma=False,
    )
```

```python
import functools

import jax
import jax.numpy as jnp
from jax import lax
from jax.experimental import pallas as pl
from jax.experimental.pallas import tpu as pltpu
from jax.sharding import Mesh
from jax.sharding import PartitionSpec as P

ATOM_DEV = 32
GRAPH = ("graph_0", "graph_1", "graph_2")
GRAPH_MP = ("graph_0", "graph_1", "graph_2", "mp")
N_X, N_Z, N_CORE, N_MP = 4, 8, 2, 4
N_GRAPH = N_X * N_Z * N_CORE
CAP = 64
EDGE_DEV = 512
ROWS = EDGE_DEV // N_MP
SLOTS = N_GRAPH * CAP
TRIPS = 4096
NSBF = 42
BASIS_PAD = 48
D = 1536
COLS = D // N_MP
TRIP = 384
MAPS = 6
HALF_MAPS = MAPS // N_CORE
UP_HALF = TRIP // N_CORE
ATOMS = ATOM_DEV * N_GRAPH
HALF_ATOMS = ATOMS // N_CORE
BLOCK = 512
ATOM_BLOCK = 512
PARTS = ((0, 128), (128, 384))

F32 = jnp.float32
BF16 = jnp.bfloat16
I32 = jnp.int32

inv_root_two = 0.7071067811865476
atom_scale = 0.2


def silu(v):
    return v / (1.0 + jnp.exp(-v))


def product(a, b):
    return jnp.dot(a, b, preferred_element_type=F32)


def ones_where(mask):
    return jnp.where(mask, jnp.ones((), F32), jnp.zeros((), F32)).astype(BF16)


def column_of(row):
    return jnp.broadcast_to(row, (128, row.shape[1])).T


def picks_of(column, count):
    lane = lax.broadcasted_iota(I32, column.shape, 1)
    low = ones_where((column & 127) == lane)
    high = (column >> 7).astype(F32).astype(BF16)
    none = jnp.zeros_like(low)
    return jnp.concatenate(
        [jnp.where(high == k, low, none) for k in range(count // 128)], axis=1
    )


def picks(row, count):
    return picks_of(column_of(row), count)


def members(row, count, first):
    shape = (128, row.shape[1])
    local = jnp.broadcast_to(row - first, shape)
    low = ones_where((local & 127) == lax.broadcasted_iota(I32, shape, 0))
    high = local >> 7
    return jnp.concatenate(
        [low * ones_where(high == k) for k in range(count // 128)], axis=0
    )


def params(mib):
    return pltpu.CompilerParams(
        dimension_semantics=("arbitrary",), vmem_limit_bytes=mib * 1024 * 1024
    )


def whole(shape):
    return pl.BlockSpec(shape, lambda *_: (0,) * len(shape))


def shape_of(*shape, kind=BF16):
    return jax.ShapeDtypeStruct(shape, kind)


SCALAR = pl.BlockSpec(memory_space=pltpu.SMEM)


def project_kernel(mp_ref, state_ref, weight_ref, *refs):
    partial = product(state_ref[...], weight_ref[...]).astype(BF16)
    for partial_ref, (low, high) in zip(refs, PARTS):
        partial_ref[...] = partial[:, low:high]
    for k, turned_ref in enumerate(refs[len(PARTS) :]):
        place = lax.rem(mp_ref[0] + k, N_MP) * ROWS
        turned_ref[...] = state_ref[pl.ds(pl.multiple_of(place, ROWS), ROWS), :]


def project(mp, edge_state, down_weight):
    widths = [high - low for low, high in PARTS]
    return pl.pallas_call(
        project_kernel,
        grid=(1,),
        in_specs=[SCALAR, whole((EDGE_DEV, COLS)), whole((COLS, TRIP))],
        out_specs=[whole((EDGE_DEV, w)) for w in widths] + [whole((ROWS, COLS))] * N_MP,
        out_shape=[shape_of(EDGE_DEV, w) for w in widths] + [shape_of(ROWS, COLS)] * N_MP,
        compiler_params=params(62),
        name="project",
        cost_estimate=pl.CostEstimate(
            flops=2 * EDGE_DEV * COLS * TRIP, bytes_accessed=1500000, transcendentals=0
        ),
    )(mp, edge_state, down_weight)


def send_kernel(list_ref, a_ref, b_ref, c_ref, d_ref, out_ref, table):
    @pl.when(pl.program_id(0) == 0)
    def _():
        total = a_ref[...].astype(F32) + b_ref[...].astype(F32)
        total = total + (c_ref[...].astype(F32) + d_ref[...].astype(F32))
        table[...] = total.astype(BF16)

    out_ref[...] = product(picks(list_ref[...], EDGE_DEV), table[...]).astype(BF16)


SEND_BLOCK = 1024


def send(lists, partials):
    width = partials[0].shape[1]
    return pl.pallas_call(
        send_kernel,
        grid=(SLOTS // SEND_BLOCK,),
        in_specs=[pl.BlockSpec((1, SEND_BLOCK), lambda i: (0, i))] + [whole((EDGE_DEV, width))] * N_MP,
        out_specs=pl.BlockSpec((SEND_BLOCK, width), lambda i: (i, 0)),
        out_shape=shape_of(SLOTS, width),
        scratch_shapes=[pltpu.VMEM((EDGE_DEV, width), BF16)],
        compiler_params=params(24),
        name="send",
        cost_estimate=pl.CostEstimate(
            flops=2 * SLOTS * EDGE_DEV * width, bytes_accessed=12000 * width, transcendentals=0
        ),
    )(lists, *partials)


TRIP_BLOCKS = {128: (512, 512, 1024, 48), 256: (1024, 512, TRIPS, 62)}


def triplet_kernel(
    groups, blocks, in_ref, live_ref, to_ref, basis_ref, weight_ref, table_ref, out_ref, table, values, padded
):
    step = pl.program_id(0)
    trip_block, slot_block, sum_chunk = blocks
    trip_steps = TRIPS // trip_block
    width = table_ref.shape[1]
    deep = SLOTS // groups

    @pl.when(step == 0)
    def _():
        padded[...] = jnp.zeros_like(padded)
        for h in range(groups):
            table[:, h * width : (h + 1) * width] = table_ref[h * deep : (h + 1) * deep, :]

    @pl.when(step < trip_steps)
    def _():
        padded[0:NSBF, :] = basis_ref[...] * live_ref[...].astype(F32)
        basis = padded[...]
        high = basis.astype(BF16)
        low = (basis - high.astype(F32)).astype(BF16)
        stacked = jnp.concatenate([high, low, high], axis=0)
        coef = lax.dot_general(
            stacked, weight_ref[...], (((0,), (0,)), ((), ())), preferred_element_type=F32
        )
        place = pl.multiple_of(step * trip_block, trip_block)
        source = column_of(in_ref[...])
        target = column_of(to_ref[:, pl.ds(place, trip_block)])
        spot = source & (deep - 1)

        candidates = product(picks_of(spot, deep), table[...])
        for k in range(0, width, 128):
            value = candidates[:, k : k + 128]
            for h in range(1, groups):
                at = h * width + k
                value = jnp.where(source >= h * deep, candidates[:, at : at + 128], value)
            value = value * coef[:, k : k + 128]
            for h in range(groups):
                at = h * width + k
                here = (target >= h * deep) & (target < (h + 1) * deep)
                values[pl.ds(place, trip_block), at : at + 128] = jnp.where(here, value, 0.0).astype(
                    BF16
                )

    @pl.when(step >= trip_steps)
    def _():
        first = (step - trip_steps) * slot_block

        def part(rows):
            chosen = members(to_ref[:, rows] & (deep - 1), slot_block, first)
            return product(chosen, values[rows, :])

        def more(i, total):
            return total + part(pl.ds(pl.multiple_of(i * sum_chunk, sum_chunk), sum_chunk))

        if sum_chunk == TRIPS:
            total = part(slice(0, TRIPS))
        else:
            empty = jnp.zeros((slot_block, groups * width), F32)
            total = lax.fori_loop(0, TRIPS // sum_chunk, more, empty)
        total = total.astype(BF16)
        for h in range(groups):
            out_ref[h] = total[:, h * width : (h + 1) * width]


def triplets(trip_in, trip_live, trip_out, basis, weight, table):
    width = table.shape[1]
    groups = 512 // width
    deep = SLOTS // groups
    trip_block, slot_block, sum_chunk, mib = TRIP_BLOCKS[width]
    trip_steps = TRIPS // trip_block
    gather_step = lambda i: (0, jnp.minimum(i, trip_steps - 1))
    return pl.pallas_call(
        functools.partial(triplet_kernel, groups, (trip_block, slot_block, sum_chunk)),
        grid=(trip_steps + deep // slot_block,),
        in_specs=[
            pl.BlockSpec((1, trip_block), gather_step),
            pl.BlockSpec((1, trip_block), gather_step),
            whole((1, TRIPS)),
            pl.BlockSpec((NSBF, trip_block), gather_step),
            whole((3 * BASIS_PAD, width)),
            whole((SLOTS, width)),
        ],
        out_specs=pl.BlockSpec(
            (groups, slot_block, width), lambda i: (0, jnp.maximum(i - trip_steps, 0), 0)
        ),
        out_shape=shape_of(groups, deep, width),
        scratch_shapes=[
            pltpu.VMEM((deep, groups * width), BF16),
            pltpu.VMEM((TRIPS, groups * width), BF16),
            pltpu.VMEM((BASIS_PAD, trip_block), F32),
        ],
        compiler_params=params(mib),
        name="triplets",
        cost_estimate=pl.CostEstimate(
            flops=4 * TRIPS * SLOTS * width, bytes_accessed=18000 * width, transcendentals=0
        ),
    )(trip_in, trip_live, trip_out, basis, weight, table)


EDGE_CHUNK = 1024


def edges_kernel(has_earlier, mp_ref, list_ref, table_ref, *refs):
    earlier, outs, total = refs[:has_earlier], refs[has_earlier:-1], refs[-1]
    step = pl.program_id(0)
    part = product(members(list_ref[...], EDGE_DEV, 0), table_ref[...])

    @pl.when(step == 0)
    def _():
        total[...] = part

    @pl.when(step > 0)
    def _():
        total[...] += part

    @pl.when(step == SLOTS // EDGE_CHUNK - 1)
    def _():
        for k in range(N_MP):
            place = lax.rem(mp_ref[0] + k, N_MP) * ROWS
            block = total[pl.ds(pl.multiple_of(place, ROWS), ROWS), :].astype(BF16)
            if earlier:
                low = earlier[0].shape[2]
                outs[k][:, :low] = earlier[0][k]
                outs[k][:, low:] = block
            else:
                outs[0][k] = block


def edges(mp, lists, returned, earlier):
    width = returned.shape[1]
    if earlier:
        shapes = [(ROWS, width + earlier[0].shape[2])] * N_MP
    else:
        shapes = [(N_MP, ROWS, width)]
    return pl.pallas_call(
        functools.partial(edges_kernel, len(earlier)),
        grid=(SLOTS // EDGE_CHUNK,),
        in_specs=[
            SCALAR,
            pl.BlockSpec((1, EDGE_CHUNK), lambda i: (0, i)),
            pl.BlockSpec((EDGE_CHUNK, width), lambda i: (i, 0)),
        ]
        + [whole(block.shape) for block in earlier],
        out_specs=[whole(shape) for shape in shapes],
        out_shape=[shape_of(*shape) for shape in shapes],
        scratch_shapes=[pltpu.VMEM((EDGE_DEV, width), F32)],
        compiler_params=params(24),
        name="edges",
        cost_estimate=pl.CostEstimate(
            flops=2 * SLOTS * EDGE_DEV * width, bytes_accessed=9000 * width, transcendentals=0
        ),
    )(mp, lists, returned, *earlier)


WIDE = 2 * COLS
AHEAD = 6
HELD = 2


def hold_kernel(from_ref, to_ref, sems):
    def fetch(i):
        which, block = i // N_MP, i % N_MP
        return pltpu.make_async_copy(
            from_ref.at[block, pl.ds(which * D, D), :],
            to_ref.at[which, :, pl.ds(block * COLS, COLS)],
            sems.at[i],
        )

    for i in range(HELD * N_MP):
        fetch(i).start()
    for i in range(HELD * N_MP):
        fetch(i).wait()


def hold(gathered):
    return pl.pallas_call(
        hold_kernel,
        in_specs=[pl.BlockSpec(memory_space=pl.ANY)],
        out_specs=pl.BlockSpec(memory_space=pl.ANY),
        out_shape=shape_of(HELD, D, D),
        scratch_shapes=[pltpu.SemaphoreType.DMA((HELD * N_MP,))],
        compiler_params=pltpu.CompilerParams(vmem_limit_bytes=44 * 1024 * 1024),
        name="hold",
        cost_estimate=pl.CostEstimate(
            flops=0, bytes_accessed=4 * HELD * D * D, transcendentals=0
        ),
    )(gathered)

AHEAD = 6


def layers_kernel(mp_ref, *refs):
    updates, states, weight_ref = refs[:N_MP], refs[N_MP : 2 * N_MP], refs[2 * N_MP]
    held, refs = refs[2 * N_MP + 1], refs[2 * N_MP + 2 :]
    outs, (hidden, given, inner, up, weights, up_sem, sems) = refs[:N_MP], refs[N_MP:]
    me = mp_ref[0]

    def fetch(i):
        which, block = lax.div(i, N_MP), lax.rem(i, N_MP)
        rows = pl.multiple_of(lax.rem(which, HALF_MAPS) * D, D)
        return pltpu.make_async_copy(
            weight_ref.at[lax.div(which, HALF_MAPS) * N_MP + block, pl.ds(rows, D), :],
            weights.at[which - HELD, :, pl.ds(pl.multiple_of(block * COLS, 128), COLS)],
            sems.at[i - HELD * N_MP],
        )

    up_fetch = pltpu.make_async_copy(
        weight_ref.at[:, pl.ds(HALF_MAPS * D, UP_HALF), :], up, up_sem
    )
    up_fetch.start()
    for i in range(HELD * N_MP, HELD * N_MP + AHEAD):
        fetch(i).start()

    a, b, c, d = (ref[...].astype(F32) for ref in updates)
    update = ((a + b) + (c + d)).astype(BF16)
    for k, state_ref in enumerate(states):
        place = pl.multiple_of(lax.rem(me + N_MP - k, N_MP) * COLS, 128)
        hidden[:, pl.ds(place, COLS)] = state_ref[...].astype(F32)
    up_fetch.wait()
    for block in range(N_MP):
        added = product(update[:, :UP_HALF], up[block])
        added = added + product(update[:, UP_HALF:], up[N_MP + block])
        at = slice(block * COLS, (block + 1) * COLS)
        fresh = hidden[:, at] + added
        hidden[:, at] = fresh
        given[:, at] = fresh.astype(BF16)

    def arrived(which, side):
        for j in range(2):
            i = which * N_MP + side * 2 + j
            fetch(i).wait()

            @pl.when(i + AHEAD < MAPS * N_MP)
            def _():
                fetch(i + AHEAD).start()

        return weights[which - HELD, :, pl.ds(pl.multiple_of(side * WIDE, 128), WIDE)]

    def ready(which, side):
        return held[which, :, pl.ds(pl.multiple_of(side * WIDE, 128), WIDE)]

    def layer(index, carry, arrived=arrived):
        def one(side, carry):
            at = pl.ds(pl.multiple_of(side * WIDE, 128), WIDE)
            inner[:, at] = silu(product(given[...], arrived(2 * index, side))).astype(BF16)
            return carry

        lax.fori_loop(0, 2, one, 0)
        for side in range(2):
            at = slice(side * WIDE, (side + 1) * WIDE)
            outer = silu(product(inner[...], arrived(2 * index + 1, side)))
            fresh = (hidden[:, at] + outer) * inv_root_two
            hidden[:, at] = fresh
            given[:, at] = fresh.astype(BF16)
        return carry

    layer(0, 0, ready)
    lax.fori_loop(HELD // 2, MAPS // 2, layer, 0)
    for k, out_ref in enumerate(outs):
        place = pl.multiple_of(lax.rem(me + k, N_MP) * COLS, 128)
        out_ref[...] = given[:, pl.ds(place, COLS)]


def layers(mp, updates, states, gathered, held):
    vmem = pl.BlockSpec(memory_space=pltpu.VMEM)
    return pl.pallas_call(
        layers_kernel,
        in_specs=[SCALAR] + [vmem] * (2 * N_MP) + [pl.BlockSpec(memory_space=pl.ANY), vmem],
        out_specs=[vmem] * N_MP,
        out_shape=[shape_of(ROWS, COLS)] * N_MP,
        scratch_shapes=[
            pltpu.VMEM((ROWS, D), F32),
            pltpu.VMEM((ROWS, D), BF16),
            pltpu.VMEM((ROWS, D), BF16),
            pltpu.VMEM((N_CORE * N_MP, UP_HALF, COLS), BF16),
            pltpu.VMEM((MAPS - HELD, D, D), BF16),
            pltpu.SemaphoreType.DMA,
            pltpu.SemaphoreType.DMA(((MAPS - HELD) * N_MP,)),
        ],
        compiler_params=pltpu.CompilerParams(vmem_limit_bytes=30 * 1024 * 1024),
        name="layers",
        cost_estimate=pl.CostEstimate(
            flops=2 * ROWS * D * D * MAPS,
            bytes_accessed=2 * D * D * MAPS,
            transcendentals=ROWS * D * MAPS,
        ),
    )(mp, *updates, *states, gathered, held)


def at_block(ref, me, k):
    place = lax.rem(me + N_MP - k, N_MP) * ROWS
    return ref[:, pl.ds(pl.multiple_of(place, ROWS), ROWS)]


def atoms_kernel(mp_ref, core_ref, atom_ref, h0, h1, h2, h3, keep_ref, give_ref):
    me, core = mp_ref[0], core_ref[0]
    row = jnp.concatenate([at_block(atom_ref, me, k) for k in range(N_MP)], axis=1)
    hidden = jnp.concatenate([h0[...], h1[...], h2[...], h3[...]], axis=0)
    group = row // ATOM_DEV
    spot = (group // N_CORE) * ATOM_DEV + row % ATOM_DEV
    for out_ref, owner in ((keep_ref, core), (give_ref, 1 - core)):
        mine = jnp.where(group % N_CORE == owner, spot, -1)

        def one(i, carry):
            first = pl.multiple_of(i * ATOM_BLOCK, ATOM_BLOCK)
            part = product(members(mine, ATOM_BLOCK, first), hidden)
            out_ref[pl.ds(first, ATOM_BLOCK), :] = part.astype(BF16)
            return carry

        lax.fori_loop(0, HALF_ATOMS // ATOM_BLOCK, one, 0, unroll=True)


def atoms(mp, core, edge_atom, hiddens):
    return pl.pallas_call(
        atoms_kernel,
        grid=(1,),
        in_specs=[SCALAR, SCALAR, whole((1, EDGE_DEV))] + [whole((ROWS, COLS))] * N_MP,
        out_specs=[whole((HALF_ATOMS, COLS))] * 2,
        out_shape=[shape_of(HALF_ATOMS, COLS)] * 2,
        compiler_params=params(24),
        name="atoms",
        cost_estimate=pl.CostEstimate(
            flops=2 * ATOMS * EDGE_DEV * COLS, bytes_accessed=2000000, transcendentals=0
        ),
    )(mp, core, edge_atom, *hiddens)


def meet_kernel(x_ref, keep_ref, got_ref, *outs):
    for k, out_ref in enumerate(outs):
        place = lax.rem(x_ref[0] + k, N_X) * (HALF_ATOMS // N_X)
        rows = pl.ds(pl.multiple_of(place, HALF_ATOMS // N_X), HALF_ATOMS // N_X)
        out_ref[...] = (keep_ref[rows, :].astype(F32) + got_ref[rows, :].astype(F32)).astype(BF16)


def meet(x, keep, got):
    return pl.pallas_call(
        meet_kernel,
        grid=(1,),
        in_specs=[SCALAR] + [whole((HALF_ATOMS, COLS))] * 2,
        out_specs=[whole((HALF_ATOMS // N_X, COLS))] * N_X,
        out_shape=[shape_of(HALF_ATOMS // N_X, COLS)] * N_X,
        compiler_params=params(24),
        name="meet",
        cost_estimate=pl.CostEstimate(
            flops=HALF_ATOMS * COLS, bytes_accessed=2400000, transcendentals=0
        ),
    )(x, keep, got)


def final_kernel(mp_ref, core_ref, atom_ref, h0, h1, h2, h3, mine_ref, other_ref, out_ref):
    me, core = mp_ref[0], core_ref[0]
    for k, hidden_ref in enumerate((h0, h1, h2, h3)):
        row = at_block(atom_ref, me, k)
        group = row // ATOM_DEV
        spot = (group // N_CORE) * ATOM_DEV + row % ATOM_DEV
        near = jnp.where(group % N_CORE == core, spot, -1)
        far = jnp.where(group % N_CORE == core, -1, spot)
        taken = product(picks(near, HALF_ATOMS), mine_ref[...])
        taken = taken + product(picks(far, HALF_ATOMS), other_ref[...])
        place = lax.rem(me + N_MP - k, N_MP) * ROWS
        out_ref[pl.ds(pl.multiple_of(place, ROWS), ROWS), :] = (
            hidden_ref[...].astype(F32) + taken
        ).astype(BF16)


def final(mp, core, edge_atom, hiddens, mine, other):
    return pl.pallas_call(
        final_kernel,
        grid=(1,),
        in_specs=[SCALAR, SCALAR, whole((1, EDGE_DEV))]
        + [whole((ROWS, COLS))] * N_MP
        + [whole((HALF_ATOMS, COLS))] * 2,
        out_specs=whole((EDGE_DEV, COLS)),
        out_shape=shape_of(EDGE_DEV, COLS),
        compiler_params=params(24),
        name="final",
        cost_estimate=pl.CostEstimate(
            flops=2 * ATOMS * EDGE_DEV * COLS, bytes_accessed=2400000, transcendentals=0
        ),
    )(mp, core, edge_atom, *hiddens, mine, other)


def turn(array, axis, count, shift):
    return lax.ppermute(array, axis, [(i, (i + shift) % count) for i in range(count)])


def turned(blocks, axis):
    count = len(blocks)
    return [blocks[0]] + [turn(blocks[k], axis, count, k) for k in range(1, count)]


def summed(blocks):
    return jnp.sum(blocks.astype(F32), axis=0)


def local(
    edge_state,
    down_weight,
    basis,
    basis_weight,
    up_weight,
    dense_weight,
    send_rows,
    trip_in,
    trip_out,
    trip_live,
    edge_atom,
):
    mp = jnp.full((1,), lax.axis_index("mp"), I32)
    core_index = lax.axis_index("graph_2")
    core = jnp.full((1,), core_index, I32)
    lists = send_rows.reshape(1, SLOTS)
    atom_row = edge_atom.reshape(1, EDGE_DEV)
    high = basis_weight.astype(BF16)
    low = (basis_weight - high.astype(F32)).astype(BF16)
    pad = ((0, BASIS_PAD - NSBF), (0, 0))
    high, low = jnp.pad(high, pad), jnp.pad(low, pad)
    coef_weight = jnp.concatenate([high, high, low], axis=0)
    half = jnp.concatenate(
        [
            lax.dynamic_slice_in_dim(
                dense_weight.reshape(MAPS * D, COLS), core_index * (HALF_MAPS * D), HALF_MAPS * D, 0
            ),
            lax.dynamic_slice_in_dim(up_weight, core_index * UP_HALF, UP_HALF, 0),
        ],
        axis=0,
    )

    trip_in = trip_in.reshape(1, TRIPS)
    trip_live = trip_live.reshape(1, TRIPS)
    trip_out = trip_out.reshape(1, TRIPS)
    first, second, *state_blocks = project(mp, edge_state, down_weight)
    exchange = functools.partial(
        lax.all_to_all, axis_name=GRAPH, split_axis=0, concat_axis=0, tiled=True
    )

    def sums(received, part):
        low, high = part
        table = received.reshape(SLOTS, high - low)
        weight = coef_weight[:, low:high]
        total = triplets(trip_in, trip_live, trip_out, basis, weight, table)
        return total.reshape(N_GRAPH, CAP, high - low)

    first = send(lists, turned([first] * N_MP, "mp")).reshape(N_GRAPH, CAP, -1)
    first, second = lax.optimization_barrier((first, second))
    partials = turned([second] * N_MP, "mp")
    first = exchange(first)
    second = send(lists, partials).reshape(N_GRAPH, CAP, -1)
    first, second, half = lax.optimization_barrier((first, second, half))
    second = exchange(second)
    gathered = lax.all_gather(half, ("graph_2", "mp"), axis=0, tiled=False)
    states = turned(state_blocks, "mp")
    first = exchange(sums(first, PARTS[0]))
    second = exchange(sums(second, PARTS[1]))
    blocks = edges(mp, lists, first.reshape(SLOTS, -1), [])
    blocks = edges(mp, lists, second.reshape(SLOTS, -1), blocks)
    gathered, *blocks = lax.optimization_barrier((gathered, *blocks))
    updates = turned(blocks, "mp")
    hiddens = turned(layers(mp, updates, states, gathered, hold(gathered)), "mp")
    keep, give = atoms(mp, core, atom_row, hiddens)
    x = jnp.full((1,), lax.axis_index("graph_0"), I32)
    parts = turned(meet(x, keep, turn(give, "graph_2", N_CORE, 1)), "graph_0")
    part = (parts[0].astype(F32) + parts[1].astype(F32)) + (
        parts[2].astype(F32) + parts[3].astype(F32)
    )
    part = part.astype(BF16).reshape(N_Z, ATOM_DEV, COLS)
    atom_sum = summed(lax.all_to_all(part, "graph_1", 0, 0, tiled=True))
    atom_out = jax.nn.silu(atom_scale * atom_sum).astype(BF16)
    table = lax.all_to_all(
        jnp.broadcast_to(atom_out[None], (N_Z, ATOM_DEV, COLS)), "graph_1", 0, 0, tiled=True
    ).reshape(N_Z * ATOM_DEV, COLS)
    table = lax.all_to_all(
        jnp.broadcast_to(table[None], (N_X, N_Z * ATOM_DEV, COLS)), "graph_0", 0, 0, tiled=True
    ).reshape(HALF_ATOMS, COLS)
    other = turn(table, "graph_2", N_CORE, 1)
    edge_out = final(mp, core, atom_row, hiddens, table, other)
    return (edge_out, atom_out)


def solution(mesh):
    split = Mesh(
        mesh.devices.reshape(N_X, N_Z, N_CORE, mesh.shape["mp"]),
        ("graph_0", "graph_1", "graph_2", "mp"),
    )
    return jax.shard_map(
        local,
        mesh=split,
        in_specs=(
            P(GRAPH, "mp"),
            P("mp", None),
            P(None, GRAPH_MP),
            P(),
            P(None, "mp"),
            P(None, None, None, "mp"),
            P(GRAPH, "mp", None),
            P(GRAPH_MP),
            P(GRAPH_MP),
            P(GRAPH_MP),
            P(GRAPH),
        ),
        out_specs=(P(GRAPH, "mp"), P(GRAPH, "mp")),
        check_vma=False,
    )
```
